32 devices in a mesh: gx: 4 (over y, x), gy: 8 (over z, core).
Axes of the slice: x: 2, y: 2, z: 4, core: 2. Of those that a mesh axis runs over, the one named last changes fastest.
Arguments:
- displacement: float32 [3, 8, 16, 3, 128], P(None, 'gx', 'gy'), may hold values from -0.15 to 0.15
- velocity: float32 [3, 8, 16, 3, 128], P(None, 'gx', 'gy'), may hold values from -18 to 18
- noise: float32 [4, 3, 8, 16, 3, 128], P(None, None, 'gx', 'gy'), may hold values from -1.7320508 to 1.7320508
- electron_temp: float32 [32, 4, 8], P(('gx', 'gy')), may hold values from 0.5 to 10
- pair_list: int32 [4, 8, 2, 324], P('gx', 'gy'), may hold values from 0 to 26, as said below
- pair_count: int32 [4, 8], P('gx', 'gy'), may hold values from 12 to 324, as said below
Outputs:
- new_displacement: float32 [3, 8, 16, 3, 128], P(None, 'gx', 'gy')
- new_velocity: float32 [3, 8, 16, 3, 128], P(None, 'gx', 'gy')
- electron_final: float32 [32, 4, 8], P(('gx', 'gy'))
The draws below stay inside these ranges and needn't reach their ends.
Inputs may be any that keep to these rules, and one draw needn't show every extreme that they name: `pair_list`: in each brick the first pair_count entries name distinct (tile, code) pairs, the tile in 0 to 11 and the code in 0 to 26; every tile's code 13 is among them. Later entries are not read. `pair_count`: some brick has exactly 324 live entries and some brick exactly 12.
All inputs are finite; a program needn't handle non-finite values.
Results may differ from the reference program's by a relative error of at most 0.0003.
Values sent between devices are 32-bit elements; how exact they have to be, the bound alone decides.
No kernel may reach another device: no remote copies, remote signals or barrier semaphores. Data moves between devices by JAX's collectives and lax.ppermute only.
A program may use at most 64 MiB of HBM per device.

```python
import math
from functools import partial
import jax
import jax.numpy as jnp
from jax import lax

CB = 4
TILE = 128
BXT = 2
BYT = 2
TZ = 3
TILES = 12
PAIRS = 324
STEPS = 4
SUB = 6
NXG = 4
NYG = 8
NZG = 32
N_GX = 4
N_GY = 8


def brick_lists(key):
    inner = jax.random.fold_in(key, 31)
    bricks = N_GX * N_GY
    keys = jax.random.split(inner, bricks + 2)
    spread = jax.random.randint(keys[0], (bricks,), 0, 1024)
    extra = (PAIRS - TILES) * spread * spread // (1023 * 1023)
    busiest = jax.random.randint(keys[1], (), 0, bricks)
    serial = jnp.arange(bricks)
    totals = jnp.where(serial == busiest, PAIRS, TILES + extra)
    totals = jnp.where(serial == (busiest + 1) % bricks, TILES, totals)
    others = jnp.arange(26 * TILES)
    other_tile = others // 26
    other_rank = others % 26
    other_code = other_rank + (other_rank >= 13).astype(other_rank.dtype)
    orders = jax.vmap(lambda brick_key: jax.random.permutation(brick_key, 26 * TILES))(keys[2:])
    own_tiles = jnp.broadcast_to(jnp.arange(TILES), (bricks, TILES))
    tiles_row = jnp.concatenate([own_tiles, other_tile[orders]], axis=1)
    codes_row = jnp.concatenate([jnp.full((bricks, TILES), 13, dtype=other_code.dtype), other_code[orders]], axis=1)
    table = jnp.stack([tiles_row, codes_row], axis=1).reshape(N_GX, N_GY, 2, PAIRS).astype(jnp.int32)
    return (table, totals.reshape(N_GX, N_GY).astype(jnp.int32))


def draw_pair_list(key, part):
    return brick_lists(key)[0]


def draw_pair_count(key, part):
    return brick_lists(key)[1]


def draw_velocity(key, part):
    shape = (3, BXT * N_GX, BYT * N_GY, TZ, TILE)
    inner = jax.random.fold_in(key, 57)
    sign_key, size_key = jax.random.split(inner)
    signs = (jax.random.randint(sign_key, shape, 0, 2) * 2 - 1).astype(jnp.float32)
    magnitude = jax.random.uniform(size_key, shape, jnp.float32, 12.0, 18.0)
    return (signs * magnitude).astype(jnp.float32)


def levels(stream_key, shape, cuts, smallest, high):
    level, own = 1.0, jax.random.fold_in(stream_key, 6)
    for dim, parts in cuts:
        steps = jnp.exp(jax.random.uniform(jax.random.fold_in(own, dim), (parts,), jnp.float32, smallest / len(cuts), high / len(cuts)))
        level = level * jnp.repeat(steps, shape[dim] // parts).reshape([-1 if axis == dim else 1 for axis in range(len(shape))])
    return level


def setup_inputs(seed: int = 0) -> dict:
    key_of = jax.random.split(jax.random.key(seed), 7)
    displacement = jnp.clip(jax.random.uniform(key_of[0], (3, BXT * N_GX, BYT * N_GY, TZ, TILE), jnp.float32, -0.15, 0.15) * levels(key_of[0], (3, BXT * N_GX, BYT * N_GY, TZ, TILE), ((1, 4), (2, 8)), -0.4, 0.0), -0.15, 0.15)
    velocity = draw_velocity(jax.random.fold_in(key_of[6], 71), 0)
    noise = jnp.clip(jax.random.uniform(key_of[2], (STEPS, 3, BXT * N_GX, BYT * N_GY, TZ, TILE), jnp.float32, -1.7320508, 1.7320508) * levels(key_of[2], (STEPS, 3, BXT * N_GX, BYT * N_GY, TZ, TILE), ((2, 4), (3, 8)), -0.4, 0.0), -1.7320508, 1.7320508)
    electron_temp = jnp.clip(jnp.exp(math.log(10.0) - 2.9957323 * jax.random.uniform(key_of[3], (NZG, NXG, NYG), jnp.float32) ** levels(key_of[3], (NZG, NXG, NYG), ((0, 32),), -0.2, 0.2)), 0.5, 10.0)
    pair_list = draw_pair_list(jax.random.fold_in(key_of[6], 71), 0)
    pair_count = draw_pair_count(jax.random.fold_in(key_of[6], 71), 0)
    return dict(displacement=displacement, velocity=velocity, noise=noise, electron_temp=electron_temp, pair_list=pair_list, pair_count=pair_count)


lattice_edge = 3.1652
density_cut = 4.400224
embed_scale = 1.896373
pair_cut = 3.25
coef_zero = 47.1346499
coef_one = -33.7665655
coef_two = 6.2541999
time_step = 0.005
atom_mass = 0.0190534
friction = 1.0
heat_capacity = 0.02
diffusion_rate = 0.12

def lattice_sites():
    serial = jnp.arange(TILE, dtype=jnp.int32)
    cell_number = serial // 2
    half_step = (serial % 2).astype(jnp.float32) * 0.5
    corners = jnp.stack([cell_number // (CB * CB), cell_number // CB % CB, cell_number % CB])
    return lattice_edge * (corners.astype(jnp.float32) + half_step[None, :])

def plane_table(plane_total):
    serial = jnp.arange(TILE, dtype=jnp.int32)
    cell_number = serial // 2
    layer = 2 * (cell_number % CB) + serial % 2
    tiles = jnp.arange(TZ, dtype=jnp.int32)
    whole = tiles[:, None] * (2 * CB) + layer[None, :]
    return (whole * plane_total // (2 * CB * TZ)).astype(jnp.int32)

def pair_geometry(window, tile_index, neighbour_code, lattice):
    wide_y = BYT + 2
    depth_t = tile_index % TZ
    inner_y = tile_index // TZ % BYT
    inner_x = tile_index // (TZ * BYT)
    shift_x = neighbour_code // 9
    shift_y = neighbour_code // 3 % 3
    shift_z = neighbour_code % 3
    flattened = window.reshape(window.shape[0], (BXT + 2) * wide_y * TZ, TILE)
    own_index = ((inner_x + 1) * wide_y + inner_y + 1) * TZ + depth_t
    other_index = ((inner_x + shift_x) * wide_y + inner_y + shift_y) * TZ + (depth_t + shift_z - 1 + TZ) % TZ
    own_tile = lax.dynamic_index_in_dim(flattened, own_index, 1, keepdims=False)
    other_tile = lax.dynamic_index_in_dim(flattened, other_index, 1, keepdims=False)
    offset = jnp.stack([shift_x - 1, shift_y - 1, shift_z - 1]).astype(jnp.float32) * (CB * lattice_edge)
    left = lattice + own_tile
    right = lattice + other_tile + offset[:, None]
    delta = left[:, :, None] - right[:, None, :]
    square = lax.optimization_barrier(jnp.sum(delta * delta, axis=0))
    serial = jnp.arange(TILE, dtype=jnp.int32)
    same_atom = (neighbour_code == 13) & (serial[:, None] == serial[None, :])
    distance = jnp.sqrt(jnp.where(same_atom, 100.0, square))
    return (delta, distance, own_index, other_index)

def density_term(window, lattice, tile_index, neighbour_code):
    delta, distance, own_index, other_index = pair_geometry(window, tile_index, neighbour_code, lattice)
    dens_gap = distance - density_cut
    return lax.optimization_barrier(jnp.sum(jnp.where(distance < density_cut, dens_gap * dens_gap, 0.0), axis=1))[None]

def force_term(window, embed_window, lattice, tile_index, neighbour_code):
    delta, distance, own_index, other_index = pair_geometry(window, tile_index, neighbour_code, lattice)
    flat_embed = embed_window.reshape((BXT + 2) * (BYT + 2) * TZ, TILE)
    own_embed = lax.dynamic_index_in_dim(flat_embed, own_index, 0, keepdims=False)
    other_embed = lax.dynamic_index_in_dim(flat_embed, other_index, 0, keepdims=False)
    pair_gap = distance - pair_cut
    poly = coef_zero + coef_one * distance + coef_two * distance * distance
    pair_slope = jnp.where(distance < pair_cut, 2.0 * pair_gap * poly + pair_gap * pair_gap * (coef_one + 2.0 * coef_two * distance), 0.0)
    dens_gap = distance - density_cut
    dens_slope = jnp.where(distance < density_cut, 2.0 * dens_gap, 0.0)
    scalar = (pair_slope + (own_embed[:, None] + other_embed[None, :]) * dens_slope) / distance
    return -lax.optimization_barrier(jnp.sum(scalar[None] * delta, axis=2))

def brick_total(term_fn, channels, pair_table, pair_total):
    initial = jnp.zeros((channels, TILES, TILE), jnp.float32)

    def visit(running, entry_index):
        tile_index = pair_table[0, entry_index]
        neighbour_code = pair_table[1, entry_index]
        term = term_fn(tile_index, neighbour_code)
        term = jnp.where(entry_index < pair_total, term, 0.0)
        return (running.at[:, tile_index].add(term), None)
    return lax.scan(visit, initial, jnp.arange(PAIRS, dtype=jnp.int32))[0]

def brick_density(window, pair_table, pair_total):
    return brick_total(partial(density_term, window, lattice_sites()), 1, pair_table, pair_total)

def brick_force(window, embed_window, pair_table, pair_total):
    return brick_total(partial(force_term, window, embed_window, lattice_sites()), 3, pair_table, pair_total)

def windows(values_in):
    channels = values_in.shape[0]
    padded = jnp.pad(values_in, ((0, 0), (1, 1), (1, 1), (0, 0), (0, 0)), mode='wrap')
    serial = jnp.arange(N_GX * N_GY, dtype=jnp.int32)

    def cut(brick):
        zero = jnp.zeros((), jnp.int32)
        starts = (zero, brick // N_GY * BXT, brick % N_GY * BYT, zero, zero)
        return lax.dynamic_slice(padded, starts, (channels, BXT + 2, BYT + 2, TZ, TILE))
    return jax.vmap(cut)(serial)

def from_bricks(per_brick):
    channels = per_brick.shape[1]
    shaped = per_brick.reshape(N_GX, N_GY, channels, BXT, BYT, TZ, TILE)
    return jnp.transpose(shaped, (2, 0, 3, 1, 4, 5, 6)).reshape(channels, N_GX * BXT, N_GY * BYT, TZ, TILE)

def to_bricks(values_in):
    channels = values_in.shape[0]
    shaped = values_in.reshape(channels, N_GX, BXT, N_GY, BYT, TZ, TILE)
    return jnp.transpose(shaped, (1, 3, 0, 2, 4, 5, 6)).reshape(N_GX * N_GY, channels, BXT, BYT, TZ, TILE)

def diffuse(heat):
    beside_all = jnp.roll(heat, 1, 0) + jnp.roll(heat, -1, 0) + jnp.roll(heat, 1, 1) + jnp.roll(heat, -1, 1)
    beside_all = beside_all + jnp.roll(heat, 1, 2) + jnp.roll(heat, -1, 2)
    return heat + diffusion_rate * (beside_all - 6.0 * heat)

def reference(displacement, velocity, noise, electron_temp, pair_list, pair_count):
    bricks = N_GX * N_GY
    positions = displacement
    speeds = velocity
    heat_field = electron_temp
    planes = plane_table(NZG).reshape(-1)
    pair_table = pair_list.reshape(bricks, 2, PAIRS)
    pair_total = pair_count.reshape(bricks)
    for step_index in range(STEPS):
        columns = jnp.transpose(heat_field.reshape(NZG, bricks))
        column_temp = jnp.take(columns, planes, axis=1).reshape(bricks, 1, 1, 1, TZ, TILE)
        local_temp = from_bricks(jnp.broadcast_to(column_temp, (bricks, 1, BXT, BYT, TZ, TILE)))[0]
        window = windows(positions)
        density = jax.vmap(brick_density)(window, pair_table, pair_total)
        density = from_bricks(density.reshape(bricks, 1, BXT, BYT, TZ, TILE))
        embed_slope = -embed_scale / (2.0 * jnp.sqrt(density))
        embed_window = windows(embed_slope)
        force = jax.vmap(brick_force)(window, embed_window, pair_table, pair_total)
        force = from_bricks(force.reshape(bricks, 3, BXT, BYT, TZ, TILE))
        kicker = jnp.sqrt(2.0 * friction * atom_mass * local_temp / time_step)[None] * noise[step_index]
        speeds = speeds + time_step / atom_mass * (force - friction * atom_mass * speeds + kicker)
        positions = positions + time_step * speeds
        power = friction * atom_mass * time_step * lax.optimization_barrier(jnp.sum(speeds * speeds, axis=0))
        brick_power = lax.optimization_barrier(jnp.sum(to_bricks(power[None])[:, 0], axis=(1, 2))).reshape(bricks, TZ * TILE)
        energy = jax.vmap(lambda values: jnp.zeros((NZG,), jnp.float32).at[planes].add(values))(brick_power)
        heat_field = heat_field + jnp.transpose(energy).reshape(NZG, N_GX, N_GY) / heat_capacity
        for sub_index in range(SUB):
            heat_field = diffuse(heat_field)
    return (positions, speeds, heat_field)
```

```python
from functools import partial

import jax
import jax.numpy as jnp
from jax import lax
from jax.experimental import pallas as pl
from jax.experimental.pallas import tpu as pltpu
from jax.sharding import PartitionSpec as P

CB = 4
TILE = 128
BXT = 2
BYT = 2
TZ = 3
TILES = 12
STEPS = 4
SUB = 6


lattice_edge = 3.1652
density_cut = 4.400224
embed_scale = 1.896373
pair_cut = 3.25
coef_zero = 47.1346499
coef_one = -33.7665655
coef_two = 6.2541999
time_step = 0.005
atom_mass = 0.0190534
friction = 1.0
heat_capacity = 0.02
diffusion_rate = 0.12


def padded_2(block, sides, width):
    for axis, dim in sides:
        count = lax.axis_size(axis)
        forward = [(i, i + 1) for i in range(count - 1)]
        forward.append((count - 1, 0))
        backward = [(target, source) for source, target in forward]
        low = lax.ppermute(
            lax.slice_in_dim(block, block.shape[dim] - width, None, axis=dim), axis, forward
        )
        high = lax.ppermute(lax.slice_in_dim(block, 0, width, axis=dim), axis, backward)
        block = jnp.concatenate([low, block, high], axis=dim)
    return block


def lattice_sites():
    serial = jnp.arange(TILE, dtype=jnp.int32)
    cell_number = serial // 2
    half_step = (serial % 2).astype(jnp.float32) * 0.5
    corners = jnp.stack([cell_number // (CB * CB), cell_number // CB % CB, cell_number % CB])
    return lattice_edge * (corners.astype(jnp.float32) + half_step[None, :])


def plane_table(plane_total):
    serial = jnp.arange(TILE, dtype=jnp.int32)
    cell_number = serial // 2
    layer = 2 * (cell_number % CB) + serial % 2
    tiles = jnp.arange(TZ, dtype=jnp.int32)
    whole = tiles[:, None] * (2 * CB) + layer[None, :]
    return whole * plane_total // (2 * CB * TZ)


def pair_geometry(window, tile_index, neighbour_code, lattice):
    wide_y = BYT + 2
    depth_t = tile_index % TZ
    inner_y = tile_index // TZ % BYT
    inner_x = tile_index // (TZ * BYT)
    shift_x = neighbour_code // 9
    shift_y = neighbour_code // 3 % 3
    shift_z = neighbour_code % 3
    flattened = window.reshape(window.shape[0], (BXT + 2) * wide_y * TZ, TILE)
    own_index = ((inner_x + 1) * wide_y + inner_y + 1) * TZ + depth_t
    other_index = ((inner_x + shift_x) * wide_y + inner_y + shift_y) * TZ + (
        depth_t + shift_z - 1 + TZ
    ) % TZ
    own_tile = lax.dynamic_index_in_dim(flattened, own_index, 1, keepdims=False)
    other_tile = lax.dynamic_index_in_dim(flattened, other_index, 1, keepdims=False)
    offset = jnp.stack([shift_x - 1, shift_y - 1, shift_z - 1]).astype(jnp.float32) * (
        CB * lattice_edge
    )
    left = lattice + own_tile
    right = lattice + other_tile + offset[:, None]
    delta = left[:, :, None] - right[:, None, :]
    square = jnp.sum(delta * delta, axis=0)
    serial = jnp.arange(TILE, dtype=jnp.int32)
    same_atom = (neighbour_code == 13) & (serial[:, None] == serial[None, :])
    distance = jnp.sqrt(jnp.where(same_atom, 100.0, square))
    return (delta, distance, own_index, other_index)


def density_term(window, lattice, tile_index, neighbour_code):
    delta, distance, own_index, other_index = pair_geometry(
        window, tile_index, neighbour_code, lattice
    )
    dens_gap = distance - density_cut
    return jnp.sum(jnp.where(distance < density_cut, dens_gap * dens_gap, 0.0), axis=1)[None]


def force_term(window, embed_window, lattice, tile_index, neighbour_code):
    delta, distance, own_index, other_index = pair_geometry(
        window, tile_index, neighbour_code, lattice
    )
    flat_embed = embed_window.reshape((BXT + 2) * (BYT + 2) * TZ, TILE)
    own_embed = lax.dynamic_index_in_dim(flat_embed, own_index, 0, keepdims=False)
    other_embed = lax.dynamic_index_in_dim(flat_embed, other_index, 0, keepdims=False)
    pair_gap = distance - pair_cut
    poly = coef_zero + coef_one * distance + coef_two * distance * distance
    pair_slope = jnp.where(
        distance < pair_cut,
        2.0 * pair_gap * poly + pair_gap * pair_gap * (coef_one + 2.0 * coef_two * distance),
        0.0,
    )
    dens_gap = distance - density_cut
    dens_slope = jnp.where(distance < density_cut, 2.0 * dens_gap, 0.0)
    scalar = (pair_slope + (own_embed[:, None] + other_embed[None, :]) * dens_slope) / distance
    return -jnp.sum(scalar[None] * delta, axis=2)


def sweep_pairs(term_fn, channels, pair_table, pair_total):
    initial = jnp.zeros((channels, TILES, TILE), jnp.float32)

    def block_add(block_index, running):
        start = block_index * 27
        chosen = lax.dynamic_slice_in_dim(pair_table, start, 27, 1)
        live = start + jnp.arange(27, dtype=jnp.int32) < pair_total
        terms = jax.vmap(term_fn)(chosen[0], chosen[1])
        terms = jnp.where(live[:, None, None], terms, 0.0)
        return running.at[:, chosen[0]].add(jnp.swapaxes(terms, 0, 1))

    blocks = (pair_total + 26) // 27
    total = lax.fori_loop(0, blocks, block_add, initial)
    return total.reshape(channels, BXT, BYT, TZ, TILE)


def relax_slab(padded):
    center = padded[1:-1]
    beside_all = padded[2:] + padded[:-2] + jnp.roll(center, 1, 1) + jnp.roll(center, -1, 1)
    beside_all = beside_all + jnp.roll(center, 1, 2) + jnp.roll(center, -1, 2)
    return center + diffusion_rate * (beside_all - 6.0 * center)


def one_step(lattice, pair_table, pair_total, planes, owners, across, carry, noise_now):
    positions, speeds, heat_field = carry
    slab_depth = heat_field.shape[0]
    plane_total = slab_depth * owners
    arrived = lax.all_to_all(
        heat_field.reshape(slab_depth, owners), ("gx", "gy"), split_axis=1, concat_axis=0, tiled=True
    )
    column = arrived.reshape(-1)
    column_temp = jnp.take(column, planes).reshape(TZ, TILE)
    local_temp = jnp.broadcast_to(column_temp, (BXT, BYT, TZ, TILE))
    window = padded_2(positions, (("gx", 1), ("gy", 2)), 1)
    density = sweep_pairs(partial(density_term, window, lattice), 1, pair_table, pair_total)
    embed_slope = -embed_scale / (2.0 * jnp.sqrt(density))
    embed_window = padded_2(embed_slope, (("gx", 1), ("gy", 2)), 1)
    force = sweep_pairs(partial(force_term, window, embed_window, lattice), 3, pair_table, pair_total)
    kicker = jnp.sqrt(2.0 * friction * atom_mass * local_temp / time_step)[None] * noise_now
    speeds = speeds + time_step / atom_mass * (force - friction * atom_mass * speeds + kicker)
    positions = positions + time_step * speeds
    power = friction * atom_mass * time_step * jnp.sum(speeds * speeds, axis=0)
    tile_power = jnp.sum(power, axis=(0, 1)).reshape(-1)
    energy = jnp.zeros((plane_total,), jnp.float32).at[planes].add(tile_power)
    arrived = lax.all_to_all(
        energy.reshape(plane_total, 1), ("gx", "gy"), split_axis=0, concat_axis=1, tiled=True
    )
    heat_field = heat_field + arrived.reshape(slab_depth, *across) / heat_capacity

    def relax(sub_index, heat):
        return relax_slab(padded_2(heat, ((("gx", "gy"), 0),), 1))

    heat_field = lax.fori_loop(0, SUB, relax, heat_field)
    return (positions, speeds, heat_field)


def whole_sweep(displacement, velocity, noise, electron_temp, pair_list, pair_count):
    across = (lax.axis_size("gx"), lax.axis_size("gy"))
    owners = across[0] * across[1]
    planes = plane_table(electron_temp.shape[0] * owners).reshape(-1)
    step = partial(
        one_step, lattice_sites(), pair_list[0, 0], pair_count[0, 0], planes, owners, across
    )
    return lax.fori_loop(
        0,
        STEPS,
        lambda n, carry: step(carry, lax.dynamic_index_in_dim(noise, n, 0, keepdims=False)),
        (displacement, velocity, electron_temp),
    )


NEAR_SHELLS = (3, 4, 8)
FAR_SHELLS = (11, 12)
NEAR_LIMIT = 0.2900
FAR_LIMIT = 0.8170
HALF = 0.5 * lattice_edge
FAR_AWAY = 1.0e6
ROWS = 24
BASE = 4
WIDTH = 16


def site_offsets(shells):
    span = range(-3, 4)
    found = []
    for x in span:
        for y in span:
            for z in span:
                if x % 2 == y % 2 == z % 2 and x * x + y * y + z * z in shells:
                    found.append((x, y, z))
    return found


def grouped(offsets):
    table = {}
    for x, y, z in offsets:
        table.setdefault((y, z), []).append(x)
    return sorted(table.items())


NEAR = site_offsets(NEAR_SHELLS)
FAR = site_offsets(FAR_SHELLS)
MASK_SLOT = {offset: slot for slot, offset in enumerate(NEAR + FAR)}
MASKS = len(MASK_SLOT)


def sign(value):
    return (value > 0) - (value < 0)


def sources(dy, dz):
    s = sign(dz)
    if dy % 2 == 0:
        k = dy // 2
        out = [(None, 0, dz + 8 * k, 0)]
        if s:
            out.append((None, s, dz - 8 * s + 8 * k, 0))
        return out
    low = (dy - 1) // 2
    out = [(0, 0, dz + 8 * low, 0), (1, 0, dz + 8 * (low + 1), 1)]
    for parity, k in ((0, low), (1, low + 1)):
        if any(not 0 <= iz + dz < 8 for iz in range(parity, 8, 2)):
            out.append((parity, s, dz - 8 * s + 8 * k, parity))
    return out


def lane_shifts(groups):
    return sorted({shift for (dy, dz), _ in groups for _, _, shift, _ in sources(dy, dz)})


def lanes_of(shape=(8, 128)):
    return lax.broadcasted_iota(jnp.int32, shape, len(shape) - 1)


def rows_of(shape=(8, 128)):
    return lax.broadcasted_iota(jnp.int32, shape, len(shape) - 2)


def turn(value, amount):
    amount = (-amount) % 128
    return value if amount == 0 else pltpu.roll(value, amount, value.ndim - 1)


class Chunk:
    def __init__(self, owners, cells):
        self.cells = cells
        self.owners = owners
        self.narrow = owners <= 32
        self.rows = WIDTH if self.narrow else WIDTH + 8
        if self.narrow:
            self.tail = 8 if cells == 2 else 14
            self.tail_lane = 96
        else:
            self.tail = WIDTH
            self.tail_lane = 0
        self.slots = 128 // (8 * cells)

    def row_home(self, plane):
        if plane == 8:
            return (9 if False else 4 * self.cells, 0) if self.cells == 3 else (8, 0)
        return (self.cells * (plane // 2), plane % 2)


def to_own(lane, first, second, cx):
    both = jnp.where(lane < 64, turn(first, 32 * cx - 32), turn(second, 32 * cx - 64))
    return jnp.where((lane >= 32) & (lane < 96), both, 0.0)


def spread(value, lane, chunk):
    if not chunk.narrow:
        return value
    value = jnp.where(lane >= 96, value, 0.0)
    value = value + pltpu.roll(value, 64, 1)
    return value + pltpu.roll(value, 32, 1)


def place_halo(own, send_ref, chunk, neighbours, tails):
    w = chunk.cells
    lane = lanes_of()
    row16 = rows_of((16, 128))
    lane16 = lanes_of((16, 128))
    in_tail = lane16 >= chunk.tail_lane
    common = jnp.zeros((16, 128), jnp.float32)
    if chunk.narrow:
        for extra, value in tails:
            common = jnp.where(in_tail & (row16 == chunk.tail + extra), value, common)
        block = common
    else:
        block = common

    def fill(index, carry):
        base = pl.multiple_of(index * chunk.rows, 8)
        send_ref[pl.ds(base, 16), :] = block
        if not chunk.narrow:
            rows8 = rows_of()
            late = jnp.zeros((8, 128), jnp.float32)
            for extra, value in tails:
                late = jnp.where(rows8 == extra, value, late)
            send_ref[pl.ds(base + 16, 8), :] = late
        return carry

    lax.fori_loop(0, chunk.owners, fill, 0, unroll=False)

    for sy in (-1, 1):
        start = 96 - 8 * w if sy == 1 else 32
        for g in range(2):
            packed = common[8 * g : 8 * g + 8]
            for plane in range(g * chunk.slots, min(9, (g + 1) * chunk.slots)):
                slot = 8 * w * (plane - g * chunk.slots)
                here = (lane >= slot) & (lane < slot + 8 * w)
                packed = jnp.where(here, turn(own(plane), start - slot), packed)
            for sx in (-1, 0, 1):
                base = pl.multiple_of(neighbours[(sx, sy)] * chunk.rows, 8)
                send_ref[pl.ds(base + 8 * g, 8), :] = packed
    for sx in (-1, 1):
        base = pl.multiple_of(neighbours[(sx, 0)] * chunk.rows, 8)
        first = 8 - w if sx == 1 else 0
        for plane in range(9):
            home, half = chunk.row_home(plane)
            value = turn(own(plane), 32 if half == 0 else -32)[first : first + w]
            here = lanes_of((w, 128)) < 64 if half == 0 else lanes_of((w, 128)) >= 64
            pltpu.store(send_ref.at[pl.ds(base + home, w), :], value, mask=here)


def build_window(own, recv_ref, window, chunk, neighbours):
    w = chunk.cells
    lane = lanes_of()
    zero = jnp.zeros((8, 128), jnp.float32)
    for plane in range(9):
        at = plane * ROWS
        window[at : at + 8, :] = zero
        window[at + 16 : at + 24, :] = zero
        centre = own(plane)
        for sy in (-1, 1):
            g, slot = divmod(plane, chunk.slots)
            slot *= 8 * w
            target = 32 - 8 * w if sy == -1 else 96
            here = (lane >= target) & (lane < target + 8 * w)
            for sx in (-1, 0, 1):
                base = pl.multiple_of(neighbours[(sx, sy)] * chunk.rows, 8)
                piece = turn(recv_ref[pl.ds(base + 8 * g, 8), :], slot - target)
                if sx == 0:
                    centre = jnp.where(here, piece, centre)
                    continue
                piece = jnp.where(here, piece, 0.0)
                if sx == -1:
                    old = window[at : at + 8, :]
                    window[at : at + 8, :] = jnp.where(here, piece, old)
                else:
                    old = window[at + 16 : at + 24, :]
                    window[at + 16 : at + 24, :] = jnp.where(here, piece, old)
        window[at + 8 : at + 16, :] = centre
        home, half = chunk.row_home(plane)
        here = (lanes_of((w, 128)) >= 32) & (lanes_of((w, 128)) < 96)
        for sx in (-1, 1):
            base = pl.multiple_of(neighbours[(sx, 0)] * chunk.rows, 8)
            piece = turn(recv_ref[pl.ds(base + home, w), :], -32 if half == 0 else 32)
            row = at + (8 - w if sx == -1 else 16)
            pltpu.store(window.at[row : row + w, :], piece, mask=here)


def shifted_planes(planes, source, rolled, out, groups, shifts, constants):
    slot_of = {shift: n for n, shift in enumerate(shifts)}
    size = planes * ROWS

    def roll_all(plane, carry):
        at = pl.multiple_of(plane * ROWS, 8)
        value = source[pl.ds(at, ROWS), :]
        for shift in shifts:
            rolled[pl.ds(pl.multiple_of(slot_of[shift] * size + at, 8), ROWS), :] = turn(value, shift)
        return carry

    lax.fori_loop(0, planes, roll_all, 0)
    count = planes // TZ
    half_layer = lanes_of((16, 128)) % 8
    parity = half_layer % 2

    def build(t, carry):
        for n, ((dy, dz), _) in enumerate(groups):
            carried = (half_layer + dz >= 8) | (half_layer + dz < 0)
            for c in range(count):
                value = None
                for want, carry_z, shift, down in sources(dy, dz):
                    tz = t
                    if carry_z == 1:
                        tz = jnp.where(t == TZ - 1, 0, t + 1)
                    elif carry_z == -1:
                        tz = jnp.where(t == 0, TZ - 1, t - 1)
                    row = slot_of[shift] * size + (c * TZ + tz) * ROWS
                    piece = rolled[pl.ds(pl.multiple_of(row, 8) + BASE + down, 16), :]
                    if value is None:
                        value = piece
                        continue
                    here = None
                    if want is not None:
                        here = parity == want
                    if carry_z:
                        here = carried if here is None else here & carried
                    value = jnp.where(here, piece, value)
                shift_by = constants(c, dy, dz)
                if shift_by:
                    value = value + shift_by
                at = pl.multiple_of(n * size + (c * TZ + t) * ROWS, 8)
                out[pl.ds(at + BASE, 16), :] = value
        return carry

    lax.fori_loop(0, TZ, build, 0)


def coordinate_shift(c, dy, dz):
    return (0.0, HALF * dy, HALF * dz)[c]


def no_shift(c, dy, dz):
    return 0.0


def row_start(dx):
    return dx // 2 if dx % 2 == 0 else (dx - 1) // 2


def densities(window, moved, masks, slope, groups):
    size = 9 * ROWS

    def at_t(t, carry):
        for block in range(2):
            at = BASE + 8 * block
            own = [window[pl.ds(pl.multiple_of((c * TZ + t) * ROWS, 8) + at, 8), :] for c in range(3)]
            total = jnp.zeros((8, 128), jnp.float32)
            for n, ((dy, dz), dxs) in enumerate(groups):
                for dx in dxs:
                    down = row_start(dx)
                    other = [
                        moved[pl.ds(pl.multiple_of(n * size + (c * TZ + t) * ROWS, 8) + at + down, 8), :]
                        for c in range(3)
                    ]
                    away = masks(dx, dy, dz, t, 8 * block)
                    ex = (own[0] - HALF * dx) - other[0]
                    ey = own[1] - other[1]
                    ez = own[2] - other[2]
                    square = ex * ex + ey * ey + (ez * ez + away)
                    distance = square * lax.rsqrt(square)
                    gap = jnp.minimum(distance - density_cut, 0.0)
                    total = total + gap * gap
            slope[pl.ds(pl.multiple_of(t * ROWS, 8) + at, 8), :] = -embed_scale * lax.rsqrt(total)
        return carry

    lax.fori_loop(0, TZ, at_t, 0)


def forces(t, window, moved, slope, slope_moved, masks, groups):
    size = 9 * ROWS
    at = BASE + 4
    own = [window[pl.ds(pl.multiple_of((c * TZ + t) * ROWS, 8) + at, 8), :] for c in range(3)]
    own_slope = slope[pl.ds(pl.multiple_of(t * ROWS, 8) + at, 8), :]
    total = [jnp.zeros((8, 128), jnp.float32) for _ in range(3)]
    first = 2.0 * (coef_zero + coef_one * pair_cut + coef_two * pair_cut * pair_cut)
    second = 3.0 * (coef_one + 2.0 * coef_two * pair_cut)
    third = 4.0 * coef_two
    for n, ((dy, dz), dxs) in enumerate(groups):
        for dx in dxs:
            down = row_start(dx)
            other = [
                moved[pl.ds(pl.multiple_of(n * size + (c * TZ + t) * ROWS, 8) + at + down, 8), :]
                for c in range(3)
            ]
            other_slope = slope_moved[
                pl.ds(pl.multiple_of(n * TZ * ROWS + t * ROWS, 8) + at + down, 8), :
            ]
            away = masks(dx, dy, dz, t, 4)
            ex = (own[0] - HALF * dx) - other[0]
            ey = own[1] - other[1]
            ez = own[2] - other[2]
            square = ex * ex + ey * ey + (ez * ez + away)
            inverse = lax.rsqrt(square)
            distance = square * inverse
            gap = jnp.minimum(distance - density_cut, 0.0)
            near = jnp.minimum(distance - pair_cut, 0.0)
            slope_sum = (own_slope + other_slope) * gap
            slope_sum = slope_sum + near * (first + near * (second + third * near))
            scalar = slope_sum * inverse
            total[0] = total[0] - scalar * ex
            total[1] = total[1] - scalar * ey
            total[2] = total[2] - scalar * ez
    return total


def diffuse_grid(grid, across):
    nx, ny = across
    for _ in range(SUB):
        columns = []
        for x in range(nx):
            heat = grid[x]
            beside = grid[(x + 1) % nx] + grid[(x - 1) % nx]
            beside = beside + pltpu.roll(heat, 1, 0) + pltpu.roll(heat, ny - 1, 0)
            beside = beside + pltpu.roll(heat, 1, 1) + pltpu.roll(heat, 127, 1)
            columns.append(heat + diffusion_rate * (beside - 6.0 * heat))
        grid = columns
    return grid


def layer_matrix(t, plane_total, rows_are_layers):
    rows = rows_of((128, 128))
    lanes = lanes_of((128, 128))
    layer, plane = (rows, lanes) if rows_are_layers else (lanes, rows)
    found = (2 * CB * t + layer % 8) * plane_total // (2 * CB * TZ)
    if rows_are_layers:
        plane = plane % plane_total
    return jnp.where(found == plane, 1.0, 0.0)


def exact_dot(a, b):
    return jnp.dot(a, b, precision=lax.Precision.HIGHEST, preferred_element_type=jnp.float32)


def neighbour_ids(across):
    nx, ny = across
    bx, by = lax.axis_index("gx"), lax.axis_index("gy")
    ids = {}
    for sx in (-1, 0, 1):
        for sy in (-1, 0, 1):
            ids[(sx, sy)] = lax.rem(bx + sx + nx, nx) * ny + lax.rem(by + sy + ny, ny)
    return ids


def prepare(across, chunk, disp, vel, noise, heat, pairs, count, send, own_u, own_v, own_noise, live, lists):
    owners = across[0] * across[1]
    lane3 = lanes_of((TZ, 128))

    def convert(read, out, first):
        for c in range(3):
            for ix in range(BXT):
                rows = [read(c, ix, iy) for iy in range(BYT)]
                for cx in range(CB):
                    start = first + c * TZ * 8 + CB * ix + cx
                    out[pl.ds(start, TZ, stride=8), :] = to_own(lane3, rows[0], rows[1], cx)

    convert(lambda c, ix, iy: disp[c, ix, iy], own_u, 0)
    convert(lambda c, ix, iy: vel[c, ix, iy], own_v, 0)
    for n in range(STEPS):
        convert(lambda c, ix, iy: noise[n, c, ix, iy], own_noise, n * 72)

    slots = pairs.shape[3]
    width = lists.shape[1]
    lists[...] = jnp.full(lists.shape, -1, jnp.int32)
    lists[0:2, 0:slots] = pairs[0, 0]
    tile = lists[0:1, :]
    code = lists[1:2, :]
    valid = (lanes_of((1, width)) < count[0, 0]) & (tile >= 0)
    column = jnp.where(tile >= 3, 1, 0) + jnp.where(tile >= 6, 1, 0) + jnp.where(tile >= 9, 1, 0)
    depth = jnp.where(valid, tile - 3 * column, -1)
    place = 32 * column + code
    left = jnp.where(rows_of((8, width)) == depth, 1.0, 0.0)
    right = jnp.where(rows_of((128, width)) == place, 1.0, 0.0)
    found = lax.dot_general(
        left, right, (((1,), (1,)), ((), ())), preferred_element_type=jnp.float32
    )
    live[...] = found

    nx, ny = across
    lane_n = lanes_of((nx, 128))
    pick = jnp.where(lanes_of((ny, 128)) % ny == rows_of((ny, 128)), 1.0, 0.0)
    field = exact_dot(heat[0], pick)
    field = jnp.where(lane_n % owners // ny == rows_of((nx, 128)), field, 0.0)
    field = jnp.sum(field, axis=0, keepdims=True)

    ids = neighbour_ids(across)
    place_halo(lambda plane: own_u[8 * plane : 8 * plane + 8, :], send, chunk, ids, [(0, field)])
    lanes_live = lanes_of((TZ, 128))
    middle = (lanes_live >= 32) & (lanes_live < 96)
    for key, ident in ids.items():
        if key == (0, 0):
            continue
        base = pl.multiple_of(ident * chunk.rows, 8)
        if chunk.narrow:
            pltpu.store(send.at[pl.ds(base + 10, TZ), :], turn(found[:TZ], -32), mask=middle)
            pltpu.store(send.at[pl.ds(base + 13, TZ), :], turn(found[:TZ], 32), mask=middle)
        else:
            send[pl.ds(base + chunk.tail + 2, TZ), :] = found[:TZ]


def make_masks(chunk, across, recv, live, masks_ref, table, spread_ref, cases):
    ids = neighbour_ids(across)
    lane3 = lanes_of((TZ, 128))
    tables = {}
    for key, ident in ids.items():
        base = pl.multiple_of(ident * chunk.rows, 8)
        if key == (0, 0):
            tables[key] = live[0:TZ, :]
        elif chunk.narrow:
            low = turn(recv[pl.ds(base + 10, TZ), :], 32)
            high = turn(recv[pl.ds(base + 13, TZ), :], -32)
            tables[key] = jnp.where(lane3 < 64, low, high)
        else:
            tables[key] = recv[pl.ds(base + chunk.tail + 2, TZ), :]
    table[...] = jnp.zeros((128, 128), jnp.float32)
    lane1 = lanes_of((1, 128))
    for x in range(4):
        for y in range(4):
            value = tables[((-1, 0, 0, 1)[x], (-1, 0, 0, 1)[y])]
            g = (1, 0, 1, 0)[x] * 2 + (1, 0, 1, 0)[y]
            row = jnp.zeros((1, 128), jnp.float32)
            for t in range(TZ):
                here = (lane1 >= 32 * t) & (lane1 < 32 * t + 32)
                row = jnp.where(here, turn(value[t : t + 1], 32 * g - 32 * t), row)
            table[4 * x + y : 4 * x + y + 1, :] = row
    by_code = jnp.transpose(table[...])
    big = (128, 128)
    for x in range(4):
        pick = jnp.where(rows_of(big) == 4 * x + lanes_of(big) // 32, 1.0, 0.0)
        alive = jnp.dot(by_code, pick, preferred_element_type=jnp.float32)
        spread_ref[128 * x : 128 * x + 128, :] = FAR_AWAY * (1.0 - alive)

    lane = lanes_of()
    half_layer = lane % 8
    parity = lane % 2
    cell_y = lane // 8 % 4
    low_rows = rows_of() < 4

    def crossing(position, step):
        return (position + step < 0) | (position + step >= 8)

    groups = grouped(NEAR + FAR)

    def at_t(t, carry):
        for code in range(27):
            for block in range(2):
                first, second = [
                    spread_ref[pl.ds(128 * x + 32 * t + code, 1), :] for x in (2 * block, 2 * block + 1)
                ]
                cases[16 * code + 8 * block : 16 * code + 8 * block + 8, :] = jnp.where(
                    low_rows, jnp.broadcast_to(first, (8, 128)), jnp.broadcast_to(second, (8, 128))
                )

        def case(ex, ey, ez, block):
            code = 9 * (ex + 1) + 3 * (ey + 1) + ez + 1
            return cases[16 * code + 8 * block : 16 * code + 8 * block + 8, :]

        for dz in sorted({key[1] for key, _ in groups}):
            cross_z = crossing(half_layer, dz)
            in_z = {}

            def level_z(ex, ey, block):
                if (ex, ey, block) not in in_z:
                    value = case(ex, ey, 0, block)
                    if dz:
                        value = jnp.where(cross_z, case(ex, ey, sign(dz), block), value)
                    in_z[(ex, ey, block)] = value
                return in_z[(ex, ey, block)]

            for (dy, other_z), dxs in groups:
                if other_z != dz:
                    continue
                cross_y = crossing(2 * cell_y + parity, dy)
                in_y = {}

                def level_y(ex, block):
                    if (ex, block) not in in_y:
                        value = level_z(ex, 0, block)
                        if dy:
                            value = jnp.where(cross_y, level_z(ex, sign(dy), block), value)
                        in_y[(ex, block)] = value
                    return in_y[(ex, block)]

                for dx in dxs:
                    cross_x = crossing(2 * (rows_of() % 4) + parity, dx)
                    for block in range(2):
                        value = level_y(0, block)
                        if dx:
                            value = jnp.where(cross_x, level_y(sign(dx), block), value)
                        at = (MASK_SLOT[(dx, dy, dz)] * TZ + t) * 16 + 8 * block
                        masks_ref[pl.ds(pl.multiple_of(at, 8), 8), :] = value
        return carry

    lax.fori_loop(0, TZ, at_t, 0)


def step_kernel(
    step,
    across,
    arriving,
    leaving,
    groups,
    limit,
    recv,
    in_u,
    in_v,
    in_noise,
    *rest,
):
    nx, ny = across
    owners = nx * ny
    plane_total = owners
    rest = list(rest)
    if step == 0:
        live = rest.pop(0)
    else:
        masks_ref = rest.pop(0)
        in_grid = rest.pop(0)
        in_bad = rest.pop(0)
    send, out_u, out_v = rest[:3]
    rest = rest[3:]
    out_grid = rest.pop(0)
    out_bad = rest.pop(0)
    if step == 0:
        masks_ref = rest.pop(0)
    window, rolled, moved, slope, slope_moved = rest[:5]
    extra = rest[5:]
    ids = neighbour_ids(across)
    lane = lanes_of()
    lane1 = lanes_of((1, 128))

    tail = recv[pl.ds(arriving.tail, owners, stride=arriving.rows), :]
    tail = spread(tail, lanes_of((owners, 128)), arriving)
    if step == 0:
        table = extra[0]
        table[...] = jnp.zeros((128, 128), jnp.float32)
        table[0:owners, :] = tail
        turned = jnp.transpose(table[...])[:owners]
        reach = 128
        while reach > owners:
            reach //= 2
            turned = turned + pltpu.roll(turned, reach, 1)
        grid = [turned[ny * x : ny * x + ny] for x in range(nx)]
        out_bad[...] = jnp.zeros((8, 128), jnp.float32)
        make_masks(arriving, across, recv, live, masks_ref, *extra)
    else:
        grid = [
            in_grid[ny * x : ny * x + ny, :] + tail[ny * x : ny * x + ny] * (1.0 / heat_capacity)
            for x in range(nx)
        ]
        grid = diffuse_grid(grid, across)
        furthest = recv[pl.ds(arriving.tail + 1, owners, stride=arriving.rows), :]
        furthest = jnp.where(lanes_of((owners, 128)) >= arriving.tail_lane, furthest, 0.0)
        reached = jnp.max(furthest, axis=0, keepdims=True)
        reached = jnp.max(reached, axis=1, keepdims=True)
        over = jnp.broadcast_to(jnp.where(reached > limit, 1.0, 0.0), (8, 128))
        out_bad[...] = jnp.maximum(in_bad[...], over)
    for x in range(nx):
        out_grid[ny * x : ny * x + ny, :] = grid[x]
    column = out_grid[pl.ds(ids[(0, 0)], 1), :]
    column = jnp.broadcast_to(jnp.where(lane1 < plane_total, column, 0.0), (8, 128))

    def masks(dx, dy, dz, t, row):
        at = (MASK_SLOT[(dx, dy, dz)] * TZ + t) * 16
        return masks_ref[pl.ds(pl.multiple_of(at, 8) + row, 8), :]

    def own_u(plane):
        return in_u[8 * plane : 8 * plane + 8, :]

    build_window(own_u, recv, window, arriving, ids)
    shifts = lane_shifts(groups)
    shifted_planes(9, window, rolled, moved, groups, shifts, coordinate_shift)
    densities(window, moved, masks, slope, groups)
    shifted_planes(3, slope, rolled, slope_moved, groups, shifts, no_shift)

    active = (lane >= 32) & (lane < 96)
    power = []
    furthest = jnp.zeros((8, 128), jnp.float32)
    for t in range(TZ):
        local = exact_dot(column, layer_matrix(t, plane_total, False))[0:1]
        kick = jnp.sqrt(local * (2.0 * friction * atom_mass / time_step))
        force = forces(t, window, moved, slope, slope_moved, masks, groups)
        layer = jnp.zeros((8, 128), jnp.float32)
        for c in range(3):
            at = 8 * (c * TZ + t)
            speed = in_v[at : at + 8, :]
            push = force[c] - friction * atom_mass * speed + kick * in_noise[72 * step + at : 72 * step + at + 8, :]
            speed = speed + time_step / atom_mass * push
            speed = jnp.where(active, speed, 0.0)
            place = own_u(c * TZ + t) + time_step * speed
            out_v[at : at + 8, :] = speed
            out_u[at : at + 8, :] = place
            layer = layer + speed * speed
            furthest = jnp.maximum(furthest, jnp.abs(place))
        power.append(jnp.sum(layer, axis=0, keepdims=True))
    energy = jnp.zeros((8, 128), jnp.float32)
    for t in range(TZ):
        energy = energy + exact_dot(
            jnp.broadcast_to(power[t], (8, 128)), layer_matrix(t, plane_total, True)
        )
    energy = energy[0:1] * (friction * atom_mass * time_step)
    if leaving is None:
        send[...] = jnp.broadcast_to(energy, (owners, 128))
        return
    furthest = jnp.max(furthest, axis=0, keepdims=True)
    furthest = jnp.broadcast_to(jnp.max(furthest, axis=1, keepdims=True), (1, 128))
    place_halo(
        lambda plane: out_u[8 * plane : 8 * plane + 8, :],
        send,
        leaving,
        ids,
        [(0, energy), (1, furthest)],
    )


def finish(across, recv, in_grid, in_u, in_v, heat, new_u, new_v):
    nx, ny = across
    owners = nx * ny
    grid = [
        in_grid[ny * x : ny * x + ny, :] + recv[ny * x : ny * x + ny, :] * (1.0 / heat_capacity)
        for x in range(nx)
    ]
    grid = diffuse_grid(grid, across)
    me = lax.axis_index("gx") * ny + lax.axis_index("gy")
    flat = rows_of((ny, 128)) == lanes_of((ny, 128))
    for x in range(nx):
        mine = jnp.where(lanes_of((ny, 128)) == me, grid[x], 0.0)
        mine = jnp.broadcast_to(jnp.sum(mine, axis=1, keepdims=True), (ny, 128))
        row = jnp.sum(jnp.where(flat, mine, 0.0), axis=0, keepdims=True)
        heat[x : x + 1, :] = row
    lane3 = lanes_of((TZ, 128))
    for source, out in ((in_u, new_u), (in_v, new_v)):
        for c in range(3):
            for ix in range(BXT):
                rows = [source[pl.ds(c * TZ * 8 + CB * ix + cx, TZ, stride=8), :] for cx in range(CB)]
                for iy in range(BYT):
                    value = None
                    for cx in range(CB):
                        piece = turn(rows[cx], 32 + 32 * iy - 32 * cx)
                        value = piece if value is None else jnp.where(lane3 >= 32 * cx, piece, value)
                    out[c, ix, iy] = value


def exchange(value):
    return lax.all_to_all(value, ("gx", "gy"), split_axis=0, concat_axis=0, tiled=True)


VMEM_BYTES = 24 * 1024 * 1024


def call(kernel, outs, scratch, operands, smem=(), name=None):
    specs = [
        pl.BlockSpec(memory_space=pltpu.SMEM if n in smem else pltpu.VMEM)
        for n in range(len(operands))
    ]
    return pl.pallas_call(
        kernel,
        out_shape=[jax.ShapeDtypeStruct(shape, jnp.float32) for shape in outs],
        in_specs=specs,
        out_specs=[pl.BlockSpec(memory_space=pltpu.VMEM)] * len(outs),
        scratch_shapes=scratch,
        compiler_params=pltpu.CompilerParams(vmem_limit_bytes=VMEM_BYTES),
        name=name,
    )(*operands)


def stencil_steps(displacement, velocity, noise, electron_temp, pair_list, pair_count):
    across = (lax.axis_size("gx"), lax.axis_size("gy"))
    owners = across[0] * across[1]
    f32 = jnp.float32
    slots = pair_list.shape[-1]
    two, three = Chunk(owners, 2), Chunk(owners, 3)
    send, own_u, own_v, own_noise, live = call(
        partial(prepare, across, two),
        [(owners * two.rows, 128), (72, 128), (72, 128), (72 * STEPS, 128), (8, 128)],
        [pltpu.VMEM((8, (slots + 127) // 128 * 128), jnp.int32)],
        (displacement, velocity, noise, electron_temp, pair_list, pair_count),
        smem=(5,),
        name="prepare",
    )
    near, far = grouped(NEAR), grouped(NEAR + FAR)
    grid_shape = (owners, 128)
    plan = [(two, two, near, 1.0), (two, three, near, NEAR_LIMIT), (three, three, far, FAR_LIMIT), (three, None, far, FAR_LIMIT)]
    masks = grid = bad = None
    for step, (arriving, leaving, groups, limit) in enumerate(plan):
        recv = exchange(send)
        send_shape = (owners, 128) if leaving is None else (owners * leaving.rows, 128)
        outs = [send_shape, (72, 128), (72, 128), grid_shape, (8, 128)]
        scratch = [
            pltpu.VMEM((9 * ROWS, 128), f32),
            pltpu.VMEM((len(lane_shifts(groups)) * 9 * ROWS, 128), f32),
            pltpu.VMEM((len(groups) * 9 * ROWS, 128), f32),
            pltpu.VMEM((3 * ROWS, 128), f32),
            pltpu.VMEM((len(groups) * 3 * ROWS, 128), f32),
        ]
        if step == 0:
            outs.append((MASKS * TZ * 16, 128))
            scratch += [
                pltpu.VMEM((128, 128), f32),
                pltpu.VMEM((512, 128), f32),
                pltpu.VMEM((27 * 16, 128), f32),
            ]
            operands = (recv, own_u, own_v, own_noise, live)
        else:
            operands = (recv, own_u, own_v, own_noise, masks, grid, bad)
        got = call(
            partial(step_kernel, step, across, arriving, leaving, groups, limit),
            outs,
            scratch,
            operands,
            name=f"step{step}",
        )
        send, own_u, own_v, grid, bad = got[:5]
        if step == 0:
            masks = got[5]
    recv = exchange(send)
    heat, new_u, new_v = call(
        partial(finish, across),
        [(across[0], 128), displacement.shape, velocity.shape],
        [],
        (recv, grid, own_u, own_v),
        name="finish",
    )
    return bad[0, 0], new_u, new_v, heat[:, : across[1]].reshape(electron_temp.shape)


def per_device(displacement, velocity, noise, electron_temp, pair_list, pair_count):
    given = (displacement, velocity, noise, electron_temp, pair_list, pair_count)
    bad, new_u, new_v, heat = stencil_steps(*given)
    return lax.cond(bad > 0.5, lambda: whole_sweep(*given), lambda: (new_u, new_v, heat))


def solution(mesh):
    placed = (
        P(None, "gx", "gy", None, None),
        P(None, "gx", "gy", None, None),
        P(None, None, "gx", "gy", None, None),
        P(("gx", "gy"), None, None),
        P("gx", "gy", None, None),
        P("gx", "gy"),
    )
    return jax.shard_map(
        per_device,
        mesh=mesh,
        in_specs=placed,
        out_specs=(
            P(None, "gx", "gy", None, None),
            P(None, "gx", "gy", None, None),
            P(("gx", "gy"), None, None),
        ),
        check_vma=False,
    )
```

```python
from functools import partial

import jax
import jax.numpy as jnp
from jax import lax
from jax.experimental import pallas as pl
from jax.experimental.pallas import tpu as pltpu
from jax.sharding import PartitionSpec as P

CB = 4
TILE = 128
BXT = 2
BYT = 2
TZ = 3
TILES = 12
STEPS = 4
SUB = 6


lattice_edge = 3.1652
density_cut = 4.400224
embed_scale = 1.896373
pair_cut = 3.25
coef_zero = 47.1346499
coef_one = -33.7665655
coef_two = 6.2541999
time_step = 0.005
atom_mass = 0.0190534
friction = 1.0
heat_capacity = 0.02
diffusion_rate = 0.12


def padded_2(block, sides, width):
    for axis, dim in sides:
        count = lax.axis_size(axis)
        forward = [(i, i + 1) for i in range(count - 1)]
        forward.append((count - 1, 0))
        backward = [(target, source) for source, target in forward]
        low = lax.ppermute(
            lax.slice_in_dim(block, block.shape[dim] - width, None, axis=dim), axis, forward
        )
        high = lax.ppermute(lax.slice_in_dim(block, 0, width, axis=dim), axis, backward)
        block = jnp.concatenate([low, block, high], axis=dim)
    return block


def lattice_sites():
    serial = jnp.arange(TILE, dtype=jnp.int32)
    cell_number = serial // 2
    half_step = (serial % 2).astype(jnp.float32) * 0.5
    corners = jnp.stack([cell_number // (CB * CB), cell_number // CB % CB, cell_number % CB])
    return lattice_edge * (corners.astype(jnp.float32) + half_step[None, :])


def plane_table(plane_total):
    serial = jnp.arange(TILE, dtype=jnp.int32)
    cell_number = serial // 2
    layer = 2 * (cell_number % CB) + serial % 2
    tiles = jnp.arange(TZ, dtype=jnp.int32)
    whole = tiles[:, None] * (2 * CB) + layer[None, :]
    return whole * plane_total // (2 * CB * TZ)


def pair_geometry(window, tile_index, neighbour_code, lattice):
    wide_y = BYT + 2
    depth_t = tile_index % TZ
    inner_y = tile_index // TZ % BYT
    inner_x = tile_index // (TZ * BYT)
    shift_x = neighbour_code // 9
    shift_y = neighbour_code // 3 % 3
    shift_z = neighbour_code % 3
    flattened = window.reshape(window.shape[0], (BXT + 2) * wide_y * TZ, TILE)
    own_index = ((inner_x + 1) * wide_y + inner_y + 1) * TZ + depth_t
    other_index = ((inner_x + shift_x) * wide_y + inner_y + shift_y) * TZ + (
        depth_t + shift_z - 1 + TZ
    ) % TZ
    own_tile = lax.dynamic_index_in_dim(flattened, own_index, 1, keepdims=False)
    other_tile = lax.dynamic_index_in_dim(flattened, other_index, 1, keepdims=False)
    offset = jnp.stack([shift_x - 1, shift_y - 1, shift_z - 1]).astype(jnp.float32) * (
        CB * lattice_edge
    )
    left = lattice + own_tile
    right = lattice + other_tile + offset[:, None]
    delta = left[:, :, None] - right[:, None, :]
    square = jnp.sum(delta * delta, axis=0)
    serial = jnp.arange(TILE, dtype=jnp.int32)
    same_atom = (neighbour_code == 13) & (serial[:, None] == serial[None, :])
    distance = jnp.sqrt(jnp.where(same_atom, 100.0, square))
    return (delta, distance, own_index, other_index)


def density_term(window, lattice, tile_index, neighbour_code):
    delta, distance, own_index, other_index = pair_geometry(
        window, tile_index, neighbour_code, lattice
    )
    dens_gap = distance - density_cut
    return jnp.sum(jnp.where(distance < density_cut, dens_gap * dens_gap, 0.0), axis=1)[None]


def force_term(window, embed_window, lattice, tile_index, neighbour_code):
    delta, distance, own_index, other_index = pair_geometry(
        window, tile_index, neighbour_code, lattice
    )
    flat_embed = embed_window.reshape((BXT + 2) * (BYT + 2) * TZ, TILE)
    own_embed = lax.dynamic_index_in_dim(flat_embed, own_index, 0, keepdims=False)
    other_embed = lax.dynamic_index_in_dim(flat_embed, other_index, 0, keepdims=False)
    pair_gap = distance - pair_cut
    poly = coef_zero + coef_one * distance + coef_two * distance * distance
    pair_slope = jnp.where(
        distance < pair_cut,
        2.0 * pair_gap * poly + pair_gap * pair_gap * (coef_one + 2.0 * coef_two * distance),
        0.0,
    )
    dens_gap = distance - density_cut
    dens_slope = jnp.where(distance < density_cut, 2.0 * dens_gap, 0.0)
    scalar = (pair_slope + (own_embed[:, None] + other_embed[None, :]) * dens_slope) / distance
    return -jnp.sum(scalar[None] * delta, axis=2)


def sweep_pairs(term_fn, channels, pair_table, pair_total):
    initial = jnp.zeros((channels, TILES, TILE), jnp.float32)

    def block_add(block_index, running):
        start = block_index * 27
        chosen = lax.dynamic_slice_in_dim(pair_table, start, 27, 1)
        live = start + jnp.arange(27, dtype=jnp.int32) < pair_total
        terms = jax.vmap(term_fn)(chosen[0], chosen[1])
        terms = jnp.where(live[:, None, None], terms, 0.0)
        return running.at[:, chosen[0]].add(jnp.swapaxes(terms, 0, 1))

    blocks = (pair_total + 26) // 27
    total = lax.fori_loop(0, blocks, block_add, initial)
    return total.reshape(channels, BXT, BYT, TZ, TILE)


def relax_slab(padded):
    center = padded[1:-1]
    beside_all = padded[2:] + padded[:-2] + jnp.roll(center, 1, 1) + jnp.roll(center, -1, 1)
    beside_all = beside_all + jnp.roll(center, 1, 2) + jnp.roll(center, -1, 2)
    return center + diffusion_rate * (beside_all - 6.0 * center)


def one_step(lattice, pair_table, pair_total, planes, owners, across, carry, noise_now):
    positions, speeds, heat_field = carry
    slab_depth = heat_field.shape[0]
    plane_total = slab_depth * owners
    arrived = lax.all_to_all(
        heat_field.reshape(slab_depth, owners), ("gx", "gy"), split_axis=1, concat_axis=0, tiled=True
    )
    column = arrived.reshape(-1)
    column_temp = jnp.take(column, planes).reshape(TZ, TILE)
    local_temp = jnp.broadcast_to(column_temp, (BXT, BYT, TZ, TILE))
    window = padded_2(positions, (("gx", 1), ("gy", 2)), 1)
    density = sweep_pairs(partial(density_term, window, lattice), 1, pair_table, pair_total)
    embed_slope = -embed_scale / (2.0 * jnp.sqrt(density))
    embed_window = padded_2(embed_slope, (("gx", 1), ("gy", 2)), 1)
    force = sweep_pairs(partial(force_term, window, embed_window, lattice), 3, pair_table, pair_total)
    kicker = jnp.sqrt(2.0 * friction * atom_mass * local_temp / time_step)[None] * noise_now
    speeds = speeds + time_step / atom_mass * (force - friction * atom_mass * speeds + kicker)
    positions = positions + time_step * speeds
    power = friction * atom_mass * time_step * jnp.sum(speeds * speeds, axis=0)
    tile_power = jnp.sum(power, axis=(0, 1)).reshape(-1)
    energy = jnp.zeros((plane_total,), jnp.float32).at[planes].add(tile_power)
    arrived = lax.all_to_all(
        energy.reshape(plane_total, 1), ("gx", "gy"), split_axis=0, concat_axis=1, tiled=True
    )
    heat_field = heat_field + arrived.reshape(slab_depth, *across) / heat_capacity

    def relax(sub_index, heat):
        return relax_slab(padded_2(heat, ((("gx", "gy"), 0),), 1))

    heat_field = lax.fori_loop(0, SUB, relax, heat_field)
    return (positions, speeds, heat_field)


def whole_sweep(displacement, velocity, noise, electron_temp, pair_list, pair_count):
    across = (lax.axis_size("gx"), lax.axis_size("gy"))
    owners = across[0] * across[1]
    planes = plane_table(electron_temp.shape[0] * owners).reshape(-1)
    step = partial(
        one_step, lattice_sites(), pair_list[0, 0], pair_count[0, 0], planes, owners, across
    )
    return lax.fori_loop(
        0,
        STEPS,
        lambda n, carry: step(carry, lax.dynamic_index_in_dim(noise, n, 0, keepdims=False)),
        (displacement, velocity, electron_temp),
    )


NEAR_SHELLS = (3, 4, 8)
FAR_SHELLS = (11, 12)
NEAR_LIMIT = 0.2900
FAR_LIMIT = 0.8170
HALF = 0.5 * lattice_edge
FAR_AWAY = 1.0e6
ROWS = 20
BASE = 2
SIZE = TZ * ROWS
EDGES = (2, 3)


def site_offsets(shells):
    span = range(-3, 4)
    found = []
    for x in span:
        for y in span:
            for z in span:
                if x % 2 == y % 2 == z % 2 and x * x + y * y + z * z in shells:
                    found.append((x, y, z))
    return found


def grouped(offsets):
    table = {}
    for x, y, z in offsets:
        table.setdefault((y, z), []).append(x)
    return sorted(table.items())


NEAR = site_offsets(NEAR_SHELLS)
FAR = site_offsets(FAR_SHELLS)
MASK_SLOT = {offset: slot for slot, offset in enumerate(NEAR + FAR)}
MASKS = len(MASK_SLOT)


def by_x(groups):
    table = {}
    for n, ((dy, dz), dxs) in enumerate(groups):
        for dx in dxs:
            table.setdefault(dx, []).append((n, dy, dz))
    return sorted(table.items())


def sign(value):
    return (value > 0) - (value < 0)


def sources(dy, dz):
    s = sign(dz)
    if dy % 2 == 0:
        k = dy // 2
        out = [(None, 0, dz + 8 * k, 0)]
        if s:
            out.append((None, s, dz - 8 * s + 8 * k, 0))
        return out
    low = (dy - 1) // 2
    out = [(0, 0, dz + 8 * low, 0), (1, 0, dz + 8 * (low + 1), 1)]
    for parity, k in ((0, low), (1, low + 1)):
        if any(not 0 <= iz + dz < 8 for iz in range(parity, 8, 2)):
            out.append((parity, s, dz - 8 * s + 8 * k, parity))
    return out


def lanes_of(shape=(8, 128)):
    return lax.broadcasted_iota(jnp.int32, shape, len(shape) - 1)


def rows_of(shape=(8, 128)):
    return lax.broadcasted_iota(jnp.int32, shape, len(shape) - 2)


def turn(value, amount):
    amount = (-amount) % 128
    return value if amount == 0 else pltpu.roll(value, amount, value.ndim - 1)


def pick_lanes(value, index):
    return jnp.take_along_axis(value, index, axis=1, mode="promise_in_bounds")


class Chunk:
    def __init__(self, owners, cells, first=False):
        self.cells = cells
        self.narrow = owners <= 32
        halo = 9 if cells == 2 else 14
        if self.narrow:
            self.tail = 9 if cells == 2 else 13
            self.tail_lane = 96
            self.reach = (self.tail, 64)
            self.rows = self.tail + 1
        else:
            self.tail = halo
            self.tail_lane = 0
            self.reach = (halo + 1, 64)
            self.rows = halo + 2
        if first:
            self.live = [(self.reach[0], 0), (self.rows, 0), (self.rows, 64)]
            self.rows += 1

    def x_home(self, plane, row):
        if plane < 8:
            return self.cells * (plane // 2) + row, plane % 2
        return 4 * self.cells + row // 2, row % 2


def repeat_tail(value, chunk):
    if not chunk.narrow:
        return value
    return pick_lanes(value, 96 + lanes_of(value.shape) % 32)


def from_tiles(read, out):
    lane = lanes_of((TZ, 128))
    own = (lane >= 32) & (lane < 96)
    for c in range(3):
        for ix in range(BXT):
            first, second = [read(c, ix, iy) for iy in range(BYT)]
            for cx in range(CB):
                both = jnp.where(lane < 64, turn(first, 32 * cx - 32), turn(second, 32 * cx - 64))
                start = c * TZ * 8 + CB * ix + cx
                out[pl.ds(start, TZ, stride=8), :] = jnp.where(own, both, 0.0)


def to_tiles(source, out):
    lane = lanes_of((TZ, 128))
    for c in range(3):
        for ix in range(BXT):
            rows = [source[pl.ds(c * TZ * 8 + CB * ix + cx, TZ, stride=8), :] for cx in range(CB)]
            for iy in range(BYT):
                value = None
                for cx in range(CB):
                    piece = turn(rows[cx], 32 + 32 * iy - 32 * cx)
                    value = piece if value is None else jnp.where(lane >= 32 * cx, piece, value)
                out[c, ix, :, iy, :] = value


def stage_halo(own, stage, chunk, tail_row, extras):
    w = chunk.cells
    lane, row = lanes_of(), rows_of()
    kinds = {}
    depth = stage.shape[0] // 4
    low = lane < 64
    third = [pick for pick in range(5)] if w == 3 else []
    for kind, (axis, side) in enumerate((("x", -1), ("x", 1), ("y", -1), ("y", 1))):
        at = kind * depth
        kinds[(axis, side)] = at
        if axis == "x":
            first = 8 - w if side == 1 else 0
            for pair in range(4):
                both = jnp.where(low, turn(own(2 * pair), 32), turn(own(2 * pair + 1), -32))
                stage[at + w * pair : at + w * pair + w, :] = both[first : first + w]
            last = own(8)
            a, b = turn(last, 32), turn(last, -32)
            low1 = lanes_of((1, 128)) < 64
            stage[at + 4 * w : at + 4 * w + 1, :] = jnp.where(
                low1, a[first : first + 1], b[first + 1 : first + 2]
            )
            if w == 3:
                stage[at + 13 : at + 14, :] = a[first + 2 : first + 3]
        else:
            start = 80 if side == 1 else 32
            packed = None
            for plane in range(8):
                piece = turn(own(plane), start - 16 * plane)
                packed = piece if packed is None else jnp.where(lane >= 16 * plane, piece, packed)
            stage[at : at + 8, :] = packed
            flat = pick_lanes(own(8), start + lane % 16)
            flat = jnp.where(lane // 16 == row, flat, 0.0)
            stage[at + 8 : at + 9, :] = jnp.sum(flat, axis=0, keepdims=True)
            start = 72 if side == 1 else 48
            for pair in third:
                flat = pick_lanes(own(2 * pair), start + lane % 8)
                if pair < 4:
                    flat = jnp.where(low, flat, pick_lanes(own(2 * pair + 1), start + lane % 8))
                flat = jnp.where(lane % 64 // 8 == row, flat, 0.0)
                stage[at + 9 + pair : at + 10 + pair, :] = jnp.sum(flat, axis=0, keepdims=True)
        for (where, lane_from, lane_to), value in tail_row + extras.get((axis, side), []):
            lane1 = lanes_of((1, 128))
            old = stage[at + where : at + where + 1, :]
            here = (lane1 >= lane_from) & (lane1 < lane_to)
            stage[at + where : at + where + 1, :] = jnp.where(here, value, old)
    return kinds


def send_chunks(stage, kinds, send_ref, chunk, ids, owners):
    tails = sorted({chunk.tail, chunk.reach[0]})
    at = kinds[("x", 1)]
    rows = {where: stage[at + where : at + where + 1, :] for where in tails}

    def fill(index, carry):
        for where in tails:
            send_ref[index, :, 128 * where : 128 * where + 128] = rows[where]
        return carry

    lax.fori_loop(0, owners, fill, 0, unroll=8)
    for (sx, sy), ident in ids.items():
        if (sx, sy) == (0, 0):
            continue
        at = kinds[("y", sy)] if sy else kinds[("x", sx)]
        for k in range(chunk.rows):
            send_ref[ident, :, 128 * k : 128 * k + 128] = stage[at + k : at + k + 1, :]


def receive_chunks(recv_ref, landed, tails_at, chunk, ids, owners):
    depth = landed.shape[0] // 9
    homes = {}
    for n, ((sx, sy), ident) in enumerate(ids.items()):
        if (sx, sy) == (0, 0):
            continue
        homes[(sx, sy)] = n * depth
        for k in range(chunk.rows):
            landed[n * depth + k : n * depth + k + 1, :] = recv_ref[ident, :, 128 * k : 128 * k + 128]

    tails = sorted({chunk.tail, chunk.reach[0]})

    def take(index, carry):
        for n, where in enumerate(tails):
            tails_at[pl.ds(n * owners + index, 1), :] = recv_ref[index, :, 128 * where : 128 * where + 128]
        return carry

    lax.fori_loop(0, owners, take, 0, unroll=8)
    return homes


def build_window(own, landed, homes, window, chunk):
    w = chunk.cells
    lane, row = lanes_of(), rows_of()
    zero = jnp.zeros((8, 128), jnp.float32)
    for plane in range(9):
        at = plane * ROWS + BASE
        centre = own(plane)
        before, after = zero, zero
        for sy in (-1, 1):
            target = 16 if sy == -1 else 96
            here = (lane >= target) & (lane < target + 16)
            beyond = 8 if sy == -1 else 112
            here_third = (lane >= beyond) & (lane < beyond + 8)
            for sx in (-1, 0, 1):
                base = homes[(sx, sy)]
                if plane < 8:
                    piece = turn(landed[base : base + 8, :], 16 * plane - target)
                else:
                    wide = jnp.broadcast_to(landed[base + 8 : base + 9, :], (8, 128))
                    piece = pick_lanes(wide, 16 * row + lane % 16)
                old = (before, centre, after)[sx + 1]
                new = jnp.where(here, piece, old)
                if w == 3:
                    wide = landed[base + 9 + plane // 2 : base + 10 + plane // 2, :]
                    wide = jnp.broadcast_to(wide, (8, 128))
                    piece = pick_lanes(wide, 64 * (plane % 2) + 8 * row + lane % 8)
                    new = jnp.where(here_third, piece, new)
                if sx == -1:
                    before = new
                elif sx == 0:
                    centre = new
                else:
                    after = new
        window[at + 4 : at + 12, :] = centre
        window[at : at + 4, :] = before[4:]
        window[at + 12 : at + 16, :] = after[:4]
        here1 = (lanes_of((1, 128)) >= 32) & (lanes_of((1, 128)) < 96)
        for sx in (-1, 1):
            base = homes[(sx, 0)]
            for k in range(w):
                home, half = chunk.x_home(plane, k)
                piece = turn(landed[base + home : base + home + 1, :], -32 if half == 0 else 32)
                to = at + (4 - w + k if sx == -1 else 12 + k)
                old = window[to : to + 1, :]
                window[to : to + 1, :] = jnp.where(here1, piece, old)


def shifted_planes(count, source, out, groups, constants):
    half_layer = lanes_of((16, 128)) % 8
    parity = half_layer % 2
    for n, ((dy, dz), _) in enumerate(groups):
        carried = (half_layer + dz >= 8) | (half_layer + dz < 0)
        for c in range(count):
            for t in range(TZ):
                value = None
                for want, carry_z, shift, down in sources(dy, dz):
                    row = (c * TZ + (t + carry_z) % TZ) * ROWS + BASE + down
                    piece = turn(source[row : row + 16, :], shift)
                    if value is None:
                        value = piece
                        continue
                    here = None
                    if want is not None:
                        here = parity == want
                    if carry_z:
                        here = carried if here is None else here & carried
                    value = jnp.where(here, piece, value)
                shift_by = constants(c, dy, dz)
                if shift_by:
                    value = value + shift_by
                at = n * count * SIZE + (c * TZ + t) * ROWS + BASE
                out[at : at + 16, :] = value


def coordinate_shift(c, dy, dz):
    return (0.0, HALF * dy, HALF * dz)[c]


def no_shift(c, dy, dz):
    return 0.0


def row_start(dx):
    return dx // 2 if dx % 2 == 0 else (dx - 1) // 2


def densities(window, moved, masks_ref, slope, gaps, inverses, groups):
    def sweep(rows, keep):
        own = [window[rows(c * SIZE), :] for c in range(3)]
        total = jnp.zeros(own[0].shape, jnp.float32)
        for dx, parts in by_x(groups):
            down = row_start(dx)
            own_x = own[0] - HALF * dx
            for n, dy, dz in parts:
                other = [moved[rows((3 * n + c) * SIZE + down), :] for c in range(3)]
                slot = MASK_SLOT[(dx, dy, dz)]
                ex = own_x - other[0]
                ey = own[1] - other[1]
                ez = own[2] - other[2]
                square = ex * ex + ey * ey + (ez * ez + masks_ref[rows(slot * SIZE), :])
                inverse = lax.rsqrt(square)
                gap = jnp.minimum(square * inverse - density_cut, 0.0)
                total = total + gap * gap
                if keep is not None:
                    gaps[keep + 24 * slot : keep + 24 * slot + 8, :] = gap
                    inverses[keep + 24 * slot : keep + 24 * slot + 8, :] = inverse
        slope[rows(0), :] = -embed_scale * lax.rsqrt(total)

    for t in range(TZ):
        sweep(lambda base: pl.ds(base + t * ROWS + BASE + 4, 8), 8 * t)
    for edge in EDGES:
        sweep(lambda base: pl.ds(base + BASE + edge, 2 * TZ, stride=ROWS // 2), None)


def forces(t, window, moved, slope, slope_moved, gaps, inverses, groups):
    at = t * ROWS + BASE + 4
    own = [window[c * SIZE + at : c * SIZE + at + 8, :] for c in range(3)]
    own_slope = slope[at : at + 8, :]
    first = 2.0 * (coef_zero + coef_one * pair_cut + coef_two * pair_cut * pair_cut)
    second = 3.0 * (coef_one + 2.0 * coef_two * pair_cut)
    third = 4.0 * coef_two
    zero = jnp.zeros((8, 128), jnp.float32)
    total = [zero, zero, zero]
    sum_all = zero
    for dx, parts in by_x(groups):
        down = row_start(dx)
        sum_here = zero
        for n, dy, dz in parts:
            slot = MASK_SLOT[(dx, dy, dz)]
            row = 3 * n * SIZE + at + down
            other_slope = slope_moved[n * SIZE + at + down : n * SIZE + at + down + 8, :]
            gap = gaps[24 * slot + 8 * t : 24 * slot + 8 * t + 8, :]
            inverse = inverses[24 * slot + 8 * t : 24 * slot + 8 * t + 8, :]
            near = jnp.minimum(gap + (density_cut - pair_cut), 0.0)
            scalar = (own_slope + other_slope) * gap + near * (first + near * (second + third * near))
            scalar = scalar * inverse
            sum_here = sum_here + scalar
            for c in range(3):
                total[c] = total[c] + scalar * moved[row + c * SIZE : row + c * SIZE + 8, :]
        sum_all = sum_all + sum_here
        if dx:
            total[0] = total[0] + (HALF * dx) * sum_here
    return [total[c] - own[c] * sum_all for c in range(3)]


def diffuse_grid(grid, across):
    nx, ny = across
    for _ in range(SUB):
        columns = []
        for x in range(nx):
            heat = grid[x]
            beside = grid[(x + 1) % nx] + grid[(x - 1) % nx]
            beside = beside + pltpu.roll(heat, 1, 0) + pltpu.roll(heat, ny - 1, 0)
            beside = beside + pltpu.roll(heat, 1, 1) + pltpu.roll(heat, 127, 1)
            columns.append(heat + diffusion_rate * (beside - 6.0 * heat))
        grid = columns
    return grid


LAYERS = 2 * CB * TZ


def temperatures_by_layer(column, plane_total):
    layer = 2 * CB * rows_of() + lanes_of() % (2 * CB)
    layer = jnp.minimum(layer, LAYERS - 1)
    return pick_lanes(jnp.broadcast_to(column, (8, 128)), layer * plane_total // LAYERS)


def energies_by_plane(power, plane_total):
    row, lane = rows_of(), lanes_of()
    stacked = jnp.zeros((8, 128), jnp.float32)
    for t in range(TZ):
        stacked = jnp.where(row == t, power[t], stacked)
    for shift in (8, 16, 32, 64):
        stacked = stacked + pltpu.roll(stacked, shift, 1)
    plane = lane % plane_total
    start = (plane * LAYERS + plane_total - 1) // plane_total
    total = jnp.zeros((8, 128), jnp.float32)
    for extra in range(max(1, -(-LAYERS // plane_total))):
        layer = start + extra
        inside = layer - 2 * CB * row
        here = (inside >= 0) & (inside < 2 * CB) & (layer < LAYERS)
        here = here & (layer * plane_total // LAYERS == plane)
        taken = pick_lanes(stacked, jnp.clip(inside, 0, 2 * CB - 1))
        total = total + jnp.where(here, taken, 0.0)
    return jnp.sum(total, axis=0, keepdims=True)


def neighbour_ids(across):
    nx, ny = across
    bx, by = lax.axis_index("gx"), lax.axis_index("gy")
    at_x = {-1: jnp.where(bx == 0, nx - 1, bx - 1), 0: bx, 1: jnp.where(bx == nx - 1, 0, bx + 1)}
    at_y = {-1: jnp.where(by == 0, ny - 1, by - 1), 0: by, 1: jnp.where(by == ny - 1, 0, by + 1)}
    return {(sx, sy): at_x[sx] * ny + at_y[sy] for sx in (-1, 0, 1) for sy in (-1, 0, 1)}


def prepare(across, chunk, disp, heat, pairs, count, send, own_u, live, lists, disp_in, heat_in, pairs_in, count_in, stage, sems):
    nx, ny = across
    owners = nx * ny
    copies = [
        pltpu.make_async_copy(source, target, sems.at[n])
        for n, (source, target) in enumerate(
            ((disp, disp_in), (heat, heat_in), (pairs, pairs_in), (count, count_in))
        )
    ]
    for copy in copies:
        copy.start()
    lists[...] = jnp.full(lists.shape, -1, jnp.int32)
    for copy in copies:
        copy.wait()

    from_tiles(lambda c, ix, iy: disp_in[c, ix, :, iy, :], own_u)

    slots = pairs_in.shape[3]
    width = lists.shape[1]
    lists[0:2, 0:slots] = pairs_in[0, 0]
    tile = lists[0:1, :]
    code = lists[1:2, :]
    valid = (lanes_of((1, width)) < count_in[0, 0]) & (tile >= 0)
    column = jnp.where(tile >= 3, 1, 0) + jnp.where(tile >= 6, 1, 0) + jnp.where(tile >= 9, 1, 0)
    depth = jnp.where(valid, tile - 3 * column, -1)
    place = 32 * column + code
    left = jnp.where(rows_of((8, width)) == depth, 1.0, 0.0)
    right = jnp.where(rows_of((128, width)) == place, 1.0, 0.0)
    found = lax.dot_general(
        left, right, (((1,), (1,)), ((), ())), preferred_element_type=jnp.float32
    )
    live[...] = found

    lane_n = lanes_of((nx, 128))
    planes = jnp.zeros((nx, 128), jnp.float32)
    for y in range(ny):
        value = jnp.broadcast_to(heat_in[0, :, y : y + 1], (nx, 128))
        planes = jnp.where(lane_n % ny == y, value, planes)
    planes = jnp.where(lane_n % owners // ny == rows_of((nx, 128)), planes, 0.0)
    field = jnp.sum(planes, axis=0, keepdims=True)

    lane = lanes_of()
    halves = {
        ("x", -1): found,
        ("x", 1): turn(found, 64),
        ("y", -1): jnp.where(lane < 32, found, turn(found, 32)),
        ("y", 1): jnp.where(lane < 32, turn(found, 32), turn(found, 64)),
    }
    extras = {}
    for key, value in halves.items():
        extras[key] = [
            ((where, to, to + 64), value[t : t + 1] if to == 0 else turn(value, -64)[t : t + 1])
            for t, (where, to) in enumerate(chunk.live)
        ]
    kinds = stage_halo(
        lambda plane: own_u[8 * plane : 8 * plane + 8, :],
        stage,
        chunk,
        [((chunk.tail, chunk.tail_lane, 128), field)],
        extras,
    )
    send_chunks(stage, kinds, send, chunk, neighbour_ids(across), owners)


def make_masks(chunk, homes, landed, live, masks_ref, table, spread_ref, cases):
    lane1 = lanes_of((1, 128))
    table[...] = jnp.zeros((128, 128), jnp.float32)
    for x in range(4):
        for y in range(4):
            sx, sy = (-1, 0, 0, 1)[x], (-1, 0, 0, 1)[y]
            ix, iy = (1, 0, 1, 0)[x], (1, 0, 1, 0)[y]
            row = jnp.zeros((1, 128), jnp.float32)
            for t in range(TZ):
                if (sx, sy) == (0, 0):
                    value, start = live[t : t + 1, :], 32 * (2 * ix + iy)
                else:
                    where, start = chunk.live[t]
                    value = landed[homes[(sx, sy)] + where : homes[(sx, sy)] + where + 1, :]
                    start = start + 32 * (ix if sy else iy)
                here = (lane1 >= 32 * t) & (lane1 < 32 * t + 32)
                row = jnp.where(here, turn(value, start - 32 * t), row)
            table[4 * x + y : 4 * x + y + 1, :] = row
    by_code = jnp.transpose(table[...])
    big = (128, 128)
    for x in range(4):
        pick = jnp.where(rows_of(big) == 4 * x + lanes_of(big) // 32, 1.0, 0.0)
        alive = jnp.dot(by_code, pick, preferred_element_type=jnp.float32)
        spread_ref[128 * x : 128 * x + 128, :] = FAR_AWAY * (1.0 - alive)

    lane = lanes_of()
    half_layer = lane % 8
    parity = lane % 2
    cell_y = lane // 8 % 4
    low_rows = rows_of() < 4

    def crossing(position, step):
        return (position + step < 0) | (position + step >= 8)

    groups = grouped(NEAR + FAR)

    def at_t(t, carry):
        for code in range(27):
            for block in range(2):
                first, second = [
                    spread_ref[pl.ds(128 * x + 32 * t + code, 1), :] for x in (2 * block, 2 * block + 1)
                ]
                cases[16 * code + 8 * block : 16 * code + 8 * block + 8, :] = jnp.where(
                    low_rows, jnp.broadcast_to(first, (8, 128)), jnp.broadcast_to(second, (8, 128))
                )

        def case(ex, ey, ez, block):
            code = 9 * (ex + 1) + 3 * (ey + 1) + ez + 1
            return cases[16 * code + 8 * block : 16 * code + 8 * block + 8, :]

        for dz in sorted({key[1] for key, _ in groups}):
            cross_z = crossing(half_layer, dz)
            in_z = {}

            def level_z(ex, ey, block):
                if (ex, ey, block) not in in_z:
                    value = case(ex, ey, 0, block)
                    if dz:
                        value = jnp.where(cross_z, case(ex, ey, sign(dz), block), value)
                    in_z[(ex, ey, block)] = value
                return in_z[(ex, ey, block)]

            for (dy, other_z), dxs in groups:
                if other_z != dz:
                    continue
                cross_y = crossing(2 * cell_y + parity, dy)
                in_y = {}

                def level_y(ex, block):
                    if (ex, block) not in in_y:
                        value = level_z(ex, 0, block)
                        if dy:
                            value = jnp.where(cross_y, level_z(ex, sign(dy), block), value)
                        in_y[(ex, block)] = value
                    return in_y[(ex, block)]

                for dx in dxs:
                    cross_x = crossing(2 * (rows_of() % 4) + parity, dx)
                    for block in range(2):
                        value = level_y(0, block)
                        if dx:
                            value = jnp.where(cross_x, level_y(sign(dx), block), value)
                        at = MASK_SLOT[(dx, dy, dz)] * SIZE + BASE + 8 * block
                        masks_ref[pl.ds(at + t * ROWS, 8), :] = value
        return carry

    lax.fori_loop(0, TZ, at_t, 0)


def step_kernel(step, across, arriving, leaving, groups, limit, *refs):
    nx, ny = across
    owners = nx * ny
    refs = list(refs)
    last = leaving is None

    def take(count):
        taken = refs[:count]
        del refs[:count]
        return taken

    recv, in_u, in_v, noise = take(4)
    if step == 0:
        (live,) = take(1)
    else:
        masks_ref, in_grid, in_bad = take(3)
    send, out_grid, out_bad, out_u, out_v = take(5)
    if step == 0:
        (masks_ref,) = take(1)
    window, moved, slope, slope_moved, gaps, inverses, landed, tails_at, noise_in, noise_own = take(10)
    sems, u_own, v_own, stage = take(4)
    extra = refs
    if not last:
        u_own, v_own = out_u, out_v
    noise_copy = pltpu.make_async_copy(noise.at[step], noise_in, sems.at[0])
    noise_copy.start()
    if step == 0:
        v_in, table, spread_ref, cases = extra
        v_copy = pltpu.make_async_copy(in_v, v_in, sems.at[1])
        v_copy.start()
    ids = neighbour_ids(across)
    lane = lanes_of()

    homes = receive_chunks(recv, landed, tails_at, arriving, ids, owners)
    if step == 0:
        make_masks(arriving, homes, landed, live, masks_ref, table, spread_ref, cases)

    def own_u(plane):
        return in_u[8 * plane : 8 * plane + 8, :]

    build_window(own_u, landed, homes, window, arriving)
    shifted_planes(3, window, moved, groups, coordinate_shift)
    densities(window, moved, masks_ref, slope, gaps, inverses, groups)
    shifted_planes(1, slope, slope_moved, groups, no_shift)

    tail = repeat_tail(tails_at[0:owners, :], arriving)
    if step == 0:
        table[...] = jnp.zeros((128, 128), jnp.float32)
        table[0:owners, :] = tail
        turned = jnp.transpose(table[...])[:owners]
        reach = 128
        while reach > owners:
            reach //= 2
            turned = turned + pltpu.roll(turned, reach, 1)
        grid = [turned[ny * x : ny * x + ny] for x in range(nx)]
        out_bad[...] = jnp.zeros((8, 128), jnp.float32)
    else:
        grid = [
            in_grid[ny * x : ny * x + ny, :] + tail[ny * x : ny * x + ny] * (1.0 / heat_capacity)
            for x in range(nx)
        ]
        grid = diffuse_grid(grid, across)
        where, start = arriving.reach
        from_row = owners * (where != arriving.tail)
        furthest = tails_at[from_row : from_row + owners, :]
        lane_n = lanes_of((owners, 128))
        furthest = jnp.where((lane_n >= start) & (lane_n < start + 32), furthest, 0.0)
        reached = jnp.max(furthest, axis=0, keepdims=True)
        reached = jnp.max(reached, axis=1, keepdims=True)
        over = jnp.broadcast_to(jnp.where(reached > limit, 1.0, 0.0), (8, 128))
        out_bad[...] = jnp.maximum(in_bad[...], over)
    for x in range(nx):
        out_grid[ny * x : ny * x + ny, :] = grid[x]
    local = temperatures_by_layer(out_grid[pl.ds(ids[(0, 0)], 1), :], owners)
    kick = jnp.sqrt(local * (2.0 * friction * atom_mass / time_step))

    noise_copy.wait()
    from_tiles(lambda c, ix, iy: noise_in[c, ix, :, iy, :], noise_own)
    speeds_in = in_v
    if step == 0:
        v_copy.wait()
        from_tiles(lambda c, ix, iy: v_in[c, ix, :, iy, :], v_own)
        speeds_in = v_own

    active = (lane >= 32) & (lane < 96)
    power = []
    furthest = jnp.zeros((8, 128), jnp.float32)
    for t in range(TZ):
        force = forces(t, window, moved, slope, slope_moved, gaps, inverses, groups)
        layer = jnp.zeros((8, 128), jnp.float32)
        for c in range(3):
            at = 8 * (c * TZ + t)
            speed = speeds_in[at : at + 8, :]
            push = force[c] - friction * atom_mass * speed + kick[t : t + 1] * noise_own[at : at + 8, :]
            speed = speed + time_step / atom_mass * push
            speed = jnp.where(active, speed, 0.0)
            place = own_u(c * TZ + t) + time_step * speed
            v_own[at : at + 8, :] = speed
            u_own[at : at + 8, :] = place
            layer = layer + speed * speed
            furthest = jnp.maximum(furthest, jnp.abs(place))
        power.append(jnp.sum(layer, axis=0, keepdims=True))
    energy = energies_by_plane(power, owners) * (friction * atom_mass * time_step)
    if last:
        send[...] = jnp.broadcast_to(energy, (owners, 128))
        to_tiles(u_own, out_u)
        to_tiles(v_own, out_v)
        return
    furthest = jnp.max(furthest, axis=0, keepdims=True)
    furthest = jnp.broadcast_to(jnp.max(furthest, axis=1, keepdims=True), (1, 128))
    where, start = leaving.reach
    tail_row = [
        ((leaving.tail, leaving.tail_lane, 128), energy),
        ((where, start, start + 32), furthest),
    ]
    kinds = stage_halo(
        lambda plane: u_own[8 * plane : 8 * plane + 8, :], stage, leaving, tail_row, {}
    )
    send_chunks(stage, kinds, send, leaving, ids, owners)


def finish(across, recv, in_grid, heat):
    nx, ny = across
    grid = [
        in_grid[ny * x : ny * x + ny, :] + recv[ny * x : ny * x + ny, :] * (1.0 / heat_capacity)
        for x in range(nx)
    ]
    grid = diffuse_grid(grid, across)
    me = lax.axis_index("gx") * ny + lax.axis_index("gy")
    flat = rows_of((ny, 128)) == lanes_of((ny, 128))
    for x in range(nx):
        mine = jnp.where(lanes_of((ny, 128)) == me, grid[x], 0.0)
        mine = jnp.broadcast_to(jnp.sum(mine, axis=1, keepdims=True), (ny, 128))
        row = jnp.sum(jnp.where(flat, mine, 0.0), axis=0, keepdims=True)
        heat[0, x : x + 1, :] = row[:, :ny]


def exchange(value):
    return lax.all_to_all(value, ("gx", "gy"), split_axis=0, concat_axis=0, tiled=True)


VMEM_BYTES = 28 * 1024 * 1024


def call(kernel, outs, scratch, operands, anywhere=(), name=None):
    specs = [
        pl.BlockSpec(memory_space=pl.ANY if n in anywhere else pltpu.VMEM)
        for n in range(len(operands))
    ]
    return pl.pallas_call(
        kernel,
        out_shape=[jax.ShapeDtypeStruct(shape, jnp.float32) for shape in outs],
        in_specs=specs,
        out_specs=[pl.BlockSpec(memory_space=pltpu.VMEM)] * len(outs),
        scratch_shapes=scratch,
        compiler_params=pltpu.CompilerParams(vmem_limit_bytes=VMEM_BYTES),
        name=name,
    )(*operands)


def stencil_steps(displacement, velocity, noise, electron_temp, pair_list, pair_count):
    across = (lax.axis_size("gx"), lax.axis_size("gy"))
    owners = across[0] * across[1]

    def vmem(*shape):
        return pltpu.VMEM(shape, jnp.float32)

    tiles = (3, BXT, TZ, BYT, TILE)
    placed_u = jnp.swapaxes(displacement, 2, 3)
    placed_v = jnp.swapaxes(velocity, 2, 3)
    placed_noise = jnp.swapaxes(noise, 3, 4)
    slots = pair_list.shape[-1]
    first, two, three = Chunk(owners, 2, True), Chunk(owners, 2), Chunk(owners, 3)
    send, own_u, live = call(
        partial(prepare, across, first),
        [(owners, 1, 128 * first.rows), (72, 128), (8, 128)],
        [
            pltpu.VMEM((8, (slots + 127) // 128 * 128), jnp.int32),
            vmem(*tiles),
            vmem(*electron_temp.shape),
            pltpu.VMEM(pair_list.shape, jnp.int32),
            pltpu.SMEM(pair_count.shape, jnp.int32),
            vmem(4 * 16, 128),
            pltpu.SemaphoreType.DMA((4,)),
        ],
        (placed_u, electron_temp, pair_list, pair_count),
        anywhere=(0, 1, 2, 3),
        name="prepare",
    )
    near, far = grouped(NEAR), grouped(NEAR + FAR)
    plan = [
        (first, two, near, 1.0),
        (two, three, near, NEAR_LIMIT),
        (three, three, far, FAR_LIMIT),
        (three, None, far, FAR_LIMIT),
    ]
    own_v = placed_v
    masks = grid = bad = None
    for step, (arriving, leaving, groups, limit) in enumerate(plan):
        recv = exchange(send)
        last = leaving is None
        pairs = sum(len(dxs) for _, dxs in groups)
        outs = [
            (owners, 128) if last else (owners, 1, 128 * leaving.rows),
            (owners, 128),
            (8, 128),
            tiles if last else (72, 128),
            tiles if last else (72, 128),
        ]
        scratch = [
            vmem(3 * SIZE, 128),
            vmem(len(groups) * 3 * SIZE, 128),
            vmem(SIZE, 128),
            vmem(len(groups) * SIZE, 128),
            vmem(24 * pairs, 128),
            vmem(24 * pairs, 128),
            vmem(9 * 16, 128),
            vmem(2 * owners, 128),
            vmem(*tiles),
            vmem(72, 128),
            pltpu.SemaphoreType.DMA((2,)),
            vmem(72, 128),
            vmem(72, 128),
            vmem(4 * 16, 128),
        ]
        if step == 0:
            outs.append((MASKS * SIZE, 128))
            scratch += [vmem(*tiles), vmem(128, 128), vmem(512, 128), vmem(27 * 16, 128)]
            operands = (recv, own_u, own_v, placed_noise, live)
        else:
            operands = (recv, own_u, own_v, placed_noise, masks, grid, bad)
        got = call(
            partial(step_kernel, step, across, arriving, leaving, groups, limit),
            outs,
            scratch,
            operands,
            anywhere=(2, 3) if step == 0 else (3,),
            name=f"step{step}",
        )
        send, grid, bad, own_u, own_v = got[:5]
        if step == 0:
            masks = got[5]
    recv = exchange(send)
    (heat,) = call(partial(finish, across), [electron_temp.shape], [], (recv, grid), name="finish")
    return bad[0, 0], jnp.swapaxes(own_u, 2, 3), jnp.swapaxes(own_v, 2, 3), heat


def per_device(displacement, velocity, noise, electron_temp, pair_list, pair_count):
    given = (displacement, velocity, noise, electron_temp, pair_list, pair_count)
    bad, new_u, new_v, heat = stencil_steps(*given)
    return lax.cond(bad > 0.5, lambda: whole_sweep(*given), lambda: (new_u, new_v, heat))


def solution(mesh):
    placed = (
        P(None, "gx", "gy", None, None),
        P(None, "gx", "gy", None, None),
        P(None, None, "gx", "gy", None, None),
        P(("gx", "gy"), None, None),
        P("gx", "gy", None, None),
        P("gx", "gy"),
    )
    return jax.shard_map(
        per_device,
        mesh=mesh,
        in_specs=placed,
        out_specs=(
            P(None, "gx", "gy", None, None),
            P(None, "gx", "gy", None, None),
            P(("gx", "gy"), None, None),
        ),
        check_vma=False,
    )
```

```python
from functools import partial

import jax
import jax.numpy as jnp
from jax import lax
from jax.experimental import pallas as pl
from jax.experimental.pallas import tpu as pltpu
from jax.sharding import PartitionSpec as P

CB = 4
TILE = 128
BXT = 2
BYT = 2
TZ = 3
TILES = 12
STEPS = 4
SUB = 6


lattice_edge = 3.1652
density_cut = 4.400224
embed_scale = 1.896373
pair_cut = 3.25
coef_zero = 47.1346499
coef_one = -33.7665655
coef_two = 6.2541999
time_step = 0.005
atom_mass = 0.0190534
friction = 1.0
heat_capacity = 0.02
diffusion_rate = 0.12


def padded_2(block, sides, width):
    for axis, dim in sides:
        count = lax.axis_size(axis)
        forward = [(i, i + 1) for i in range(count - 1)]
        forward.append((count - 1, 0))
        backward = [(target, source) for source, target in forward]
        low = lax.ppermute(
            lax.slice_in_dim(block, block.shape[dim] - width, None, axis=dim), axis, forward
        )
        high = lax.ppermute(lax.slice_in_dim(block, 0, width, axis=dim), axis, backward)
        block = jnp.concatenate([low, block, high], axis=dim)
    return block


def lattice_sites():
    serial = jnp.arange(TILE, dtype=jnp.int32)
    cell_number = serial // 2
    half_step = (serial % 2).astype(jnp.float32) * 0.5
    corners = jnp.stack([cell_number // (CB * CB), cell_number // CB % CB, cell_number % CB])
    return lattice_edge * (corners.astype(jnp.float32) + half_step[None, :])


def plane_table(plane_total):
    serial = jnp.arange(TILE, dtype=jnp.int32)
    cell_number = serial // 2
    layer = 2 * (cell_number % CB) + serial % 2
    tiles = jnp.arange(TZ, dtype=jnp.int32)
    whole = tiles[:, None] * (2 * CB) + layer[None, :]
    return whole * plane_total // (2 * CB * TZ)


def pair_geometry(window, tile_index, neighbour_code, lattice):
    wide_y = BYT + 2
    depth_t = tile_index % TZ
    inner_y = tile_index // TZ % BYT
    inner_x = tile_index // (TZ * BYT)
    shift_x = neighbour_code // 9
    shift_y = neighbour_code // 3 % 3
    shift_z = neighbour_code % 3
    flattened = window.reshape(window.shape[0], (BXT + 2) * wide_y * TZ, TILE)
    own_index = ((inner_x + 1) * wide_y + inner_y + 1) * TZ + depth_t
    other_index = ((inner_x + shift_x) * wide_y + inner_y + shift_y) * TZ + (
        depth_t + shift_z - 1 + TZ
    ) % TZ
    own_tile = lax.dynamic_index_in_dim(flattened, own_index, 1, keepdims=False)
    other_tile = lax.dynamic_index_in_dim(flattened, other_index, 1, keepdims=False)
    offset = jnp.stack([shift_x - 1, shift_y - 1, shift_z - 1]).astype(jnp.float32) * (
        CB * lattice_edge
    )
    left = lattice + own_tile
    right = lattice + other_tile + offset[:, None]
    delta = left[:, :, None] - right[:, None, :]
    square = jnp.sum(delta * delta, axis=0)
    serial = jnp.arange(TILE, dtype=jnp.int32)
    same_atom = (neighbour_code == 13) & (serial[:, None] == serial[None, :])
    distance = jnp.sqrt(jnp.where(same_atom, 100.0, square))
    return (delta, distance, own_index, other_index)


def density_term(window, lattice, tile_index, neighbour_code):
    delta, distance, own_index, other_index = pair_geometry(
        window, tile_index, neighbour_code, lattice
    )
    dens_gap = distance - density_cut
    return jnp.sum(jnp.where(distance < density_cut, dens_gap * dens_gap, 0.0), axis=1)[None]


def force_term(window, embed_window, lattice, tile_index, neighbour_code):
    delta, distance, own_index, other_index = pair_geometry(
        window, tile_index, neighbour_code, lattice
    )
    flat_embed = embed_window.reshape((BXT + 2) * (BYT + 2) * TZ, TILE)
    own_embed = lax.dynamic_index_in_dim(flat_embed, own_index, 0, keepdims=False)
    other_embed = lax.dynamic_index_in_dim(flat_embed, other_index, 0, keepdims=False)
    pair_gap = distance - pair_cut
    poly = coef_zero + coef_one * distance + coef_two * distance * distance
    pair_slope = jnp.where(
        distance < pair_cut,
        2.0 * pair_gap * poly + pair_gap * pair_gap * (coef_one + 2.0 * coef_two * distance),
        0.0,
    )
    dens_gap = distance - density_cut
    dens_slope = jnp.where(distance < density_cut, 2.0 * dens_gap, 0.0)
    scalar = (pair_slope + (own_embed[:, None] + other_embed[None, :]) * dens_slope) / distance
    return -jnp.sum(scalar[None] * delta, axis=2)


def sweep_pairs(term_fn, channels, pair_table, pair_total):
    initial = jnp.zeros((channels, TILES, TILE), jnp.float32)

    def block_add(block_index, running):
        start = block_index * 27
        chosen = lax.dynamic_slice_in_dim(pair_table, start, 27, 1)
        live = start + jnp.arange(27, dtype=jnp.int32) < pair_total
        terms = jax.vmap(term_fn)(chosen[0], chosen[1])
        terms = jnp.where(live[:, None, None], terms, 0.0)
        return running.at[:, chosen[0]].add(jnp.swapaxes(terms, 0, 1))

    blocks = (pair_total + 26) // 27
    total = lax.fori_loop(0, blocks, block_add, initial)
    return total.reshape(channels, BXT, BYT, TZ, TILE)


def relax_slab(padded):
    center = padded[1:-1]
    beside_all = padded[2:] + padded[:-2] + jnp.roll(center, 1, 1) + jnp.roll(center, -1, 1)
    beside_all = beside_all + jnp.roll(center, 1, 2) + jnp.roll(center, -1, 2)
    return center + diffusion_rate * (beside_all - 6.0 * center)


def one_step(lattice, pair_table, pair_total, planes, owners, across, carry, noise_now):
    positions, speeds, heat_field = carry
    slab_depth = heat_field.shape[0]
    plane_total = slab_depth * owners
    arrived = lax.all_to_all(
        heat_field.reshape(slab_depth, owners), ("gx", "gy"), split_axis=1, concat_axis=0, tiled=True
    )
    column = arrived.reshape(-1)
    column_temp = jnp.take(column, planes).reshape(TZ, TILE)
    local_temp = jnp.broadcast_to(column_temp, (BXT, BYT, TZ, TILE))
    window = padded_2(positions, (("gx", 1), ("gy", 2)), 1)
    density = sweep_pairs(partial(density_term, window, lattice), 1, pair_table, pair_total)
    embed_slope = -embed_scale / (2.0 * jnp.sqrt(density))
    embed_window = padded_2(embed_slope, (("gx", 1), ("gy", 2)), 1)
    force = sweep_pairs(partial(force_term, window, embed_window, lattice), 3, pair_table, pair_total)
    kicker = jnp.sqrt(2.0 * friction * atom_mass * local_temp / time_step)[None] * noise_now
    speeds = speeds + time_step / atom_mass * (force - friction * atom_mass * speeds + kicker)
    positions = positions + time_step * speeds
    power = friction * atom_mass * time_step * jnp.sum(speeds * speeds, axis=0)
    tile_power = jnp.sum(power, axis=(0, 1)).reshape(-1)
    energy = jnp.zeros((plane_total,), jnp.float32).at[planes].add(tile_power)
    arrived = lax.all_to_all(
        energy.reshape(plane_total, 1), ("gx", "gy"), split_axis=0, concat_axis=1, tiled=True
    )
    heat_field = heat_field + arrived.reshape(slab_depth, *across) / heat_capacity

    def relax(sub_index, heat):
        return relax_slab(padded_2(heat, ((("gx", "gy"), 0),), 1))

    heat_field = lax.fori_loop(0, SUB, relax, heat_field)
    return (positions, speeds, heat_field)


def whole_sweep(displacement, velocity, noise, electron_temp, pair_list, pair_count):
    across = (lax.axis_size("gx"), lax.axis_size("gy"))
    owners = across[0] * across[1]
    planes = plane_table(electron_temp.shape[0] * owners).reshape(-1)
    step = partial(
        one_step, lattice_sites(), pair_list[0, 0], pair_count[0, 0], planes, owners, across
    )
    return lax.fori_loop(
        0,
        STEPS,
        lambda n, carry: step(carry, lax.dynamic_index_in_dim(noise, n, 0, keepdims=False)),
        (displacement, velocity, electron_temp),
    )


NEAR_SHELLS = (3, 4, 8)
FAR_SHELLS = (11, 12)
NEAR_LIMIT = 0.2900
FAR_LIMIT = 0.8170
HALF = 0.5 * lattice_edge
FAR_AWAY = 1.0e6
ROWS = 20
BASE = 2
SIZE = TZ * ROWS
EDGES = (2, 3)


def site_offsets(shells):
    span = range(-3, 4)
    found = []
    for x in span:
        for y in span:
            for z in span:
                if x % 2 == y % 2 == z % 2 and x * x + y * y + z * z in shells:
                    found.append((x, y, z))
    return found


def grouped(offsets):
    table = {}
    for x, y, z in offsets:
        table.setdefault((y, z), []).append(x)
    return sorted(table.items())


NEAR = site_offsets(NEAR_SHELLS)
FAR = site_offsets(FAR_SHELLS)
MASK_SLOT = {offset: slot for slot, offset in enumerate(NEAR + FAR)}
MASKS = len(MASK_SLOT)


def by_x(groups):
    table = {}
    for n, ((dy, dz), dxs) in enumerate(groups):
        for dx in dxs:
            table.setdefault(dx, []).append((n, dy, dz))
    return sorted(table.items())


def sign(value):
    return (value > 0) - (value < 0)


def lanes_of(shape=(8, 128)):
    return lax.broadcasted_iota(jnp.int32, shape, len(shape) - 1)


def rows_of(shape=(8, 128)):
    return lax.broadcasted_iota(jnp.int32, shape, len(shape) - 2)


def turn(value, amount):
    amount = (-amount) % 128
    return value if amount == 0 else pltpu.roll(value, amount, value.ndim - 1)


def pick_lanes(value, index):
    return jnp.take_along_axis(value, index, axis=1, mode="promise_in_bounds")


class Chunk:
    def __init__(self, owners, cells, first=False):
        self.cells = cells
        self.narrow = owners <= 32
        halo = 9 if cells == 2 else 14
        if self.narrow:
            self.tail = 9 if cells == 2 else 13
            self.tail_lane = 96
            self.reach = (self.tail, 64)
            self.rows = self.tail + 1
        else:
            self.tail = halo
            self.tail_lane = 0
            self.reach = (halo + 1, 64)
            self.rows = halo + 2
        if first:
            self.live = [(self.reach[0], 0), (self.rows, 0), (self.rows, 64)]
            self.rows += 1

    def x_home(self, plane, row):
        if plane < 8:
            return self.cells * (plane // 2) + row, plane % 2
        return 4 * self.cells + row // 2, row % 2


def repeat_tail(value, chunk):
    if not chunk.narrow:
        return value
    return pick_lanes(value, 96 + lanes_of(value.shape) % 32)


def from_tiles(read, out):
    lane = lanes_of((TZ, 128))
    own = (lane >= 32) & (lane < 96)
    for c in range(3):
        for ix in range(BXT):
            first, second = [read(c, ix, iy) for iy in range(BYT)]
            for cx in range(CB):
                both = jnp.where(lane < 64, turn(first, 32 * cx - 32), turn(second, 32 * cx - 64))
                start = c * TZ * 8 + CB * ix + cx
                out[pl.ds(start, TZ, stride=8), :] = jnp.where(own, both, 0.0)


def to_tiles(source, out):
    lane = lanes_of((TZ, 128))
    for c in range(3):
        for ix in range(BXT):
            rows = [source[pl.ds(c * TZ * 8 + CB * ix + cx, TZ, stride=8), :] for cx in range(CB)]
            for iy in range(BYT):
                value = None
                for cx in range(CB):
                    piece = turn(rows[cx], 32 + 32 * iy - 32 * cx)
                    value = piece if value is None else jnp.where(lane >= 32 * cx, piece, value)
                out[c, ix, :, iy, :] = value


def stage_halo(own, stage, chunk, tail_row, extras):
    w = chunk.cells
    lane, row = lanes_of(), rows_of()
    kinds = {}
    depth = stage.shape[0] // 4
    low = lane < 64
    third = [pick for pick in range(5)] if w == 3 else []
    for kind, (axis, side) in enumerate((("x", -1), ("x", 1), ("y", -1), ("y", 1))):
        at = kind * depth
        kinds[(axis, side)] = at
        if axis == "x":
            first = 8 - w if side == 1 else 0
            for pair in range(4):
                both = jnp.where(low, turn(own(2 * pair), 32), turn(own(2 * pair + 1), -32))
                stage[at + w * pair : at + w * pair + w, :] = both[first : first + w]
            last = own(8)
            a, b = turn(last, 32), turn(last, -32)
            low1 = lanes_of((1, 128)) < 64
            stage[at + 4 * w : at + 4 * w + 1, :] = jnp.where(
                low1, a[first : first + 1], b[first + 1 : first + 2]
            )
            if w == 3:
                stage[at + 13 : at + 14, :] = a[first + 2 : first + 3]
        else:
            start = 80 if side == 1 else 32
            packed = None
            for plane in range(8):
                piece = turn(own(plane), start - 16 * plane)
                packed = piece if packed is None else jnp.where(lane >= 16 * plane, piece, packed)
            stage[at : at + 8, :] = packed
            flat = pick_lanes(own(8), start + lane % 16)
            flat = jnp.where(lane // 16 == row, flat, 0.0)
            stage[at + 8 : at + 9, :] = jnp.sum(flat, axis=0, keepdims=True)
            start = 72 if side == 1 else 48
            for pair in third:
                flat = pick_lanes(own(2 * pair), start + lane % 8)
                if pair < 4:
                    flat = jnp.where(low, flat, pick_lanes(own(2 * pair + 1), start + lane % 8))
                flat = jnp.where(lane % 64 // 8 == row, flat, 0.0)
                stage[at + 9 + pair : at + 10 + pair, :] = jnp.sum(flat, axis=0, keepdims=True)
        for (where, lane_from, lane_to), value in tail_row + extras.get((axis, side), []):
            lane1 = lanes_of((1, 128))
            old = stage[at + where : at + where + 1, :]
            here = (lane1 >= lane_from) & (lane1 < lane_to)
            stage[at + where : at + where + 1, :] = jnp.where(here, value, old)
    return kinds


def send_chunks(stage, kinds, send_ref, chunk, ids, owners):
    tails = sorted({chunk.tail, chunk.reach[0]})
    at = kinds[("x", 1)]
    rows = {where: stage[at + where : at + where + 1, :] for where in tails}

    def fill(index, carry):
        for where in tails:
            send_ref[index, :, 128 * where : 128 * where + 128] = rows[where]
        return carry

    lax.fori_loop(0, owners, fill, 0, unroll=8)
    for (sx, sy), ident in ids.items():
        if (sx, sy) == (0, 0):
            continue
        at = kinds[("y", sy)] if sy else kinds[("x", sx)]
        for k in range(chunk.rows):
            send_ref[ident, :, 128 * k : 128 * k + 128] = stage[at + k : at + k + 1, :]


def receive_chunks(recv_ref, landed, tails_at, chunk, ids, owners):
    depth = (landed.shape[0] - 2 * PAD) // 9
    homes = {}
    for n, ((sx, sy), ident) in enumerate(ids.items()):
        if (sx, sy) == (0, 0):
            continue
        homes[(sx, sy)] = PAD + n * depth
        for k in range(chunk.rows):
            landed[PAD + n * depth + k : PAD + n * depth + k + 1, :] = recv_ref[ident, :, 128 * k : 128 * k + 128]

    tails = sorted({chunk.tail, chunk.reach[0]})

    def take(index, carry):
        for n, where in enumerate(tails):
            tails_at[pl.ds(n * owners + index, 1), :] = recv_ref[index, :, 128 * where : 128 * where + 128]
        return carry

    lax.fori_loop(0, owners, take, 0, unroll=8)
    return homes


PAD = 8


def build_window(own, landed, homes, window, chunk, origin):
    w = chunk.cells
    lane, row = lanes_of(), rows_of()
    zero = jnp.zeros((8, 128), jnp.float32)
    middle = (lane >= 32) & (lane < 96)
    first_rows = row < 4

    def outer(start, size, sy):
        values = [landed[homes[(sx, sy)] + start : homes[(sx, sy)] + start + size, :] for sx in (1, -1)]
        if size == 1:
            values = [jnp.broadcast_to(value, (8, 128)) for value in values]
        return jnp.where(first_rows, values[0], values[1])

    def inner(start, size, sy):
        value = landed[homes[(0, sy)] + start : homes[(0, sy)] + start + size, :]
        return jnp.broadcast_to(value, (8, 128))

    sides = (-1, 1)
    packed = {(sy, out): (outer if out else inner)(0, 8, sy) for sy in sides for out in (0, 1)}
    for plane in range(9):
        at = plane * ROWS + BASE
        parts = [own(plane), zero]
        for sy in sides:
            target = 16 if sy == -1 else 96
            here = (lane >= target) & (lane < target + 16)
            beyond = 8 if sy == -1 else 112
            here_third = (lane >= beyond) & (lane < beyond + 8)
            for out in (0, 1):
                if plane < 8:
                    piece = turn(packed[(sy, out)], 16 * plane - target)
                else:
                    wide = (outer if out else inner)(8, 1, sy)
                    piece = pick_lanes(wide, 16 * row + lane % 16)
                parts[out] = jnp.where(here, piece, parts[out])
                if w == 3:
                    wide = (outer if out else inner)(9 + plane // 2, 1, sy)
                    piece = pick_lanes(wide, 64 * (plane % 2) + 8 * row + lane % 8)
                    parts[out] = jnp.where(here_third, piece, parts[out])
        centre, rim = parts
        if plane < 8:
            home, half = chunk.x_home(plane, 0)
            back = -32 if half == 0 else 32
            behind = landed[pl.ds(origin + homes[(1, 0)] + home, 8), :]
            ahead = landed[pl.ds(origin + homes[(-1, 0)] + home - (4 - w) - 4, 8), :]
            piece = turn(jnp.where(first_rows, behind, ahead), back)
            rim = jnp.where(middle & ((row < w) | (row >= 8 - w)), piece, rim)
        else:
            for k in range(w):
                home, half = chunk.x_home(plane, k)
                back = -32 if half == 0 else 32
                for sx, to in ((1, k), (-1, 8 - w + k)):
                    base = homes[(sx, 0)] + home
                    piece = turn(jnp.broadcast_to(landed[base : base + 1, :], (8, 128)), back)
                    rim = jnp.where(middle & (row == to), piece, rim)
        window[pl.ds(origin + at, 8), :] = pltpu.roll(rim, 4, 0)
        window[pl.ds(origin + at + 12, 8), :] = rim
        window[pl.ds(origin + at + 4, 8), :] = centre


def mix_planes(count, source, mixed, origin):
    even = lanes_of((16, 128)) % 2 == 0
    for plane in range(count * TZ):
        at = plane * ROWS + BASE
        here = source[pl.ds(origin + at, 16), :]
        after = turn(source[pl.ds(origin + at + 1, 16), :], 8)
        mixed[pl.ds(origin + at, 16), :] = jnp.where(even, after, here)


def sources(dy, dz, use_mixed):
    s = sign(dz)
    low = dy // 2
    if dy % 2 == 0 or use_mixed:
        out = [(None, 0, dz + 8 * low, 0)]
        if s:
            out.append((None, s, dz - 8 * s + 8 * low, 0))
        return out
    out = [(0, 0, dz + 8 * low, 0), (1, 0, dz + 8 * (low + 1), 1)]
    for parity, k in ((0, low), (1, low + 1)):
        if any(not 0 <= iz + dz < 8 for iz in range(parity, 8, 2)):
            out.append((parity, s, dz - 8 * s + 8 * k, parity))
    return out


def shift_planes(count, source, mixed, out, groups, constants, origin):
    half_layer = lanes_of((16, 128)) % 8
    parity = half_layer % 2
    slots = {key: n for n, (key, _) in enumerate(groups)}
    for c in range(count):
        for dz in sorted({key[1] for key in slots}, key=abs):
            dys = sorted(key[0] for key in slots if key[1] == dz)
            carried = (half_layer + dz >= 8) | (half_layer + dz < 0)
            ref = mixed if dz % 2 and mixed is not None else source
            wanted = {dy: sources(dy, dz, mixed is not None) for dy in dys}
            turned = {}
            for shift, down in sorted({part[2:] for parts in wanted.values() for part in parts}):
                for t in range(TZ):
                    at = (c * TZ + t) * ROWS + BASE + down
                    turned[(t, shift, down)] = turn(ref[pl.ds(origin + at, 16), :], shift)
            for dy in dys:
                for t in range(TZ):
                    value = None
                    for want, carry_z, shift, down in wanted[dy]:
                        piece = turned[((t + carry_z) % TZ, shift, down)]
                        if value is None:
                            value = piece
                            continue
                        here = None
                        if want is not None:
                            here = parity == want
                        if carry_z:
                            here = carried if here is None else here & carried
                        value = jnp.where(here, piece, value)
                    shift_by = constants(c, dy, dz)
                    if shift_by:
                        value = value + shift_by
                    at = slots[(dy, dz)] * count * SIZE + (c * TZ + t) * ROWS + BASE
                    out[pl.ds(origin + at, 16), :] = value


def coordinate_shift(c, dy, dz):
    return (0.0, HALF * dy, HALF * dz)[c]


def no_shift(c, dy, dz):
    return 0.0


def row_start(dx):
    return dx // 2 if dx % 2 == 0 else (dx - 1) // 2


def density_sweep(rows, keep, window, moved, masks_ref, slope, gaps, inverses, groups):
    own = [window[rows(c * SIZE), :] for c in range(3)]
    total = jnp.zeros(own[0].shape, jnp.float32)
    for dx, parts in by_x(groups):
        down = row_start(dx)
        own_x = own[0] - HALF * dx
        for n, dy, dz in parts:
            other = [moved[rows((3 * n + c) * SIZE + down), :] for c in range(3)]
            slot = MASK_SLOT[(dx, dy, dz)]
            ex = own_x - other[0]
            ey = own[1] - other[1]
            ez = own[2] - other[2]
            square = ex * ex + ey * ey + (ez * ez + masks_ref[rows(slot * SIZE), :])
            inverse = lax.rsqrt(square)
            gap = jnp.minimum(square * inverse - density_cut, 0.0)
            total = total + gap * gap
            if keep is not None:
                gaps[keep + 24 * slot : keep + 24 * slot + 8, :] = gap
                inverses[keep + 24 * slot : keep + 24 * slot + 8, :] = inverse
    slope[rows(0), :] = -embed_scale * lax.rsqrt(total)


def forces(t, window, moved, slope, slope_moved, gaps, inverses, groups, origin):
    at = t * ROWS + BASE + 4
    own = [window[pl.ds(origin + (c * SIZE + at), 8), :] for c in range(3)]
    own_slope = slope[pl.ds(origin + at, 8), :]
    first = 2.0 * (coef_zero + coef_one * pair_cut + coef_two * pair_cut * pair_cut)
    second = 3.0 * (coef_one + 2.0 * coef_two * pair_cut)
    third = 4.0 * coef_two
    zero = jnp.zeros((8, 128), jnp.float32)
    total = [zero, zero, zero]
    sum_all = zero
    for dx, parts in by_x(groups):
        down = row_start(dx)
        sum_here = zero
        for n, dy, dz in parts:
            slot = MASK_SLOT[(dx, dy, dz)]
            row = 3 * n * SIZE + at + down
            other_slope = slope_moved[pl.ds(origin + (n * SIZE + at + down), 8), :]
            gap = gaps[24 * slot + 8 * t : 24 * slot + 8 * t + 8, :]
            inverse = inverses[24 * slot + 8 * t : 24 * slot + 8 * t + 8, :]
            near = jnp.minimum(gap + (density_cut - pair_cut), 0.0)
            scalar = (own_slope + other_slope) * gap + near * (first + near * (second + third * near))
            scalar = scalar * inverse
            sum_here = sum_here + scalar
            for c in range(3):
                total[c] = total[c] + scalar * moved[pl.ds(origin + (row + c * SIZE), 8), :]
        sum_all = sum_all + sum_here
        if dx:
            total[0] = total[0] + (HALF * dx) * sum_here
    return [total[c] - own[c] * sum_all for c in range(3)]


def binomial(n, k):
    value = 1
    for j in range(k):
        value = value * (n - j) // (j + 1)
    return value


def diffuse_grid(grid, across):
    nx, ny = across
    d = diffusion_rate
    pairs = [
        [heat] + [pltpu.roll(heat, k, 1) + pltpu.roll(heat, 128 - k, 1) for k in range(1, SUB + 1)]
        for heat in grid
    ]

    def powers(x, k):
        total = None
        for j in range(k // 2 + 1):
            weight = binomial(k, j) * binomial(SUB, k) * d**k
            term = weight * pairs[x][k - 2 * j]
            total = term if total is None else total + term
        return total

    result = [powers(x, 0) for x in range(nx)]
    for k in range(1, SUB + 1):
        columns = []
        for x in range(nx):
            heat = result[x]
            beside = result[(x + 1) % nx] + result[(x - 1) % nx]
            beside = beside + pltpu.roll(heat, 1, 0) + pltpu.roll(heat, ny - 1, 0)
            columns.append(((1.0 - 6.0 * d) * heat + powers(x, k)) + d * beside)
        result = columns
    return result


LAYERS = 2 * CB * TZ


def temperatures_by_layer(column, plane_total):
    layer = 2 * CB * rows_of() + lanes_of() % (2 * CB)
    layer = jnp.minimum(layer, LAYERS - 1)
    return pick_lanes(jnp.broadcast_to(column, (8, 128)), layer * plane_total // LAYERS)


def energies_by_plane(power, plane_total):
    row, lane = rows_of(), lanes_of()
    stacked = jnp.zeros((8, 128), jnp.float32)
    for t in range(TZ):
        stacked = jnp.where(row == t, power[t], stacked)
    plane = lane % plane_total
    start = (plane * LAYERS + plane_total - 1) // plane_total
    total = jnp.zeros((8, 128), jnp.float32)
    for extra in range(max(1, -(-LAYERS // plane_total))):
        layer = start + extra
        inside = layer - 2 * CB * row
        here = (inside >= 0) & (inside < 2 * CB) & (layer < LAYERS)
        here = here & (layer * plane_total // LAYERS == plane)
        first = 32 + jnp.clip(inside, 0, 2 * CB - 1)
        taken = [pick_lanes(stacked, first + 8 * y) for y in range(BYT * CB)]
        while len(taken) > 1:
            taken = [a + b for a, b in zip(taken[::2], taken[1::2])]
        total = total + jnp.where(here, taken[0], 0.0)
    return jnp.sum(total, axis=0, keepdims=True)


def neighbour_ids(across):
    nx, ny = across
    bx, by = lax.axis_index("gx"), lax.axis_index("gy")
    at_x = {-1: jnp.where(bx == 0, nx - 1, bx - 1), 0: bx, 1: jnp.where(bx == nx - 1, 0, bx + 1)}
    at_y = {-1: jnp.where(by == 0, ny - 1, by - 1), 0: by, 1: jnp.where(by == ny - 1, 0, by + 1)}
    return {(sx, sy): at_x[sx] * ny + at_y[sy] for sx in (-1, 0, 1) for sy in (-1, 0, 1)}


def prepare(across, chunk, disp, heat, pairs, count, send, own_u, live, lists, disp_in, heat_in, pairs_in, count_in, stage, sems):
    nx, ny = across
    owners = nx * ny
    copies = [
        pltpu.make_async_copy(source, target, sems.at[n])
        for n, (source, target) in enumerate(
            ((disp, disp_in), (heat, heat_in), (pairs, pairs_in), (count, count_in))
        )
    ]
    for copy in copies:
        copy.start()
    lists[...] = jnp.full(lists.shape, -1, jnp.int32)
    for copy in copies:
        copy.wait()

    from_tiles(lambda c, ix, iy: disp_in[c, ix, :, iy, :], own_u)

    slots = pairs_in.shape[3]
    width = lists.shape[1]
    lists[0:2, 0:slots] = pairs_in[0, 0]
    tile = lists[0:1, :]
    code = lists[1:2, :]
    valid = (lanes_of((1, width)) < count_in[0, 0]) & (tile >= 0)
    column = jnp.where(tile >= 3, 1, 0) + jnp.where(tile >= 6, 1, 0) + jnp.where(tile >= 9, 1, 0)
    depth = jnp.where(valid, tile - 3 * column, -1)
    place = 32 * column + code
    left = jnp.where(rows_of((8, width)) == depth, 1.0, 0.0)
    right = jnp.where(rows_of((128, width)) == place, 1.0, 0.0)
    found = lax.dot_general(
        left, right, (((1,), (1,)), ((), ())), preferred_element_type=jnp.float32
    )
    live[...] = found

    lane_n = lanes_of((nx, 128))
    planes = jnp.zeros((nx, 128), jnp.float32)
    for y in range(ny):
        value = jnp.broadcast_to(heat_in[0, :, y : y + 1], (nx, 128))
        planes = jnp.where(lane_n % ny == y, value, planes)
    planes = jnp.where(lane_n % owners // ny == rows_of((nx, 128)), planes, 0.0)
    field = jnp.sum(planes, axis=0, keepdims=True)

    lane = lanes_of()
    halves = {
        ("x", -1): found,
        ("x", 1): turn(found, 64),
        ("y", -1): jnp.where(lane < 32, found, turn(found, 32)),
        ("y", 1): jnp.where(lane < 32, turn(found, 32), turn(found, 64)),
    }
    extras = {}
    for key, value in halves.items():
        extras[key] = [
            ((where, to, to + 64), value[t : t + 1] if to == 0 else turn(value, -64)[t : t + 1])
            for t, (where, to) in enumerate(chunk.live)
        ]
    kinds = stage_halo(
        lambda plane: own_u[8 * plane : 8 * plane + 8, :],
        stage,
        chunk,
        [((chunk.tail, chunk.tail_lane, 128), field)],
        extras,
    )
    send_chunks(stage, kinds, send, chunk, neighbour_ids(across), owners)


def make_masks(chunk, homes, landed, live, masks_ref, table, spread_ref, cases):
    lane1 = lanes_of((1, 128))
    table[...] = jnp.zeros((128, 128), jnp.float32)
    for x in range(4):
        for y in range(4):
            sx, sy = (-1, 0, 0, 1)[x], (-1, 0, 0, 1)[y]
            ix, iy = (1, 0, 1, 0)[x], (1, 0, 1, 0)[y]
            row = jnp.zeros((1, 128), jnp.float32)
            for t in range(TZ):
                if (sx, sy) == (0, 0):
                    value, start = live[t : t + 1, :], 32 * (2 * ix + iy)
                else:
                    where, start = chunk.live[t]
                    value = landed[homes[(sx, sy)] + where : homes[(sx, sy)] + where + 1, :]
                    start = start + 32 * (ix if sy else iy)
                here = (lane1 >= 32 * t) & (lane1 < 32 * t + 32)
                row = jnp.where(here, turn(value, start - 32 * t), row)
            table[4 * x + y : 4 * x + y + 1, :] = row
    by_code = jnp.transpose(table[...])
    big = (128, 128)
    for x in range(4):
        pick = jnp.where(rows_of(big) == 4 * x + lanes_of(big) // 32, 1.0, 0.0)
        alive = jnp.dot(by_code, pick, preferred_element_type=jnp.float32)
        spread_ref[128 * x : 128 * x + 128, :] = FAR_AWAY * (1.0 - alive)

    lane = lanes_of()
    half_layer = lane % 8
    parity = lane % 2
    cell_y = lane // 8 % 4
    low_rows = rows_of() < 4

    def crossing(position, step):
        return (position + step < 0) | (position + step >= 8)

    groups = grouped(NEAR + FAR)

    def at_t(t, carry):
        for code in range(27):
            for block in range(2):
                first, second = [
                    spread_ref[pl.ds(128 * x + 32 * t + code, 1), :] for x in (2 * block, 2 * block + 1)
                ]
                cases[16 * code + 8 * block : 16 * code + 8 * block + 8, :] = jnp.where(
                    low_rows, jnp.broadcast_to(first, (8, 128)), jnp.broadcast_to(second, (8, 128))
                )

        def case(ex, ey, ez, block):
            code = 9 * (ex + 1) + 3 * (ey + 1) + ez + 1
            return cases[16 * code + 8 * block : 16 * code + 8 * block + 8, :]

        for dz in sorted({key[1] for key, _ in groups}):
            cross_z = crossing(half_layer, dz)
            in_z = {}

            def level_z(ex, ey, block):
                if (ex, ey, block) not in in_z:
                    value = case(ex, ey, 0, block)
                    if dz:
                        value = jnp.where(cross_z, case(ex, ey, sign(dz), block), value)
                    in_z[(ex, ey, block)] = value
                return in_z[(ex, ey, block)]

            for (dy, other_z), dxs in groups:
                if other_z != dz:
                    continue
                cross_y = crossing(2 * cell_y + parity, dy)
                in_y = {}

                def level_y(ex, block):
                    if (ex, block) not in in_y:
                        value = level_z(ex, 0, block)
                        if dy:
                            value = jnp.where(cross_y, level_z(ex, sign(dy), block), value)
                        in_y[(ex, block)] = value
                    return in_y[(ex, block)]

                for dx in dxs:
                    cross_x = crossing(2 * (rows_of() % 4) + parity, dx)
                    for block in range(2):
                        value = level_y(0, block)
                        if dx:
                            value = jnp.where(cross_x, level_y(sign(dx), block), value)
                        at = MASK_SLOT[(dx, dy, dz)] * SIZE + BASE + 8 * block
                        masks_ref[pl.ds(at + t * ROWS, 8), :] = value
        return carry

    lax.fori_loop(0, TZ, at_t, 0)


def step_kernel(step, across, arriving, leaving, groups, limit, *refs):
    nx, ny = across
    owners = nx * ny
    refs = list(refs)
    last = leaving is None

    def take(count):
        taken = refs[:count]
        del refs[:count]
        return taken

    recv, in_u, in_v, noise = take(4)
    if step == 0:
        (live,) = take(1)
    else:
        masks_ref, in_grid, in_bad = take(3)
    send, out_grid, out_bad, out_u, out_v = take(5)
    if step == 0:
        (masks_ref,) = take(1)
    window, moved, slope, slope_moved, gaps, inverses, landed, tails_at, noise_in, noise_own = take(10)
    sems, u_own, v_own, stage, mixed = take(5)
    extra = refs
    if not last:
        u_own, v_own = out_u, out_v
    noise_copy = pltpu.make_async_copy(noise.at[step], noise_in, sems.at[0])
    noise_copy.start()
    if step == 0:
        v_in, table, spread_ref, cases = extra
        v_copy = pltpu.make_async_copy(in_v, v_in, sems.at[1])
        v_copy.start()
    ids = neighbour_ids(across)
    lane = lanes_of()

    homes = receive_chunks(recv, landed, tails_at, arriving, ids, owners)
    if step == 0:
        make_masks(arriving, homes, landed, live, masks_ref, table, spread_ref, cases)

    tail = repeat_tail(tails_at[0:owners, :], arriving)
    if step == 0:
        table[...] = jnp.zeros((128, 128), jnp.float32)
        table[0:owners, :] = tail
        turned = jnp.transpose(table[...])[:owners]
        reach = 128
        while reach > owners:
            reach //= 2
            turned = turned + pltpu.roll(turned, reach, 1)
        grid = [turned[ny * x : ny * x + ny] for x in range(nx)]
        out_bad[...] = jnp.zeros((8, 128), jnp.float32)
    else:
        grid = [
            in_grid[ny * x : ny * x + ny, :] + tail[ny * x : ny * x + ny] * (1.0 / heat_capacity)
            for x in range(nx)
        ]
        grid = diffuse_grid(grid, across)
        where, start = arriving.reach
        from_row = owners * (where != arriving.tail)
        furthest = tails_at[from_row : from_row + owners, :]
        lane_n = lanes_of((owners, 128))
        furthest = jnp.where((lane_n >= start) & (lane_n < start + 32), furthest, 0.0)
        reached = jnp.max(furthest, axis=0, keepdims=True)
        reached = jnp.max(reached, axis=1, keepdims=True)
        over = jnp.broadcast_to(jnp.where(reached > limit, 1.0, 0.0), (8, 128))
        out_bad[...] = jnp.maximum(in_bad[...], over)
    for x in range(nx):
        out_grid[ny * x : ny * x + ny, :] = grid[x]
    local = temperatures_by_layer(out_grid[pl.ds(ids[(0, 0)], 1), :], owners)
    kick = jnp.sqrt(local * (2.0 * friction * atom_mass / time_step))

    def own_u(plane):
        return in_u[8 * plane : 8 * plane + 8, :]

    origin = jnp.minimum(lax.axis_index("gx"), 0)
    build_window(own_u, landed, homes, window, arriving, origin)
    mix_planes(3, window, mixed, origin)
    known = (window, moved, masks_ref, slope, gaps, inverses, groups)
    shift_planes(3, window, mixed, moved, groups, coordinate_shift, origin)
    for t in range(TZ):
        start = t * ROWS + BASE + 4
        density_sweep(lambda base: pl.ds(origin + (base + start), 8), 8 * t, *known)
    for edge in EDGES:
        start = BASE + edge
        density_sweep(
            lambda base: pl.ds(origin + (base + start), 2 * TZ, stride=ROWS // 2), None, *known
        )
    shift_planes(1, slope, None, slope_moved, groups, no_shift, origin)

    noise_copy.wait()
    from_tiles(lambda c, ix, iy: noise_in[c, ix, :, iy, :], noise_own)
    speeds_in = in_v
    if step == 0:
        v_copy.wait()
        from_tiles(lambda c, ix, iy: v_in[c, ix, :, iy, :], v_own)
        speeds_in = v_own

    active = (lane >= 32) & (lane < 96)
    power = []
    furthest = jnp.zeros((8, 128), jnp.float32)
    for t in range(TZ):
        force = forces(t, window, moved, slope, slope_moved, gaps, inverses, groups, origin)
        layer = jnp.zeros((8, 128), jnp.float32)
        for c in range(3):
            at = 8 * (c * TZ + t)
            speed = speeds_in[at : at + 8, :]
            push = force[c] - friction * atom_mass * speed + kick[t : t + 1] * noise_own[at : at + 8, :]
            speed = speed + time_step / atom_mass * push
            speed = jnp.where(active, speed, 0.0)
            place = own_u(c * TZ + t) + time_step * speed
            v_own[at : at + 8, :] = speed
            u_own[at : at + 8, :] = place
            layer = layer + speed * speed
            furthest = jnp.maximum(furthest, jnp.abs(place))
        power.append(jnp.sum(layer, axis=0, keepdims=True))
    energy = energies_by_plane(power, owners) * (friction * atom_mass * time_step)
    if last:
        send[...] = jnp.broadcast_to(energy, (owners, 128))
        to_tiles(u_own, out_u)
        to_tiles(v_own, out_v)
        return
    furthest = jnp.max(furthest, axis=0, keepdims=True)
    furthest = jnp.broadcast_to(jnp.max(furthest, axis=1, keepdims=True), (1, 128))
    where, start = leaving.reach
    tail_row = [
        ((leaving.tail, leaving.tail_lane, 128), energy),
        ((where, start, start + 32), furthest),
    ]
    kinds = stage_halo(
        lambda plane: u_own[8 * plane : 8 * plane + 8, :], stage, leaving, tail_row, {}
    )
    send_chunks(stage, kinds, send, leaving, ids, owners)


def finish(across, recv, in_grid, heat):
    nx, ny = across
    grid = [
        in_grid[ny * x : ny * x + ny, :] + recv[ny * x : ny * x + ny, :] * (1.0 / heat_capacity)
        for x in range(nx)
    ]
    grid = diffuse_grid(grid, across)
    me = lax.axis_index("gx") * ny + lax.axis_index("gy")
    flat = rows_of((ny, 128)) == lanes_of((ny, 128))
    for x in range(nx):
        mine = jnp.where(lanes_of((ny, 128)) == me, grid[x], 0.0)
        mine = jnp.broadcast_to(jnp.sum(mine, axis=1, keepdims=True), (ny, 128))
        row = jnp.sum(jnp.where(flat, mine, 0.0), axis=0, keepdims=True)
        heat[0, x : x + 1, :] = row[:, :ny]


def exchange(value):
    return lax.all_to_all(value, ("gx", "gy"), split_axis=0, concat_axis=0, tiled=True)


VMEM_BYTES = 28 * 1024 * 1024


def call(kernel, outs, scratch, operands, in_hbm=(), name=None):
    specs = [
        pl.BlockSpec(memory_space=pltpu.HBM if n in in_hbm else pltpu.VMEM)
        for n in range(len(operands))
    ]
    return pl.pallas_call(
        kernel,
        out_shape=[jax.ShapeDtypeStruct(shape, jnp.float32) for shape in outs],
        in_specs=specs,
        out_specs=[pl.BlockSpec(memory_space=pltpu.VMEM)] * len(outs),
        scratch_shapes=scratch,
        compiler_params=pltpu.CompilerParams(vmem_limit_bytes=VMEM_BYTES),
        name=name,
    )(*operands)


def stencil_steps(displacement, velocity, noise, electron_temp, pair_list, pair_count):
    across = (lax.axis_size("gx"), lax.axis_size("gy"))
    owners = across[0] * across[1]

    def vmem(*shape):
        return pltpu.VMEM(shape, jnp.float32)

    tiles = (3, BXT, TZ, BYT, TILE)
    placed_u = jnp.swapaxes(displacement, 2, 3)
    placed_v = jnp.swapaxes(velocity, 2, 3)
    placed_noise = jnp.swapaxes(noise, 3, 4)
    slots = pair_list.shape[-1]
    first, two, three = Chunk(owners, 2, True), Chunk(owners, 2), Chunk(owners, 3)
    send, own_u, live = call(
        partial(prepare, across, first),
        [(owners, 1, 128 * first.rows), (72, 128), (8, 128)],
        [
            pltpu.VMEM((8, (slots + 127) // 128 * 128), jnp.int32),
            vmem(*tiles),
            vmem(*electron_temp.shape),
            pltpu.VMEM(pair_list.shape, jnp.int32),
            pltpu.SMEM(pair_count.shape, jnp.int32),
            vmem(4 * 16, 128),
            pltpu.SemaphoreType.DMA((4,)),
        ],
        (placed_u, electron_temp, pair_list, pair_count),
        in_hbm=(0, 1, 2, 3),
        name="prepare",
    )
    near, far = grouped(NEAR), grouped(NEAR + FAR)
    plan = [
        (first, two, near, 1.0),
        (two, three, near, NEAR_LIMIT),
        (three, three, far, FAR_LIMIT),
        (three, None, far, FAR_LIMIT),
    ]
    own_v = placed_v
    masks = grid = bad = None
    for step, (arriving, leaving, groups, limit) in enumerate(plan):
        recv = exchange(send)
        last = leaving is None
        pairs = sum(len(dxs) for _, dxs in groups)
        outs = [
            (owners, 128) if last else (owners, 1, 128 * leaving.rows),
            (owners, 128),
            (8, 128),
            tiles if last else (72, 128),
            tiles if last else (72, 128),
        ]
        scratch = [
            vmem(3 * SIZE + PAD, 128),
            vmem(len(groups) * 3 * SIZE, 128),
            vmem(SIZE, 128),
            vmem(len(groups) * SIZE, 128),
            vmem(24 * pairs, 128),
            vmem(24 * pairs, 128),
            vmem(9 * 16 + 2 * PAD, 128),
            vmem(2 * owners, 128),
            vmem(*tiles),
            vmem(72, 128),
            pltpu.SemaphoreType.DMA((2,)),
            vmem(72, 128),
            vmem(72, 128),
            vmem(4 * 16, 128),
            vmem(3 * SIZE, 128),
        ]
        if step == 0:
            outs.append((MASKS * SIZE, 128))
            scratch += [vmem(*tiles), vmem(128, 128), vmem(512, 128), vmem(27 * 16, 128)]
            operands = (recv, own_u, own_v, placed_noise, live)
        else:
            operands = (recv, own_u, own_v, placed_noise, masks, grid, bad)
        got = call(
            partial(step_kernel, step, across, arriving, leaving, groups, limit),
            outs,
            scratch,
            operands,
            in_hbm=(2, 3) if step == 0 else (3,),
            name=f"step{step}",
        )
        send, grid, bad, own_u, own_v = got[:5]
        if step == 0:
            masks = got[5]
    recv = exchange(send)
    (heat,) = call(partial(finish, across), [electron_temp.shape], [], (recv, grid), name="finish")
    return bad[0, 0], jnp.swapaxes(own_u, 2, 3), jnp.swapaxes(own_v, 2, 3), heat


def per_device(displacement, velocity, noise, electron_temp, pair_list, pair_count):
    given = (displacement, velocity, noise, electron_temp, pair_list, pair_count)
    bad, new_u, new_v, heat = stencil_steps(*given)
    return lax.cond(bad > 0.5, lambda: whole_sweep(*given), lambda: (new_u, new_v, heat))


def solution(mesh):
    placed = (
        P(None, "gx", "gy", None, None),
        P(None, "gx", "gy", None, None),
        P(None, None, "gx", "gy", None, None),
        P(("gx", "gy"), None, None),
        P("gx", "gy", None, None),
        P("gx", "gy"),
    )
    return jax.shard_map(
        per_device,
        mesh=mesh,
        in_specs=placed,
        out_specs=(
            P(None, "gx", "gy", None, None),
            P(None, "gx", "gy", None, None),
            P(("gx", "gy"), None, None),
        ),
        check_vma=False,
    )
```

```python
from functools import partial

import jax
import jax.numpy as jnp
from jax import lax
from jax.experimental import pallas as pl
from jax.experimental.pallas import tpu as pltpu
from jax.sharding import PartitionSpec as P

CB = 4
TILE = 128
BXT = 2
BYT = 2
TZ = 3
TILES = 12
STEPS = 4
SUB = 6


lattice_edge = 3.1652
density_cut = 4.400224
embed_scale = 1.896373
pair_cut = 3.25
coef_zero = 47.1346499
coef_one = -33.7665655
coef_two = 6.2541999
time_step = 0.005
atom_mass = 0.0190534
friction = 1.0
heat_capacity = 0.02
diffusion_rate = 0.12


def padded_2(block, sides, width):
    for axis, dim in sides:
        count = lax.axis_size(axis)
        forward = [(i, i + 1) for i in range(count - 1)]
        forward.append((count - 1, 0))
        backward = [(target, source) for source, target in forward]
        low = lax.ppermute(
            lax.slice_in_dim(block, block.shape[dim] - width, None, axis=dim), axis, forward
        )
        high = lax.ppermute(lax.slice_in_dim(block, 0, width, axis=dim), axis, backward)
        block = jnp.concatenate([low, block, high], axis=dim)
    return block


def lattice_sites():
    serial = jnp.arange(TILE, dtype=jnp.int32)
    cell_number = serial // 2
    half_step = (serial % 2).astype(jnp.float32) * 0.5
    corners = jnp.stack([cell_number // (CB * CB), cell_number // CB % CB, cell_number % CB])
    return lattice_edge * (corners.astype(jnp.float32) + half_step[None, :])


def plane_table(plane_total):
    serial = jnp.arange(TILE, dtype=jnp.int32)
    cell_number = serial // 2
    layer = 2 * (cell_number % CB) + serial % 2
    tiles = jnp.arange(TZ, dtype=jnp.int32)
    whole = tiles[:, None] * (2 * CB) + layer[None, :]
    return whole * plane_total // (2 * CB * TZ)


def pair_geometry(window, tile_index, neighbour_code, lattice):
    wide_y = BYT + 2
    depth_t = tile_index % TZ
    inner_y = tile_index // TZ % BYT
    inner_x = tile_index // (TZ * BYT)
    shift_x = neighbour_code // 9
    shift_y = neighbour_code // 3 % 3
    shift_z = neighbour_code % 3
    flattened = window.reshape(window.shape[0], (BXT + 2) * wide_y * TZ, TILE)
    own_index = ((inner_x + 1) * wide_y + inner_y + 1) * TZ + depth_t
    other_index = ((inner_x + shift_x) * wide_y + inner_y + shift_y) * TZ + (
        depth_t + shift_z - 1 + TZ
    ) % TZ
    own_tile = lax.dynamic_index_in_dim(flattened, own_index, 1, keepdims=False)
    other_tile = lax.dynamic_index_in_dim(flattened, other_index, 1, keepdims=False)
    offset = jnp.stack([shift_x - 1, shift_y - 1, shift_z - 1]).astype(jnp.float32) * (
        CB * lattice_edge
    )
    left = lattice + own_tile
    right = lattice + other_tile + offset[:, None]
    delta = left[:, :, None] - right[:, None, :]
    square = jnp.sum(delta * delta, axis=0)
    serial = jnp.arange(TILE, dtype=jnp.int32)
    same_atom = (neighbour_code == 13) & (serial[:, None] == serial[None, :])
    distance = jnp.sqrt(jnp.where(same_atom, 100.0, square))
    return (delta, distance, own_index, other_index)


def density_term(window, lattice, tile_index, neighbour_code):
    delta, distance, own_index, other_index = pair_geometry(
        window, tile_index, neighbour_code, lattice
    )
    dens_gap = distance - density_cut
    return jnp.sum(jnp.where(distance < density_cut, dens_gap * dens_gap, 0.0), axis=1)[None]


def force_term(window, embed_window, lattice, tile_index, neighbour_code):
    delta, distance, own_index, other_index = pair_geometry(
        window, tile_index, neighbour_code, lattice
    )
    flat_embed = embed_window.reshape((BXT + 2) * (BYT + 2) * TZ, TILE)
    own_embed = lax.dynamic_index_in_dim(flat_embed, own_index, 0, keepdims=False)
    other_embed = lax.dynamic_index_in_dim(flat_embed, other_index, 0, keepdims=False)
    pair_gap = distance - pair_cut
    poly = coef_zero + coef_one * distance + coef_two * distance * distance
    pair_slope = jnp.where(
        distance < pair_cut,
        2.0 * pair_gap * poly + pair_gap * pair_gap * (coef_one + 2.0 * coef_two * distance),
        0.0,
    )
    dens_gap = distance - density_cut
    dens_slope = jnp.where(distance < density_cut, 2.0 * dens_gap, 0.0)
    scalar = (pair_slope + (own_embed[:, None] + other_embed[None, :]) * dens_slope) / distance
    return -jnp.sum(scalar[None] * delta, axis=2)


def sweep_pairs(term_fn, channels, pair_table, pair_total):
    initial = jnp.zeros((channels, TILES, TILE), jnp.float32)

    def block_add(block_index, running):
        start = block_index * 27
        chosen = lax.dynamic_slice_in_dim(pair_table, start, 27, 1)
        live = start + jnp.arange(27, dtype=jnp.int32) < pair_total
        terms = jax.vmap(term_fn)(chosen[0], chosen[1])
        terms = jnp.where(live[:, None, None], terms, 0.0)
        return running.at[:, chosen[0]].add(jnp.swapaxes(terms, 0, 1))

    blocks = (pair_total + 26) // 27
    total = lax.fori_loop(0, blocks, block_add, initial)
    return total.reshape(channels, BXT, BYT, TZ, TILE)


def relax_slab(padded):
    center = padded[1:-1]
    beside_all = padded[2:] + padded[:-2] + jnp.roll(center, 1, 1) + jnp.roll(center, -1, 1)
    beside_all = beside_all + jnp.roll(center, 1, 2) + jnp.roll(center, -1, 2)
    return center + diffusion_rate * (beside_all - 6.0 * center)


def one_step(lattice, pair_table, pair_total, planes, owners, across, carry, noise_now):
    positions, speeds, heat_field = carry
    slab_depth = heat_field.shape[0]
    plane_total = slab_depth * owners
    arrived = lax.all_to_all(
        heat_field.reshape(slab_depth, owners), ("gx", "gy"), split_axis=1, concat_axis=0, tiled=True
    )
    column = arrived.reshape(-1)
    column_temp = jnp.take(column, planes).reshape(TZ, TILE)
    local_temp = jnp.broadcast_to(column_temp, (BXT, BYT, TZ, TILE))
    window = padded_2(positions, (("gx", 1), ("gy", 2)), 1)
    density = sweep_pairs(partial(density_term, window, lattice), 1, pair_table, pair_total)
    embed_slope = -embed_scale / (2.0 * jnp.sqrt(density))
    embed_window = padded_2(embed_slope, (("gx", 1), ("gy", 2)), 1)
    force = sweep_pairs(partial(force_term, window, embed_window, lattice), 3, pair_table, pair_total)
    kicker = jnp.sqrt(2.0 * friction * atom_mass * local_temp / time_step)[None] * noise_now
    speeds = speeds + time_step / atom_mass * (force - friction * atom_mass * speeds + kicker)
    positions = positions + time_step * speeds
    power = friction * atom_mass * time_step * jnp.sum(speeds * speeds, axis=0)
    tile_power = jnp.sum(power, axis=(0, 1)).reshape(-1)
    energy = jnp.zeros((plane_total,), jnp.float32).at[planes].add(tile_power)
    arrived = lax.all_to_all(
        energy.reshape(plane_total, 1), ("gx", "gy"), split_axis=0, concat_axis=1, tiled=True
    )
    heat_field = heat_field + arrived.reshape(slab_depth, *across) / heat_capacity

    def relax(sub_index, heat):
        return relax_slab(padded_2(heat, ((("gx", "gy"), 0),), 1))

    heat_field = lax.fori_loop(0, SUB, relax, heat_field)
    return (positions, speeds, heat_field)


def whole_sweep(displacement, velocity, noise, electron_temp, pair_list, pair_count):
    across = (lax.axis_size("gx"), lax.axis_size("gy"))
    owners = across[0] * across[1]
    planes = plane_table(electron_temp.shape[0] * owners).reshape(-1)
    step = partial(
        one_step, lattice_sites(), pair_list[0, 0], pair_count[0, 0], planes, owners, across
    )
    return lax.fori_loop(
        0,
        STEPS,
        lambda n, carry: step(carry, lax.dynamic_index_in_dim(noise, n, 0, keepdims=False)),
        (displacement, velocity, electron_temp),
    )


NEAR_SHELLS = (3, 4, 8)
FAR_SHELLS = (11, 12)
NEAR_LIMIT = 0.2900
FAR_LIMIT = 0.8170
HALF = 0.5 * lattice_edge
FAR_AWAY = 1.0e6
ROWS = 20
BASE = 2
SIZE = TZ * ROWS
EDGES = (2, 3)


def site_offsets(shells):
    span = range(-3, 4)
    found = []
    for x in span:
        for y in span:
            for z in span:
                if x % 2 == y % 2 == z % 2 and x * x + y * y + z * z in shells:
                    found.append((x, y, z))
    return found


def grouped(offsets):
    table = {}
    for x, y, z in offsets:
        table.setdefault((y, z), []).append(x)
    return sorted(table.items())


NEAR = site_offsets(NEAR_SHELLS)
FAR = site_offsets(FAR_SHELLS)
MASK_SLOT = {offset: slot for slot, offset in enumerate(NEAR + FAR)}
MASKS = len(MASK_SLOT)


def by_x(groups):
    table = {}
    for n, ((dy, dz), dxs) in enumerate(groups):
        for dx in dxs:
            table.setdefault(dx, []).append((n, dy, dz))
    return sorted(table.items())


def sign(value):
    return (value > 0) - (value < 0)


def lanes_of(shape=(8, 128)):
    return lax.broadcasted_iota(jnp.int32, shape, len(shape) - 1)


def rows_of(shape=(8, 128)):
    return lax.broadcasted_iota(jnp.int32, shape, len(shape) - 2)


def turn(value, amount):
    amount = (-amount) % 128
    return value if amount == 0 else pltpu.roll(value, amount, value.ndim - 1)


def pick_lanes(value, index):
    return jnp.take_along_axis(value, index, axis=1, mode="promise_in_bounds")


class Chunk:
    def __init__(self, owners, cells, first=False):
        self.cells = cells
        self.narrow = owners <= 32
        halo = 9 if cells == 2 else 14
        if self.narrow:
            self.tail = 9 if cells == 2 else 13
            self.tail_lane = 96
            self.reach = (self.tail, 64)
            self.rows = self.tail + 1
        else:
            self.tail = halo
            self.tail_lane = 0
            self.reach = (halo + 1, 64)
            self.rows = halo + 2
        if first:
            self.live = [(self.reach[0], 0), (self.rows, 0), (self.rows, 64)]
            self.rows += 1

    def x_home(self, plane, row):
        if plane < 8:
            return self.cells * (plane // 2) + row, plane % 2
        return 4 * self.cells + row // 2, row % 2


def repeat_tail(value, chunk):
    if not chunk.narrow:
        return value
    return pick_lanes(value, 96 + lanes_of(value.shape) % 32)


def from_tiles(read, out):
    lane = lanes_of((TZ, 128))
    own = (lane >= 32) & (lane < 96)
    for c in range(3):
        for ix in range(BXT):
            first, second = [read(c, ix, iy) for iy in range(BYT)]
            for cx in range(CB):
                both = jnp.where(lane < 64, turn(first, 32 * cx - 32), turn(second, 32 * cx - 64))
                start = c * TZ * 8 + CB * ix + cx
                out[pl.ds(start, TZ, stride=8), :] = jnp.where(own, both, 0.0)


def to_tiles(source, out):
    lane = lanes_of((TZ, 128))
    for c in range(3):
        for ix in range(BXT):
            rows = [source[pl.ds(c * TZ * 8 + CB * ix + cx, TZ, stride=8), :] for cx in range(CB)]
            for iy in range(BYT):
                value = None
                for cx in range(CB):
                    piece = turn(rows[cx], 32 + 32 * iy - 32 * cx)
                    value = piece if value is None else jnp.where(lane >= 32 * cx, piece, value)
                out[c, ix, :, iy, :] = value


def each(count, body):
    if count <= 32:
        for index in range(count):
            body(index, 0)
    else:
        lax.fori_loop(0, count, body, 0, unroll=8)


def stage_halo(own, stage, chunk, tail_row, extras):
    w = chunk.cells
    lane, row = lanes_of(), rows_of()
    kinds = {}
    depth = stage.shape[0] // 4
    low = lane < 64
    third = [pick for pick in range(5)] if w == 3 else []
    for kind, (axis, side) in enumerate((("x", -1), ("x", 1), ("y", -1), ("y", 1))):
        at = kind * depth
        kinds[(axis, side)] = at
        if axis == "x":
            first = 8 - w if side == 1 else 0
            for pair in range(4):
                both = jnp.where(low, turn(own(2 * pair), 32), turn(own(2 * pair + 1), -32))
                stage[at + w * pair : at + w * pair + w, :] = both[first : first + w]
            last = own(8)
            a, b = turn(last, 32), turn(last, -32)
            low1 = lanes_of((1, 128)) < 64
            stage[at + 4 * w : at + 4 * w + 1, :] = jnp.where(
                low1, a[first : first + 1], b[first + 1 : first + 2]
            )
            if w == 3:
                stage[at + 13 : at + 14, :] = a[first + 2 : first + 3]
        else:
            start = 80 if side == 1 else 32
            packed = None
            for plane in range(8):
                piece = turn(own(plane), start - 16 * plane)
                packed = piece if packed is None else jnp.where(lane >= 16 * plane, piece, packed)
            stage[at : at + 8, :] = packed
            flat = pick_lanes(own(8), start + lane % 16)
            flat = jnp.where(lane // 16 == row, flat, 0.0)
            stage[at + 8 : at + 9, :] = jnp.sum(flat, axis=0, keepdims=True)
            start = 72 if side == 1 else 48
            for pair in third:
                flat = pick_lanes(own(2 * pair), start + lane % 8)
                if pair < 4:
                    flat = jnp.where(low, flat, pick_lanes(own(2 * pair + 1), start + lane % 8))
                flat = jnp.where(lane % 64 // 8 == row, flat, 0.0)
                stage[at + 9 + pair : at + 10 + pair, :] = jnp.sum(flat, axis=0, keepdims=True)
        for (where, lane_from, lane_to), value in tail_row + extras.get((axis, side), []):
            lane1 = lanes_of((1, 128))
            old = stage[at + where : at + where + 1, :]
            here = (lane1 >= lane_from) & (lane1 < lane_to)
            stage[at + where : at + where + 1, :] = jnp.where(here, value, old)
    return kinds


def send_chunks(stage, kinds, send_ref, chunk, ids, owners):
    tails = sorted({chunk.tail, chunk.reach[0]})
    at = kinds[("x", 1)]
    rows = {where: stage[at + where : at + where + 1, :] for where in tails}

    for (sx, sy), ident in ids.items():
        if (sx, sy) == (0, 0):
            continue
        at = kinds[("y", sy)] if sy else kinds[("x", sx)]
        for k in range(chunk.rows):
            if k not in tails:
                send_ref[ident, :, 128 * k : 128 * k + 128] = stage[at + k : at + k + 1, :]

    def fill(index, carry):
        for where in tails:
            send_ref[index, :, 128 * where : 128 * where + 128] = rows[where]
        return carry

    each(owners, fill)
    for (sx, sy), ident in ids.items():
        if (sx, sy) == (0, 0):
            continue
        at = kinds[("y", sy)] if sy else kinds[("x", sx)]
        for k in tails:
            send_ref[ident, :, 128 * k : 128 * k + 128] = stage[at + k : at + k + 1, :]


def receive_chunks(recv_ref, landed, tails_at, chunk, ids, owners):
    depth = (landed.shape[0] - 2 * PAD) // 9
    homes = {}
    for n, ((sx, sy), ident) in enumerate(ids.items()):
        if (sx, sy) == (0, 0):
            continue
        homes[(sx, sy)] = PAD + n * depth
        for k in range(chunk.rows):
            landed[PAD + n * depth + k : PAD + n * depth + k + 1, :] = recv_ref[ident, :, 128 * k : 128 * k + 128]

    tails = sorted({chunk.tail, chunk.reach[0]})

    def take(index, carry):
        for n, where in enumerate(tails):
            tails_at[pl.ds(n * owners + index, 1), :] = recv_ref[index, :, 128 * where : 128 * where + 128]
        return carry

    each(owners, take)
    return homes


PAD = 8


def build_window(own, landed, homes, window, chunk, origin):
    w = chunk.cells
    lane, row = lanes_of(), rows_of()
    zero = jnp.zeros((8, 128), jnp.float32)
    middle = (lane >= 32) & (lane < 96)
    first_rows = row < 4

    def outer(start, size, sy):
        values = [landed[homes[(sx, sy)] + start : homes[(sx, sy)] + start + size, :] for sx in (1, -1)]
        if size == 1:
            values = [jnp.broadcast_to(value, (8, 128)) for value in values]
        return jnp.where(first_rows, values[0], values[1])

    def inner(start, size, sy):
        value = landed[homes[(0, sy)] + start : homes[(0, sy)] + start + size, :]
        return jnp.broadcast_to(value, (8, 128))

    sides = (-1, 1)
    packed = {(sy, out): (outer if out else inner)(0, 8, sy) for sy in sides for out in (0, 1)}
    for plane in range(9):
        at = plane * ROWS + BASE
        parts = [own(plane), zero]
        for sy in sides:
            target = 16 if sy == -1 else 96
            here = (lane >= target) & (lane < target + 16)
            beyond = 8 if sy == -1 else 112
            here_third = (lane >= beyond) & (lane < beyond + 8)
            for out in (0, 1):
                if plane < 8:
                    piece = turn(packed[(sy, out)], 16 * plane - target)
                else:
                    wide = (outer if out else inner)(8, 1, sy)
                    piece = pick_lanes(wide, 16 * row + lane % 16)
                parts[out] = jnp.where(here, piece, parts[out])
                if w == 3:
                    wide = (outer if out else inner)(9 + plane // 2, 1, sy)
                    piece = pick_lanes(wide, 64 * (plane % 2) + 8 * row + lane % 8)
                    parts[out] = jnp.where(here_third, piece, parts[out])
        centre, rim = parts
        if plane < 8:
            home, half = chunk.x_home(plane, 0)
            back = -32 if half == 0 else 32
            behind = landed[pl.ds(origin + homes[(1, 0)] + home, 8), :]
            ahead = landed[pl.ds(origin + homes[(-1, 0)] + home - (4 - w) - 4, 8), :]
            piece = turn(jnp.where(first_rows, behind, ahead), back)
            rim = jnp.where(middle & ((row < w) | (row >= 8 - w)), piece, rim)
        else:
            for k in range(w):
                home, half = chunk.x_home(plane, k)
                back = -32 if half == 0 else 32
                for sx, to in ((1, k), (-1, 8 - w + k)):
                    base = homes[(sx, 0)] + home
                    piece = turn(jnp.broadcast_to(landed[base : base + 1, :], (8, 128)), back)
                    rim = jnp.where(middle & (row == to), piece, rim)
        window[pl.ds(origin + at, 8), :] = pltpu.roll(rim, 4, 0)
        window[pl.ds(origin + at + 12, 8), :] = rim
        window[pl.ds(origin + at + 4, 8), :] = centre


def mix_planes(count, source, mixed, origin):
    even = lanes_of((16, 128)) % 2 == 0
    for plane in range(count * TZ):
        at = plane * ROWS + BASE
        here = source[pl.ds(origin + at, 16), :]
        after = turn(source[pl.ds(origin + at + 1, 16), :], 8)
        mixed[pl.ds(origin + at, 16), :] = jnp.where(even, after, here)


def sources(dy, dz, use_mixed):
    s = sign(dz)
    low = dy // 2
    if dy % 2 == 0 or use_mixed:
        out = [(None, 0, dz + 8 * low, 0)]
        if s:
            out.append((None, s, dz - 8 * s + 8 * low, 0))
        return out
    out = [(0, 0, dz + 8 * low, 0), (1, 0, dz + 8 * (low + 1), 1)]
    for parity, k in ((0, low), (1, low + 1)):
        if any(not 0 <= iz + dz < 8 for iz in range(parity, 8, 2)):
            out.append((parity, s, dz - 8 * s + 8 * k, parity))
    return out


def shift_planes(count, source, mixed, out, groups, constants, origin):
    half_layer = lanes_of((16, 128)) % 8
    parity = half_layer % 2
    slots = {key: n for n, (key, _) in enumerate(groups)}
    for c in range(count):
        for dz in sorted({key[1] for key in slots}, key=lambda z: (z % 2, abs(z))):
            dys = sorted(key[0] for key in slots if key[1] == dz)
            carried = (half_layer + dz >= 8) | (half_layer + dz < 0)
            ref = mixed if dz % 2 and mixed is not None else source
            wanted = {dy: sources(dy, dz, mixed is not None) for dy in dys}
            turned = {}
            for shift, down in sorted({part[2:] for parts in wanted.values() for part in parts}):
                for t in range(TZ):
                    at = (c * TZ + t) * ROWS + BASE + down
                    turned[(t, shift, down)] = turn(ref[pl.ds(origin + at, 16), :], shift)
            for dy in dys:
                for t in range(TZ):
                    value = None
                    for want, carry_z, shift, down in wanted[dy]:
                        piece = turned[((t + carry_z) % TZ, shift, down)]
                        if value is None:
                            value = piece
                            continue
                        here = None
                        if want is not None:
                            here = parity == want
                        if carry_z:
                            here = carried if here is None else here & carried
                        value = jnp.where(here, piece, value)
                    shift_by = constants(c, dy, dz)
                    if shift_by:
                        value = value + shift_by
                    at = slots[(dy, dz)] * count * SIZE + (c * TZ + t) * ROWS + BASE
                    out[pl.ds(origin + at, 16), :] = value


def coordinate_shift(c, dy, dz):
    return (0.0, HALF * dy, HALF * dz)[c]


def no_shift(c, dy, dz):
    return 0.0


def row_start(dx):
    return dx // 2 if dx % 2 == 0 else (dx - 1) // 2


def density_sweep(rows, keep, window, moved, masks_ref, slope, gaps, inverses, groups):
    own = [window[rows(c * SIZE), :] for c in range(3)]
    total = jnp.zeros(own[0].shape, jnp.float32)
    for dx, parts in by_x(groups):
        down = row_start(dx)
        own_x = own[0] - HALF * dx
        for n, dy, dz in parts:
            other = [moved[rows((3 * n + c) * SIZE + down), :] for c in range(3)]
            slot = MASK_SLOT[(dx, dy, dz)]
            ex = own_x - other[0]
            ey = own[1] - other[1]
            ez = own[2] - other[2]
            square = ex * ex + ey * ey + (ez * ez + masks_ref[rows(slot * SIZE), :])
            inverse = lax.rsqrt(square)
            gap = jnp.minimum(square * inverse - density_cut, 0.0)
            total = total + gap * gap
            if keep is not None:
                gaps[keep + 24 * slot : keep + 24 * slot + 8, :] = gap
                inverses[keep + 24 * slot : keep + 24 * slot + 8, :] = inverse
    slope[rows(0), :] = -embed_scale * lax.rsqrt(total)


def forces(t, window, moved, slope, slope_moved, gaps, inverses, groups, origin):
    at = t * ROWS + BASE + 4
    own = [window[pl.ds(origin + (c * SIZE + at), 8), :] for c in range(3)]
    own_slope = slope[pl.ds(origin + at, 8), :]
    first = 2.0 * (coef_zero + coef_one * pair_cut + coef_two * pair_cut * pair_cut)
    second = 3.0 * (coef_one + 2.0 * coef_two * pair_cut)
    third = 4.0 * coef_two
    zero = jnp.zeros((8, 128), jnp.float32)
    total = [zero, zero, zero]
    sum_all = zero
    for dx, parts in by_x(groups):
        down = row_start(dx)
        sum_here = zero
        for n, dy, dz in parts:
            slot = MASK_SLOT[(dx, dy, dz)]
            row = 3 * n * SIZE + at + down
            other_slope = slope_moved[pl.ds(origin + (n * SIZE + at + down), 8), :]
            gap = gaps[24 * slot + 8 * t : 24 * slot + 8 * t + 8, :]
            inverse = inverses[24 * slot + 8 * t : 24 * slot + 8 * t + 8, :]
            near = jnp.minimum(gap + (density_cut - pair_cut), 0.0)
            scalar = (own_slope + other_slope) * gap + near * (first + near * (second + third * near))
            scalar = scalar * inverse
            sum_here = sum_here + scalar
            for c in range(3):
                total[c] = total[c] + scalar * moved[pl.ds(origin + (row + c * SIZE), 8), :]
        sum_all = sum_all + sum_here
        if dx:
            total[0] = total[0] + (HALF * dx) * sum_here
    return [total[c] - own[c] * sum_all for c in range(3)]


def binomial(n, k):
    value = 1
    for j in range(k):
        value = value * (n - j) // (j + 1)
    return value


def diffuse_grid(grid, across):
    nx, ny = across
    d = diffusion_rate
    pairs = [
        [heat] + [pltpu.roll(heat, k, 1) + pltpu.roll(heat, 128 - k, 1) for k in range(1, SUB + 1)]
        for heat in grid
    ]

    def powers(x, k):
        total = None
        for j in range(k // 2 + 1):
            weight = binomial(k, j) * binomial(SUB, k) * d**k
            term = weight * pairs[x][k - 2 * j]
            total = term if total is None else total + term
        return total

    result = [powers(x, 0) for x in range(nx)]
    for k in range(1, SUB + 1):
        columns = []
        for x in range(nx):
            heat = result[x]
            beside = result[(x + 1) % nx] + result[(x - 1) % nx]
            beside = beside + pltpu.roll(heat, 1, 0) + pltpu.roll(heat, ny - 1, 0)
            columns.append(((1.0 - 6.0 * d) * heat + powers(x, k)) + d * beside)
        result = columns
    return result


LAYERS = 2 * CB * TZ


def temperatures_by_layer(column, plane_total):
    layer = 2 * CB * rows_of() + lanes_of() % (2 * CB)
    layer = jnp.minimum(layer, LAYERS - 1)
    return pick_lanes(jnp.broadcast_to(column, (8, 128)), layer * plane_total // LAYERS)


def energies_by_plane(power, plane_total):
    row, lane = rows_of(), lanes_of()
    stacked = jnp.zeros((8, 128), jnp.float32)
    for t in range(TZ):
        stacked = jnp.where(row == t, power[t], stacked)
    plane = lane % plane_total
    start = (plane * LAYERS + plane_total - 1) // plane_total
    total = jnp.zeros((8, 128), jnp.float32)
    for extra in range(max(1, -(-LAYERS // plane_total))):
        layer = start + extra
        inside = layer - 2 * CB * row
        here = (inside >= 0) & (inside < 2 * CB) & (layer < LAYERS)
        here = here & (layer * plane_total // LAYERS == plane)
        first = 32 + jnp.clip(inside, 0, 2 * CB - 1)
        taken = [pick_lanes(stacked, first + 8 * y) for y in range(BYT * CB)]
        while len(taken) > 1:
            taken = [a + b for a, b in zip(taken[::2], taken[1::2])]
        total = total + jnp.where(here, taken[0], 0.0)
    return jnp.sum(total, axis=0, keepdims=True)


def neighbour_ids(across):
    nx, ny = across
    bx, by = lax.axis_index("gx"), lax.axis_index("gy")
    at_x = {-1: jnp.where(bx == 0, nx - 1, bx - 1), 0: bx, 1: jnp.where(bx == nx - 1, 0, bx + 1)}
    at_y = {-1: jnp.where(by == 0, ny - 1, by - 1), 0: by, 1: jnp.where(by == ny - 1, 0, by + 1)}
    return {(sx, sy): at_x[sx] * ny + at_y[sy] for sx in (-1, 0, 1) for sy in (-1, 0, 1)}


def prepare(across, chunk, disp, heat, pairs, count, vel, noise, send, own_u, live, kept_heat, kept_count, near_vel, near_noise, lists, disp_in, heat_in, pairs_in, count_in, stage, sems):
    nx, ny = across
    owners = nx * ny
    copies = [
        pltpu.make_async_copy(source, target, sems.at[n])
        for n, (source, target) in enumerate(
            ((disp, disp_in), (heat, heat_in), (pairs, pairs_in), (count, count_in))
        )
    ]
    later = [
        pltpu.make_async_copy(vel, near_vel, sems.at[4]),
        pltpu.make_async_copy(noise, near_noise, sems.at[5]),
    ]
    for copy in copies + later:
        copy.start()
    lists[...] = jnp.full(lists.shape, -1, jnp.int32)
    for copy in copies:
        copy.wait()

    from_tiles(lambda c, ix, iy: disp_in[c, ix, :, iy, :], own_u)
    kept_heat[...] = heat_in[...]
    kept_count[...] = jnp.full((8, 128), count_in[0, 0], jnp.int32)

    slots = pairs_in.shape[3]
    width = lists.shape[1]
    lists[0:2, 0:slots] = pairs_in[0, 0]
    tile = lists[0:1, :]
    code = lists[1:2, :]
    valid = (lanes_of((1, width)) < count_in[0, 0]) & (tile >= 0)
    column = jnp.where(tile >= 3, 1, 0) + jnp.where(tile >= 6, 1, 0) + jnp.where(tile >= 9, 1, 0)
    depth = jnp.where(valid, tile - 3 * column, -1)
    place = 32 * column + code
    left = jnp.where(rows_of((8, width)) == depth, 1.0, 0.0)
    right = jnp.where(rows_of((128, width)) == place, 1.0, 0.0)
    found = lax.dot_general(
        left, right, (((1,), (1,)), ((), ())), preferred_element_type=jnp.float32
    )
    live[...] = found

    lane_n = lanes_of((nx, 128))
    planes = jnp.zeros((nx, 128), jnp.float32)
    for y in range(ny):
        value = jnp.broadcast_to(heat_in[0, :, y : y + 1], (nx, 128))
        planes = jnp.where(lane_n % ny == y, value, planes)
    planes = jnp.where(lane_n % owners // ny == rows_of((nx, 128)), planes, 0.0)
    field = jnp.sum(planes, axis=0, keepdims=True)

    lane = lanes_of()
    halves = {
        ("x", -1): found,
        ("x", 1): turn(found, 64),
        ("y", -1): jnp.where(lane < 32, found, turn(found, 32)),
        ("y", 1): jnp.where(lane < 32, turn(found, 32), turn(found, 64)),
    }
    extras = {}
    for key, value in halves.items():
        extras[key] = [
            ((where, to, to + 64), value[t : t + 1] if to == 0 else turn(value, -64)[t : t + 1])
            for t, (where, to) in enumerate(chunk.live)
        ]
    kinds = stage_halo(
        lambda plane: own_u[8 * plane : 8 * plane + 8, :],
        stage,
        chunk,
        [((chunk.tail, chunk.tail_lane, 128), field)],
        extras,
    )
    send_chunks(stage, kinds, send, chunk, neighbour_ids(across), owners)
    for copy in later:
        copy.wait()


def make_masks(chunk, homes, landed, live, masks_ref, table, spread_ref, cases):
    lane1 = lanes_of((1, 128))
    table[...] = jnp.zeros((128, 128), jnp.float32)
    for x in range(4):
        for y in range(4):
            sx, sy = (-1, 0, 0, 1)[x], (-1, 0, 0, 1)[y]
            ix, iy = (1, 0, 1, 0)[x], (1, 0, 1, 0)[y]
            row = jnp.zeros((1, 128), jnp.float32)
            for t in range(TZ):
                if (sx, sy) == (0, 0):
                    value, start = live[t : t + 1, :], 32 * (2 * ix + iy)
                else:
                    where, start = chunk.live[t]
                    value = landed[homes[(sx, sy)] + where : homes[(sx, sy)] + where + 1, :]
                    start = start + 32 * (ix if sy else iy)
                here = (lane1 >= 32 * t) & (lane1 < 32 * t + 32)
                row = jnp.where(here, turn(value, start - 32 * t), row)
            table[4 * x + y : 4 * x + y + 1, :] = row
    by_code = jnp.transpose(table[...])
    big = (128, 128)
    for x in range(4):
        pick = jnp.where(rows_of(big) == 4 * x + lanes_of(big) // 32, 1.0, 0.0)
        alive = jnp.dot(by_code, pick, preferred_element_type=jnp.float32)
        spread_ref[128 * x : 128 * x + 128, :] = FAR_AWAY * (1.0 - alive)

    lane = lanes_of()
    half_layer = lane % 8
    parity = lane % 2
    cell_y = lane // 8 % 4
    low_rows = rows_of() < 4

    def crossing(position, step):
        return (position + step < 0) | (position + step >= 8)

    groups = grouped(NEAR + FAR)

    def at_t(t, carry):
        for code in range(27):
            for block in range(2):
                first, second = [
                    spread_ref[pl.ds(128 * x + 32 * t + code, 1), :] for x in (2 * block, 2 * block + 1)
                ]
                cases[16 * code + 8 * block : 16 * code + 8 * block + 8, :] = jnp.where(
                    low_rows, jnp.broadcast_to(first, (8, 128)), jnp.broadcast_to(second, (8, 128))
                )

        def case(ex, ey, ez, block):
            code = 9 * (ex + 1) + 3 * (ey + 1) + ez + 1
            return cases[16 * code + 8 * block : 16 * code + 8 * block + 8, :]

        for dz in sorted({key[1] for key, _ in groups}):
            cross_z = crossing(half_layer, dz)
            in_z = {}

            def level_z(ex, ey, block):
                if (ex, ey, block) not in in_z:
                    value = case(ex, ey, 0, block)
                    if dz:
                        value = jnp.where(cross_z, case(ex, ey, sign(dz), block), value)
                    in_z[(ex, ey, block)] = value
                return in_z[(ex, ey, block)]

            for (dy, other_z), dxs in groups:
                if other_z != dz:
                    continue
                cross_y = crossing(2 * cell_y + parity, dy)
                in_y = {}

                def level_y(ex, block):
                    if (ex, block) not in in_y:
                        value = level_z(ex, 0, block)
                        if dy:
                            value = jnp.where(cross_y, level_z(ex, sign(dy), block), value)
                        in_y[(ex, block)] = value
                    return in_y[(ex, block)]

                for dx in dxs:
                    cross_x = crossing(2 * (rows_of() % 4) + parity, dx)
                    for block in range(2):
                        value = level_y(0, block)
                        if dx:
                            value = jnp.where(cross_x, level_y(sign(dx), block), value)
                        at = MASK_SLOT[(dx, dy, dz)] * SIZE + BASE + 8 * block
                        masks_ref[pl.ds(at + t * ROWS, 8), :] = value
        return carry

    lax.fori_loop(0, TZ, at_t, 0)


def step_kernel(step, across, arriving, leaving, groups, limit, *refs):
    nx, ny = across
    owners = nx * ny
    refs = list(refs)
    last = leaving is None

    def take(count):
        taken = refs[:count]
        del refs[:count]
        return taken

    recv, in_u, in_v, noise = take(4)
    if step == 0:
        (live,) = take(1)
    else:
        masks_ref, in_grid, in_bad = take(3)
    send, out_grid, out_bad, out_u, out_v = take(5)
    if step == 0:
        (masks_ref,) = take(1)
    window, moved, slope, slope_moved, gaps, inverses, landed, tails_at, noise_own = take(9)
    v_own, stage, mixed = take(3)
    extra = refs
    u_own = out_u
    if step:
        v_own = out_v
    else:
        v_own, v_start = out_v, v_own
    if step == 0:
        table, spread_ref, cases = extra
    ids = neighbour_ids(across)
    lane = lanes_of()

    homes = receive_chunks(recv, landed, tails_at, arriving, ids, owners)
    if step == 0:
        make_masks(arriving, homes, landed, live, masks_ref, table, spread_ref, cases)

    tail = repeat_tail(tails_at[0:owners, :], arriving)
    if step == 0:
        table[...] = jnp.zeros((128, 128), jnp.float32)
        table[0:owners, :] = tail
        turned = jnp.transpose(table[...])[:owners]
        reach = 128
        while reach > owners:
            reach //= 2
            turned = turned + pltpu.roll(turned, reach, 1)
        grid = [turned[ny * x : ny * x + ny] for x in range(nx)]
        out_bad[...] = jnp.zeros((8, 128), jnp.float32)
    else:
        grid = [
            in_grid[ny * x : ny * x + ny, :] + tail[ny * x : ny * x + ny] * (1.0 / heat_capacity)
            for x in range(nx)
        ]
        grid = diffuse_grid(grid, across)
        where, start = arriving.reach
        from_row = owners * (where != arriving.tail)
        furthest = tails_at[from_row : from_row + owners, :]
        lane_n = lanes_of((owners, 128))
        furthest = jnp.where((lane_n >= start) & (lane_n < start + 32), furthest, 0.0)
        reached = jnp.max(furthest, axis=0, keepdims=True)
        reached = jnp.max(reached, axis=1, keepdims=True)
        over = jnp.broadcast_to(jnp.where(reached > limit, 1.0, 0.0), (8, 128))
        out_bad[...] = jnp.maximum(in_bad[...], over)
    for x in range(nx):
        out_grid[ny * x : ny * x + ny, :] = grid[x]
    local = temperatures_by_layer(out_grid[pl.ds(ids[(0, 0)], 1), :], owners)
    kick = jnp.sqrt(local * (2.0 * friction * atom_mass / time_step))

    def own_u(plane):
        return in_u[8 * plane : 8 * plane + 8, :]

    origin = jnp.minimum(lax.axis_index("gx"), 0)
    build_window(own_u, landed, homes, window, arriving, origin)
    mix_planes(3, window, mixed, origin)
    known = (window, moved, masks_ref, slope, gaps, inverses, groups)
    shift_planes(3, window, mixed, moved, groups, coordinate_shift, origin)
    for t in range(TZ):
        start = t * ROWS + BASE + 4
        density_sweep(lambda base: pl.ds(origin + (base + start), 8), 8 * t, *known)
    for edge in EDGES:
        start = BASE + edge
        density_sweep(
            lambda base: pl.ds(origin + (base + start), 2 * TZ, stride=ROWS // 2), None, *known
        )
    shift_planes(1, slope, None, slope_moved, groups, no_shift, origin)

    from_tiles(lambda c, ix, iy: noise[step, c, ix, :, iy, :], noise_own)
    speeds_in = in_v
    if step == 0:
        from_tiles(lambda c, ix, iy: in_v[c, ix, :, iy, :], v_start)
        speeds_in = v_start

    active = (lane >= 32) & (lane < 96)
    power = []
    furthest = jnp.zeros((8, 128), jnp.float32)
    for t in range(TZ):
        force = forces(t, window, moved, slope, slope_moved, gaps, inverses, groups, origin)
        layer = jnp.zeros((8, 128), jnp.float32)
        for c in range(3):
            at = 8 * (c * TZ + t)
            speed = speeds_in[at : at + 8, :]
            push = force[c] - friction * atom_mass * speed + kick[t : t + 1] * noise_own[at : at + 8, :]
            speed = speed + time_step / atom_mass * push
            speed = jnp.where(active, speed, 0.0)
            place = own_u(c * TZ + t) + time_step * speed
            v_own[at : at + 8, :] = speed
            u_own[at : at + 8, :] = place
            layer = layer + speed * speed
            furthest = jnp.maximum(furthest, jnp.abs(place))
        power.append(jnp.sum(layer, axis=0, keepdims=True))
    energy = energies_by_plane(power, owners) * (friction * atom_mass * time_step)
    if last:
        send[...] = jnp.broadcast_to(energy, (owners, 128))
        return
    furthest = jnp.max(furthest, axis=0, keepdims=True)
    furthest = jnp.broadcast_to(jnp.max(furthest, axis=1, keepdims=True), (1, 128))
    where, start = leaving.reach
    tail_row = [
        ((leaving.tail, leaving.tail_lane, 128), energy),
        ((where, start, start + 32), furthest),
    ]
    kinds = stage_halo(
        lambda plane: u_own[8 * plane : 8 * plane + 8, :], stage, leaving, tail_row, {}
    )
    send_chunks(stage, kinds, send, leaving, ids, owners)


def finish(across, recv, in_grid, heat):
    nx, ny = across
    grid = [
        in_grid[ny * x : ny * x + ny, :] + recv[ny * x : ny * x + ny, :] * (1.0 / heat_capacity)
        for x in range(nx)
    ]
    grid = diffuse_grid(grid, across)
    me = lax.axis_index("gx") * ny + lax.axis_index("gy")
    flat = rows_of((ny, 128)) == lanes_of((ny, 128))
    for x in range(nx):
        mine = jnp.where(lanes_of((ny, 128)) == me, grid[x], 0.0)
        mine = jnp.broadcast_to(jnp.sum(mine, axis=1, keepdims=True), (ny, 128))
        row = jnp.sum(jnp.where(flat, mine, 0.0), axis=0, keepdims=True)
        heat[0, x : x + 1, :] = row[:, :ny]


def leave(in_u, in_v, new_u, new_v):
    to_tiles(in_u, new_u)
    to_tiles(in_v, new_v)


def exchange(value):
    return lax.all_to_all(value, ("gx", "gy"), split_axis=0, concat_axis=0, tiled=True)


VMEM_BYTES = 28 * 1024 * 1024


def call(kernel, outs, scratch, operands, in_hbm=(), name=None):
    specs = [
        pl.BlockSpec(memory_space=pltpu.HBM if n in in_hbm else pltpu.VMEM)
        for n in range(len(operands))
    ]
    return pl.pallas_call(
        kernel,
        out_shape=[
            jax.ShapeDtypeStruct(*(out if isinstance(out[1], type) else (out, jnp.float32)))
            for out in outs
        ],
        in_specs=specs,
        out_specs=[pl.BlockSpec(memory_space=pltpu.VMEM)] * len(outs),
        scratch_shapes=scratch,
        compiler_params=pltpu.CompilerParams(vmem_limit_bytes=VMEM_BYTES),
        name=name,
    )(*operands)


def stencil_steps(displacement, velocity, noise, electron_temp, pair_list, pair_count):
    across = (lax.axis_size("gx"), lax.axis_size("gy"))
    owners = across[0] * across[1]

    def vmem(*shape):
        return pltpu.VMEM(shape, jnp.float32)

    tiles = (3, BXT, TZ, BYT, TILE)
    placed_u = jnp.swapaxes(displacement, 2, 3)
    placed_v = jnp.swapaxes(velocity, 2, 3)
    placed_noise = jnp.swapaxes(noise, 3, 4)
    slots = pair_list.shape[-1]
    first, two, three = Chunk(owners, 2, True), Chunk(owners, 2), Chunk(owners, 3)
    send, own_u, live, kept_heat, kept_count, own_v, near_noise = call(
        partial(prepare, across, first),
        [
            (owners, 1, 128 * first.rows),
            (72, 128),
            (8, 128),
            electron_temp.shape,
            ((8, 128), jnp.int32),
            placed_v.shape,
            placed_noise.shape,
        ],
        [
            pltpu.VMEM((8, (slots + 127) // 128 * 128), jnp.int32),
            vmem(*tiles),
            vmem(*electron_temp.shape),
            pltpu.VMEM(pair_list.shape, jnp.int32),
            pltpu.SMEM(pair_count.shape, jnp.int32),
            vmem(4 * 16, 128),
            pltpu.SemaphoreType.DMA((6,)),
        ],
        (
            placed_u,
            pltpu.with_memory_space_constraint(electron_temp, pltpu.HBM),
            pair_list,
            pair_count,
            placed_v,
            placed_noise,
        ),
        in_hbm=(0, 1, 2, 3, 4, 5),
        name="prepare",
    )
    near, far = grouped(NEAR), grouped(NEAR + FAR)
    plan = [
        (first, two, near, 1.0),
        (two, three, near, NEAR_LIMIT),
        (three, three, far, FAR_LIMIT),
        (three, None, far, FAR_LIMIT),
    ]
    masks = grid = bad = None
    for step, (arriving, leaving, groups, limit) in enumerate(plan):
        recv = exchange(send)
        last = leaving is None
        pairs = sum(len(dxs) for _, dxs in groups)
        outs = [
            (owners, 128) if last else (owners, 1, 128 * leaving.rows),
            (owners, 128),
            (8, 128),
            (72, 128),
            (72, 128),
        ]
        scratch = [
            vmem(3 * SIZE + PAD, 128),
            vmem(len(groups) * 3 * SIZE, 128),
            vmem(SIZE, 128),
            vmem(len(groups) * SIZE, 128),
            vmem(24 * pairs, 128),
            vmem(24 * pairs, 128),
            vmem(9 * 16 + 2 * PAD, 128),
            vmem(2 * owners, 128),
            vmem(72, 128),
            vmem(72, 128),
            vmem(4 * 16, 128),
            vmem(3 * SIZE, 128),
        ]
        if step == 0:
            outs.append((MASKS * SIZE, 128))
            scratch += [vmem(128, 128), vmem(512, 128), vmem(27 * 16, 128)]
            operands = (recv, own_u, own_v, near_noise, live)
        else:
            operands = (recv, own_u, own_v, near_noise, masks, grid, bad)
        got = call(
            partial(step_kernel, step, across, arriving, leaving, groups, limit),
            outs,
            scratch,
            operands,
            name=f"step{step}",
        )
        send, grid, bad, own_u, own_v = got[:5]
        if step == 0:
            masks = got[5]
    recv = exchange(send)
    new_u, new_v = call(leave, [tiles, tiles], [], (own_u, own_v), name="leave")
    (heat,) = call(partial(finish, across), [electron_temp.shape], [], (recv, grid), name="finish")
    kept = (kept_heat, kept_count[:1, :1])
    return bad[0, 0], kept, jnp.swapaxes(new_u, 2, 3), jnp.swapaxes(new_v, 2, 3), heat


def per_device(displacement, velocity, noise, electron_temp, pair_list, pair_count):
    given = (displacement, velocity, noise, electron_temp, pair_list, pair_count)
    bad, (kept_heat, kept_count), new_u, new_v, heat = stencil_steps(*given)
    given = (displacement, velocity, noise, kept_heat, pair_list, kept_count)
    return lax.cond(bad > 0.5, lambda: whole_sweep(*given), lambda: (new_u, new_v, heat))


def solution(mesh):
    placed = (
        P(None, "gx", "gy", None, None),
        P(None, "gx", "gy", None, None),
        P(None, None, "gx", "gy", None, None),
        P(("gx", "gy"), None, None),
        P("gx", "gy", None, None),
        P("gx", "gy"),
    )
    return jax.shard_map(
        per_device,
        mesh=mesh,
        in_specs=placed,
        out_specs=(
            P(None, "gx", "gy", None, None),
            P(None, "gx", "gy", None, None),
            P(("gx", "gy"), None, None),
        ),
        check_vma=False,
    )
```

```python
from functools import partial

import jax
import jax.numpy as jnp
from jax import lax
from jax.experimental import pallas as pl
from jax.experimental.pallas import tpu as pltpu
from jax.sharding import PartitionSpec as P

CB = 4
TILE = 128
BXT = 2
BYT = 2
TZ = 3
TILES = 12
STEPS = 4
SUB = 6


lattice_edge = 3.1652
density_cut = 4.400224
embed_scale = 1.896373
pair_cut = 3.25
coef_zero = 47.1346499
coef_one = -33.7665655
coef_two = 6.2541999
time_step = 0.005
atom_mass = 0.0190534
friction = 1.0
heat_capacity = 0.02
diffusion_rate = 0.12


def padded_2(block, sides, width):
    for axis, dim in sides:
        count = lax.axis_size(axis)
        forward = [(i, i + 1) for i in range(count - 1)]
        forward.append((count - 1, 0))
        backward = [(target, source) for source, target in forward]
        low = lax.ppermute(
            lax.slice_in_dim(block, block.shape[dim] - width, None, axis=dim), axis, forward
        )
        high = lax.ppermute(lax.slice_in_dim(block, 0, width, axis=dim), axis, backward)
        block = jnp.concatenate([low, block, high], axis=dim)
    return block


def lattice_sites():
    serial = jnp.arange(TILE, dtype=jnp.int32)
    cell_number = serial // 2
    half_step = (serial % 2).astype(jnp.float32) * 0.5
    corners = jnp.stack([cell_number // (CB * CB), cell_number // CB % CB, cell_number % CB])
    return lattice_edge * (corners.astype(jnp.float32) + half_step[None, :])


def plane_table(plane_total):
    serial = jnp.arange(TILE, dtype=jnp.int32)
    cell_number = serial // 2
    layer = 2 * (cell_number % CB) + serial % 2
    tiles = jnp.arange(TZ, dtype=jnp.int32)
    whole = tiles[:, None] * (2 * CB) + layer[None, :]
    return whole * plane_total // (2 * CB * TZ)


def pair_geometry(window, tile_index, neighbour_code, lattice):
    wide_y = BYT + 2
    depth_t = tile_index % TZ
    inner_y = tile_index // TZ % BYT
    inner_x = tile_index // (TZ * BYT)
    shift_x = neighbour_code // 9
    shift_y = neighbour_code // 3 % 3
    shift_z = neighbour_code % 3
    flattened = window.reshape(window.shape[0], (BXT + 2) * wide_y * TZ, TILE)
    own_index = ((inner_x + 1) * wide_y + inner_y + 1) * TZ + depth_t
    other_index = ((inner_x + shift_x) * wide_y + inner_y + shift_y) * TZ + (
        depth_t + shift_z - 1 + TZ
    ) % TZ
    own_tile = lax.dynamic_index_in_dim(flattened, own_index, 1, keepdims=False)
    other_tile = lax.dynamic_index_in_dim(flattened, other_index, 1, keepdims=False)
    offset = jnp.stack([shift_x - 1, shift_y - 1, shift_z - 1]).astype(jnp.float32) * (
        CB * lattice_edge
    )
    left = lattice + own_tile
    right = lattice + other_tile + offset[:, None]
    delta = left[:, :, None] - right[:, None, :]
    square = jnp.sum(delta * delta, axis=0)
    serial = jnp.arange(TILE, dtype=jnp.int32)
    same_atom = (neighbour_code == 13) & (serial[:, None] == serial[None, :])
    distance = jnp.sqrt(jnp.where(same_atom, 100.0, square))
    return (delta, distance, own_index, other_index)


def density_term(window, lattice, tile_index, neighbour_code):
    delta, distance, own_index, other_index = pair_geometry(
        window, tile_index, neighbour_code, lattice
    )
    dens_gap = distance - density_cut
    return jnp.sum(jnp.where(distance < density_cut, dens_gap * dens_gap, 0.0), axis=1)[None]


def force_term(window, embed_window, lattice, tile_index, neighbour_code):
    delta, distance, own_index, other_index = pair_geometry(
        window, tile_index, neighbour_code, lattice
    )
    flat_embed = embed_window.reshape((BXT + 2) * (BYT + 2) * TZ, TILE)
    own_embed = lax.dynamic_index_in_dim(flat_embed, own_index, 0, keepdims=False)
    other_embed = lax.dynamic_index_in_dim(flat_embed, other_index, 0, keepdims=False)
    pair_gap = distance - pair_cut
    poly = coef_zero + coef_one * distance + coef_two * distance * distance
    pair_slope = jnp.where(
        distance < pair_cut,
        2.0 * pair_gap * poly + pair_gap * pair_gap * (coef_one + 2.0 * coef_two * distance),
        0.0,
    )
    dens_gap = distance - density_cut
    dens_slope = jnp.where(distance < density_cut, 2.0 * dens_gap, 0.0)
    scalar = (pair_slope + (own_embed[:, None] + other_embed[None, :]) * dens_slope) / distance
    return -jnp.sum(scalar[None] * delta, axis=2)


def sweep_pairs(term_fn, channels, pair_table, pair_total):
    initial = jnp.zeros((channels, TILES, TILE), jnp.float32)

    def block_add(block_index, running):
        start = block_index * 27
        chosen = lax.dynamic_slice_in_dim(pair_table, start, 27, 1)
        live = start + jnp.arange(27, dtype=jnp.int32) < pair_total
        terms = jax.vmap(term_fn)(chosen[0], chosen[1])
        terms = jnp.where(live[:, None, None], terms, 0.0)
        return running.at[:, chosen[0]].add(jnp.swapaxes(terms, 0, 1))

    blocks = (pair_total + 26) // 27
    total = lax.fori_loop(0, blocks, block_add, initial)
    return total.reshape(channels, BXT, BYT, TZ, TILE)


def relax_slab(padded):
    center = padded[1:-1]
    beside_all = padded[2:] + padded[:-2] + jnp.roll(center, 1, 1) + jnp.roll(center, -1, 1)
    beside_all = beside_all + jnp.roll(center, 1, 2) + jnp.roll(center, -1, 2)
    return center + diffusion_rate * (beside_all - 6.0 * center)


def one_step(lattice, pair_table, pair_total, planes, owners, across, carry, noise_now):
    positions, speeds, heat_field = carry
    slab_depth = heat_field.shape[0]
    plane_total = slab_depth * owners
    arrived = lax.all_to_all(
        heat_field.reshape(slab_depth, owners), ("gx", "gy"), split_axis=1, concat_axis=0, tiled=True
    )
    column = arrived.reshape(-1)
    column_temp = jnp.take(column, planes).reshape(TZ, TILE)
    local_temp = jnp.broadcast_to(column_temp, (BXT, BYT, TZ, TILE))
    window = padded_2(positions, (("gx", 1), ("gy", 2)), 1)
    density = sweep_pairs(partial(density_term, window, lattice), 1, pair_table, pair_total)
    embed_slope = -embed_scale / (2.0 * jnp.sqrt(density))
    embed_window = padded_2(embed_slope, (("gx", 1), ("gy", 2)), 1)
    force = sweep_pairs(partial(force_term, window, embed_window, lattice), 3, pair_table, pair_total)
    kicker = jnp.sqrt(2.0 * friction * atom_mass * local_temp / time_step)[None] * noise_now
    speeds = speeds + time_step / atom_mass * (force - friction * atom_mass * speeds + kicker)
    positions = positions + time_step * speeds
    power = friction * atom_mass * time_step * jnp.sum(speeds * speeds, axis=0)
    tile_power = jnp.sum(power, axis=(0, 1)).reshape(-1)
    energy = jnp.zeros((plane_total,), jnp.float32).at[planes].add(tile_power)
    arrived = lax.all_to_all(
        energy.reshape(plane_total, 1), ("gx", "gy"), split_axis=0, concat_axis=1, tiled=True
    )
    heat_field = heat_field + arrived.reshape(slab_depth, *across) / heat_capacity

    def relax(sub_index, heat):
        return relax_slab(padded_2(heat, ((("gx", "gy"), 0),), 1))

    heat_field = lax.fori_loop(0, SUB, relax, heat_field)
    return (positions, speeds, heat_field)


def whole_sweep(displacement, velocity, noise, electron_temp, pair_list, pair_count):
    across = (lax.axis_size("gx"), lax.axis_size("gy"))
    owners = across[0] * across[1]
    planes = plane_table(electron_temp.shape[0] * owners).reshape(-1)
    step = partial(
        one_step, lattice_sites(), pair_list[0, 0], pair_count[0, 0], planes, owners, across
    )
    return lax.fori_loop(
        0,
        STEPS,
        lambda n, carry: step(carry, lax.dynamic_index_in_dim(noise, n, 0, keepdims=False)),
        (displacement, velocity, electron_temp),
    )


NEAR_SHELLS = (3, 4, 8)
FAR_SHELLS = (11, 12)
NEAR_LIMIT = 0.2900
FAR_LIMIT = 0.8170
HALF = 0.5 * lattice_edge
FAR_AWAY = 1.0e6
ROWS = 20
BASE = 2
SIZE = TZ * ROWS
EDGES = (2, 3)


def site_offsets(shells):
    span = range(-3, 4)
    found = []
    for x in span:
        for y in span:
            for z in span:
                if x % 2 == y % 2 == z % 2 and x * x + y * y + z * z in shells:
                    found.append((x, y, z))
    return found


def grouped(offsets):
    table = {}
    for x, y, z in offsets:
        table.setdefault((y, z), []).append(x)
    return sorted(table.items())


NEAR = site_offsets(NEAR_SHELLS)
FAR = site_offsets(FAR_SHELLS)
MASK_SLOT = {offset: slot for slot, offset in enumerate(NEAR + FAR)}
MASKS = len(MASK_SLOT)


def by_x(groups):
    table = {}
    for n, ((dy, dz), dxs) in enumerate(groups):
        for dx in dxs:
            table.setdefault(dx, []).append((n, dy, dz))
    return sorted(table.items())


def sign(value):
    return (value > 0) - (value < 0)


def lanes_of(shape=(8, 128)):
    return lax.broadcasted_iota(jnp.int32, shape, len(shape) - 1)


def rows_of(shape=(8, 128)):
    return lax.broadcasted_iota(jnp.int32, shape, len(shape) - 2)


def turn(value, amount):
    amount = (-amount) % 128
    return value if amount == 0 else pltpu.roll(value, amount, value.ndim - 1)


def pick_lanes(value, index):
    return jnp.take_along_axis(value, index, axis=1, mode="promise_in_bounds")


class Chunk:
    def __init__(self, owners, cells, first=False):
        self.cells = cells
        self.narrow = owners <= 32
        halo = 9 if cells == 2 else 14
        if self.narrow:
            self.tail = 9 if cells == 2 else 13
            self.tail_lane = 96
            self.reach = (self.tail, 64)
            self.rows = self.tail + 1
        else:
            self.tail = halo
            self.tail_lane = 0
            self.reach = (halo + 1, 64)
            self.rows = halo + 2
        if first:
            self.live = [(self.reach[0], 0), (self.rows, 0), (self.rows, 64)]
            self.rows += 1

    def x_home(self, plane, row):
        if plane < 8:
            return self.cells * (plane // 2) + row, plane % 2
        return 4 * self.cells + row // 2, row % 2


def repeat_tail(value, chunk):
    if not chunk.narrow:
        return value
    return pick_lanes(value, 96 + lanes_of(value.shape) % 32)


def from_tiles(read, out):
    lane = lanes_of((TZ, 128))
    own = (lane >= 32) & (lane < 96)
    for c in range(3):
        for ix in range(BXT):
            first, second = [read(c, ix, iy) for iy in range(BYT)]
            for cx in range(CB):
                both = jnp.where(lane < 64, turn(first, 32 * cx - 32), turn(second, 32 * cx - 64))
                start = c * TZ * 8 + CB * ix + cx
                out[pl.ds(start, TZ, stride=8), :] = jnp.where(own, both, 0.0)


def to_tiles(source, out):
    lane = lanes_of((TZ, 128))
    for c in range(3):
        for ix in range(BXT):
            rows = [source[pl.ds(c * TZ * 8 + CB * ix + cx, TZ, stride=8), :] for cx in range(CB)]
            for iy in range(BYT):
                value = None
                for cx in range(CB):
                    piece = turn(rows[cx], 32 + 32 * iy - 32 * cx)
                    value = piece if value is None else jnp.where(lane >= 32 * cx, piece, value)
                out[c, ix, :, iy, :] = value


def each(count, body):
    if count <= 32:
        for index in range(count):
            body(index, 0)
    else:
        lax.fori_loop(0, count, body, 0, unroll=8)


def stage_halo(own, stage, chunk, tail_row, extras):
    w = chunk.cells
    lane, row = lanes_of(), rows_of()
    kinds = {}
    depth = stage.shape[0] // 4
    low = lane < 64
    third = [pick for pick in range(5)] if w == 3 else []
    for kind, (axis, side) in enumerate((("x", -1), ("x", 1), ("y", -1), ("y", 1))):
        at = kind * depth
        kinds[(axis, side)] = at
        if axis == "x":
            first = 8 - w if side == 1 else 0
            for pair in range(4):
                both = jnp.where(low, turn(own(2 * pair), 32), turn(own(2 * pair + 1), -32))
                stage[at + w * pair : at + w * pair + w, :] = both[first : first + w]
            last = own(8)
            a, b = turn(last, 32), turn(last, -32)
            low1 = lanes_of((1, 128)) < 64
            stage[at + 4 * w : at + 4 * w + 1, :] = jnp.where(
                low1, a[first : first + 1], b[first + 1 : first + 2]
            )
            if w == 3:
                stage[at + 13 : at + 14, :] = a[first + 2 : first + 3]
        else:
            start = 80 if side == 1 else 32
            packed = None
            for plane in range(8):
                piece = turn(own(plane), start - 16 * plane)
                packed = piece if packed is None else jnp.where(lane >= 16 * plane, piece, packed)
            stage[at : at + 8, :] = packed
            flat = pick_lanes(own(8), start + lane % 16)
            flat = jnp.where(lane // 16 == row, flat, 0.0)
            stage[at + 8 : at + 9, :] = jnp.sum(flat, axis=0, keepdims=True)
            start = 72 if side == 1 else 48
            for pair in third:
                flat = pick_lanes(own(2 * pair), start + lane % 8)
                if pair < 4:
                    flat = jnp.where(low, flat, pick_lanes(own(2 * pair + 1), start + lane % 8))
                flat = jnp.where(lane % 64 // 8 == row, flat, 0.0)
                stage[at + 9 + pair : at + 10 + pair, :] = jnp.sum(flat, axis=0, keepdims=True)
        for (where, lane_from, lane_to), value in tail_row + extras.get((axis, side), []):
            lane1 = lanes_of((1, 128))
            old = stage[at + where : at + where + 1, :]
            here = (lane1 >= lane_from) & (lane1 < lane_to)
            stage[at + where : at + where + 1, :] = jnp.where(here, value, old)
    return kinds


def send_chunks(stage, kinds, send_ref, chunk, ids, owners):
    tails = sorted({chunk.tail, chunk.reach[0]})
    at = kinds[("x", 1)]
    rows = {where: stage[at + where : at + where + 1, :] for where in tails}

    for (sx, sy), ident in ids.items():
        if (sx, sy) == (0, 0):
            continue
        at = kinds[("y", sy)] if sy else kinds[("x", sx)]
        for k in range(chunk.rows):
            if k not in tails:
                send_ref[ident, :, 128 * k : 128 * k + 128] = stage[at + k : at + k + 1, :]

    def fill(index, carry):
        for where in tails:
            send_ref[index, :, 128 * where : 128 * where + 128] = rows[where]
        return carry

    each(owners, fill)
    for (sx, sy), ident in ids.items():
        if (sx, sy) == (0, 0):
            continue
        at = kinds[("y", sy)] if sy else kinds[("x", sx)]
        for k in tails:
            send_ref[ident, :, 128 * k : 128 * k + 128] = stage[at + k : at + k + 1, :]


def receive_chunks(recv_ref, landed, tails_at, chunk, ids, owners):
    depth = (landed.shape[0] - 2 * PAD) // 9
    homes = {}
    for n, ((sx, sy), ident) in enumerate(ids.items()):
        if (sx, sy) == (0, 0):
            continue
        homes[(sx, sy)] = PAD + n * depth
        for k in range(chunk.rows):
            landed[PAD + n * depth + k : PAD + n * depth + k + 1, :] = recv_ref[ident, :, 128 * k : 128 * k + 128]

    tails = sorted({chunk.tail, chunk.reach[0]})

    def take(index, carry):
        for n, where in enumerate(tails):
            tails_at[pl.ds(n * owners + index, 1), :] = recv_ref[index, :, 128 * where : 128 * where + 128]
        return carry

    each(owners, take)
    return homes


PAD = 8


def build_window(own, landed, homes, window, chunk, origin):
    w = chunk.cells
    lane, row = lanes_of(), rows_of()
    zero = jnp.zeros((8, 128), jnp.float32)
    middle = (lane >= 32) & (lane < 96)
    first_rows = row < 4

    def outer(start, size, sy):
        values = [landed[homes[(sx, sy)] + start : homes[(sx, sy)] + start + size, :] for sx in (1, -1)]
        if size == 1:
            values = [jnp.broadcast_to(value, (8, 128)) for value in values]
        return jnp.where(first_rows, values[0], values[1])

    def inner(start, size, sy):
        value = landed[homes[(0, sy)] + start : homes[(0, sy)] + start + size, :]
        return jnp.broadcast_to(value, (8, 128))

    sides = (-1, 1)
    packed = {(sy, out): (outer if out else inner)(0, 8, sy) for sy in sides for out in (0, 1)}
    for plane in range(9):
        at = plane * ROWS + BASE
        parts = [own(plane), zero]
        for sy in sides:
            target = 16 if sy == -1 else 96
            here = (lane >= target) & (lane < target + 16)
            beyond = 8 if sy == -1 else 112
            here_third = (lane >= beyond) & (lane < beyond + 8)
            for out in (0, 1):
                if plane < 8:
                    piece = turn(packed[(sy, out)], 16 * plane - target)
                else:
                    wide = (outer if out else inner)(8, 1, sy)
                    piece = pick_lanes(wide, 16 * row + lane % 16)
                parts[out] = jnp.where(here, piece, parts[out])
                if w == 3:
                    wide = (outer if out else inner)(9 + plane // 2, 1, sy)
                    piece = pick_lanes(wide, 64 * (plane % 2) + 8 * row + lane % 8)
                    parts[out] = jnp.where(here_third, piece, parts[out])
        centre, rim = parts
        if plane < 8:
            home, half = chunk.x_home(plane, 0)
            back = -32 if half == 0 else 32
            behind = landed[pl.ds(origin + homes[(1, 0)] + home, 8), :]
            ahead = landed[pl.ds(origin + homes[(-1, 0)] + home - (4 - w) - 4, 8), :]
            piece = turn(jnp.where(first_rows, behind, ahead), back)
            rim = jnp.where(middle & ((row < w) | (row >= 8 - w)), piece, rim)
        else:
            for k in range(w):
                home, half = chunk.x_home(plane, k)
                back = -32 if half == 0 else 32
                for sx, to in ((1, k), (-1, 8 - w + k)):
                    base = homes[(sx, 0)] + home
                    piece = turn(jnp.broadcast_to(landed[base : base + 1, :], (8, 128)), back)
                    rim = jnp.where(middle & (row == to), piece, rim)
        window[pl.ds(origin + at, 8), :] = pltpu.roll(rim, 4, 0)
        window[pl.ds(origin + at + 12, 8), :] = rim
        window[pl.ds(origin + at + 4, 8), :] = centre


def mix_planes(count, source, mixed, origin):
    even = lanes_of((16, 128)) % 2 == 0
    for plane in range(count * TZ):
        at = plane * ROWS + BASE
        here = source[pl.ds(origin + at, 16), :]
        after = turn(source[pl.ds(origin + at + 1, 16), :], 8)
        mixed[pl.ds(origin + at, 16), :] = jnp.where(even, after, here)


def sources(dy, dz, use_mixed):
    s = sign(dz)
    low = dy // 2
    if dy % 2 == 0 or use_mixed:
        out = [(None, 0, dz + 8 * low, 0)]
        if s:
            out.append((None, s, dz - 8 * s + 8 * low, 0))
        return out
    out = [(0, 0, dz + 8 * low, 0), (1, 0, dz + 8 * (low + 1), 1)]
    for parity, k in ((0, low), (1, low + 1)):
        if any(not 0 <= iz + dz < 8 for iz in range(parity, 8, 2)):
            out.append((parity, s, dz - 8 * s + 8 * k, parity))
    return out


def shift_planes(count, source, mixed, out, groups, constants, origin, ready=None):
    half_layer = lanes_of((16, 128)) % 8
    parity = half_layer % 2
    slots = {key: n for n, (key, _) in enumerate(groups)}
    planes = [(c, t) for c in range(count) for t in range(TZ)]
    for dz in sorted({key[1] for key in slots}, key=lambda z: (z % 2, abs(z))):
        dys = sorted((key[0] for key in slots if key[1] == dz), key=abs)
        carried = (half_layer + dz >= 8) | (half_layer + dz < 0)
        ref = mixed if dz % 2 and mixed is not None else source
        turned = {}

        def taken(c, t, shift, down):
            key = (c, t, shift, down)
            if key not in turned:
                at = (c * TZ + t) * ROWS + BASE + down
                turned[key] = turn(ref[pl.ds(origin + at, 16), :], shift)
            return turned[key]

        for dy in dys:
            parts = sources(dy, dz, mixed is not None)
            for want, carry_z, shift, down in parts:
                for c, t in planes:
                    taken(c, t, shift, down)
            for c, t in planes:
                value = None
                for want, carry_z, shift, down in parts:
                    piece = taken(c, (t + carry_z) % TZ, shift, down)
                    if value is None:
                        value = piece
                        continue
                    here = None
                    if want is not None:
                        here = parity == want
                    if carry_z:
                        here = carried if here is None else here & carried
                    value = jnp.where(here, piece, value)
                shift_by = constants(c, dy, dz)
                if shift_by:
                    value = value + shift_by
                at = slots[(dy, dz)] * count * SIZE + (c * TZ + t) * ROWS + BASE
                out[pl.ds(origin + at, 16), :] = value
            if ready is not None:
                ready(slots[(dy, dz)], dy, dz)


def coordinate_shift(c, dy, dz):
    return (0.0, HALF * dy, HALF * dz)[c]


def no_shift(c, dy, dz):
    return 0.0


def row_start(dx):
    return dx // 2 if dx % 2 == 0 else (dx - 1) // 2


class DensitySweep:
    def __init__(self, window, moved, masks_ref, gaps, inverses, starts, groups, origin):
        self.refs = (window, moved, masks_ref, gaps, inverses, starts)
        self.groups = dict(groups)
        self.targets = []
        for t in range(TZ):
            self.targets.append((self.own_rows(origin, t * ROWS + BASE + 4), 8 * t, 8))
        for edge in EDGES:
            self.targets.append((self.edge_rows(origin, BASE + edge), None, 2 * TZ))
        self.xs = sorted({dx for dxs in self.groups.values() for dx in dxs})
        self.totals = [jnp.zeros((height, 128), jnp.float32) for _, _, height in self.targets]
        self.own = []
        for k, (rows, _, height) in enumerate(self.targets):
            self.own.append([window[rows(c * SIZE), :] for c in (1, 2)])
            own_x = window[rows(0), :]
            for j, dx in enumerate(self.xs):
                at = 8 * (k * len(self.xs) + j)
                starts[at : at + height, :] = own_x - HALF * dx

    @staticmethod
    def own_rows(origin, start):
        return lambda base: pl.ds(origin + (base + start), 8)

    @staticmethod
    def edge_rows(origin, start):
        return lambda base: pl.ds(origin + (base + start), 2 * TZ, stride=ROWS // 2)

    def part(self, n, dy, dz):
        window, moved, masks_ref, gaps, inverses, starts = self.refs
        for dx in self.groups[(dy, dz)]:
            down = row_start(dx)
            slot = MASK_SLOT[(dx, dy, dz)]
            for k, (rows, keep, height) in enumerate(self.targets):
                other = [moved[rows((3 * n + c) * SIZE + down), :] for c in range(3)]
                at = 8 * (k * len(self.xs) + self.xs.index(dx))
                ex = starts[at : at + height, :] - other[0]
                ey = self.own[k][0] - other[1]
                ez = self.own[k][1] - other[2]
                square = ex * ex + ey * ey + (ez * ez + masks_ref[rows(slot * SIZE), :])
                inverse = lax.rsqrt(square)
                gap = jnp.minimum(square * inverse - density_cut, 0.0)
                self.totals[k] = self.totals[k] + gap * gap
                if keep is not None:
                    gaps[keep + 24 * slot : keep + 24 * slot + 8, :] = gap
                    inverses[keep + 24 * slot : keep + 24 * slot + 8, :] = inverse

    def finish(self, slope):
        for total, (rows, _, _) in zip(self.totals, self.targets):
            slope[rows(0), :] = -embed_scale * lax.rsqrt(total)


def forces(t, window, moved, slope, slope_moved, gaps, inverses, groups, origin):
    at = t * ROWS + BASE + 4
    own = [window[pl.ds(origin + (c * SIZE + at), 8), :] for c in range(3)]
    own_slope = slope[pl.ds(origin + at, 8), :]
    first = 2.0 * (coef_zero + coef_one * pair_cut + coef_two * pair_cut * pair_cut)
    second = 3.0 * (coef_one + 2.0 * coef_two * pair_cut)
    third = 4.0 * coef_two
    zero = jnp.zeros((8, 128), jnp.float32)
    total = [zero, zero, zero]
    sum_all = zero
    for dx, parts in by_x(groups):
        down = row_start(dx)
        sum_here = zero
        for n, dy, dz in parts:
            slot = MASK_SLOT[(dx, dy, dz)]
            row = 3 * n * SIZE + at + down
            other_slope = slope_moved[pl.ds(origin + (n * SIZE + at + down), 8), :]
            gap = gaps[24 * slot + 8 * t : 24 * slot + 8 * t + 8, :]
            inverse = inverses[24 * slot + 8 * t : 24 * slot + 8 * t + 8, :]
            near = jnp.minimum(gap + (density_cut - pair_cut), 0.0)
            scalar = (own_slope + other_slope) * gap + near * (first + near * (second + third * near))
            scalar = scalar * inverse
            sum_here = sum_here + scalar
            for c in range(3):
                total[c] = total[c] + scalar * moved[pl.ds(origin + (row + c * SIZE), 8), :]
        sum_all = sum_all + sum_here
        if dx:
            total[0] = total[0] + (HALF * dx) * sum_here
    return [total[c] - own[c] * sum_all for c in range(3)]


def binomial(n, k):
    value = 1
    for j in range(k):
        value = value * (n - j) // (j + 1)
    return value


def diffuse_grid(grid, across):
    nx, ny = across
    d = diffusion_rate
    pairs = [
        [heat] + [pltpu.roll(heat, k, 1) + pltpu.roll(heat, 128 - k, 1) for k in range(1, SUB + 1)]
        for heat in grid
    ]

    def powers(x, k):
        total = None
        for j in range(k // 2 + 1):
            weight = binomial(k, j) * binomial(SUB, k) * d**k
            term = weight * pairs[x][k - 2 * j]
            total = term if total is None else total + term
        return total

    result = [powers(x, 0) for x in range(nx)]
    for k in range(1, SUB + 1):
        columns = []
        for x in range(nx):
            heat = result[x]
            beside = result[(x + 1) % nx] + result[(x - 1) % nx]
            beside = beside + pltpu.roll(heat, 1, 0) + pltpu.roll(heat, ny - 1, 0)
            columns.append(((1.0 - 6.0 * d) * heat + powers(x, k)) + d * beside)
        result = columns
    return result


LAYERS = 2 * CB * TZ


def temperatures_by_layer(column, plane_total):
    layer = 2 * CB * rows_of() + lanes_of() % (2 * CB)
    layer = jnp.minimum(layer, LAYERS - 1)
    return pick_lanes(jnp.broadcast_to(column, (8, 128)), layer * plane_total // LAYERS)


def energies_by_plane(power, plane_total):
    row, lane = rows_of(), lanes_of()
    stacked = jnp.zeros((8, 128), jnp.float32)
    for t in range(TZ):
        stacked = jnp.where(row == t, power[t], stacked)
    plane = lane % plane_total
    start = (plane * LAYERS + plane_total - 1) // plane_total
    total = jnp.zeros((8, 128), jnp.float32)
    for extra in range(max(1, -(-LAYERS // plane_total))):
        layer = start + extra
        inside = layer - 2 * CB * row
        here = (inside >= 0) & (inside < 2 * CB) & (layer < LAYERS)
        here = here & (layer * plane_total // LAYERS == plane)
        first = 32 + jnp.clip(inside, 0, 2 * CB - 1)
        taken = [pick_lanes(stacked, first + 8 * y) for y in range(BYT * CB)]
        while len(taken) > 1:
            taken = [a + b for a, b in zip(taken[::2], taken[1::2])]
        total = total + jnp.where(here, taken[0], 0.0)
    return jnp.sum(total, axis=0, keepdims=True)


def neighbour_ids(across):
    nx, ny = across
    bx, by = lax.axis_index("gx"), lax.axis_index("gy")
    at_x = {-1: jnp.where(bx == 0, nx - 1, bx - 1), 0: bx, 1: jnp.where(bx == nx - 1, 0, bx + 1)}
    at_y = {-1: jnp.where(by == 0, ny - 1, by - 1), 0: by, 1: jnp.where(by == ny - 1, 0, by + 1)}
    return {(sx, sy): at_x[sx] * ny + at_y[sy] for sx in (-1, 0, 1) for sy in (-1, 0, 1)}


def prepare(across, chunk, disp, heat, pairs, count, vel, noise, send, own_u, live, kept_heat, kept_count, near_vel, near_noise, lists, disp_in, heat_in, pairs_in, count_in, stage, sems):
    nx, ny = across
    owners = nx * ny
    copies = [
        pltpu.make_async_copy(source, target, sems.at[n])
        for n, (source, target) in enumerate(
            ((disp, disp_in), (heat, heat_in), (pairs, pairs_in), (count, count_in))
        )
    ]
    later = [
        pltpu.make_async_copy(vel, near_vel, sems.at[4]),
        pltpu.make_async_copy(noise, near_noise, sems.at[5]),
    ]
    for copy in copies + later:
        copy.start()
    lists[...] = jnp.full(lists.shape, -1, jnp.int32)
    for copy in copies:
        copy.wait()

    from_tiles(lambda c, ix, iy: disp_in[c, ix, :, iy, :], own_u)
    kept_heat[...] = heat_in[...]
    kept_count[...] = jnp.full((8, 128), count_in[0, 0], jnp.int32)

    slots = pairs_in.shape[3]
    width = lists.shape[1]
    lists[0:2, 0:slots] = pairs_in[0, 0]
    tile = lists[0:1, :]
    code = lists[1:2, :]
    valid = (lanes_of((1, width)) < count_in[0, 0]) & (tile >= 0)
    column = jnp.where(tile >= 3, 1, 0) + jnp.where(tile >= 6, 1, 0) + jnp.where(tile >= 9, 1, 0)
    depth = jnp.where(valid, tile - 3 * column, -1)
    place = 32 * column + code
    left = jnp.where(rows_of((8, width)) == depth, 1.0, 0.0)
    right = jnp.where(rows_of((128, width)) == place, 1.0, 0.0)
    found = lax.dot_general(
        left, right, (((1,), (1,)), ((), ())), preferred_element_type=jnp.float32
    )
    live[...] = found

    lane_n = lanes_of((nx, 128))
    planes = jnp.zeros((nx, 128), jnp.float32)
    for y in range(ny):
        value = jnp.broadcast_to(heat_in[0, :, y : y + 1], (nx, 128))
        planes = jnp.where(lane_n % ny == y, value, planes)
    planes = jnp.where(lane_n % owners // ny == rows_of((nx, 128)), planes, 0.0)
    field = jnp.sum(planes, axis=0, keepdims=True)

    lane = lanes_of()
    halves = {
        ("x", -1): found,
        ("x", 1): turn(found, 64),
        ("y", -1): jnp.where(lane < 32, found, turn(found, 32)),
        ("y", 1): jnp.where(lane < 32, turn(found, 32), turn(found, 64)),
    }
    extras = {}
    for key, value in halves.items():
        extras[key] = [
            ((where, to, to + 64), value[t : t + 1] if to == 0 else turn(value, -64)[t : t + 1])
            for t, (where, to) in enumerate(chunk.live)
        ]
    kinds = stage_halo(
        lambda plane: own_u[8 * plane : 8 * plane + 8, :],
        stage,
        chunk,
        [((chunk.tail, chunk.tail_lane, 128), field)],
        extras,
    )
    send_chunks(stage, kinds, send, chunk, neighbour_ids(across), owners)
    for copy in later:
        copy.wait()


def make_masks(chunk, homes, landed, live, masks_ref, table, spread_ref, cases):
    lane1 = lanes_of((1, 128))
    table[...] = jnp.zeros((128, 128), jnp.float32)
    for x in range(4):
        for y in range(4):
            sx, sy = (-1, 0, 0, 1)[x], (-1, 0, 0, 1)[y]
            ix, iy = (1, 0, 1, 0)[x], (1, 0, 1, 0)[y]
            row = jnp.zeros((1, 128), jnp.float32)
            for t in range(TZ):
                if (sx, sy) == (0, 0):
                    value, start = live[t : t + 1, :], 32 * (2 * ix + iy)
                else:
                    where, start = chunk.live[t]
                    value = landed[homes[(sx, sy)] + where : homes[(sx, sy)] + where + 1, :]
                    start = start + 32 * (ix if sy else iy)
                here = (lane1 >= 32 * t) & (lane1 < 32 * t + 32)
                row = jnp.where(here, turn(value, start - 32 * t), row)
            table[4 * x + y : 4 * x + y + 1, :] = row
    by_code = jnp.transpose(table[...])
    big = (128, 128)
    for x in range(4):
        pick = jnp.where(rows_of(big) == 4 * x + lanes_of(big) // 32, 1.0, 0.0)
        alive = jnp.dot(by_code, pick, preferred_element_type=jnp.float32)
        spread_ref[128 * x : 128 * x + 128, :] = FAR_AWAY * (1.0 - alive)

    lane = lanes_of()
    half_layer = lane % 8
    parity = lane % 2
    cell_y = lane // 8 % 4
    low_rows = rows_of() < 4

    def crossing(position, step):
        return (position + step < 0) | (position + step >= 8)

    groups = grouped(NEAR + FAR)

    def at_t(t, carry):
        for code in range(27):
            for block in range(2):
                first, second = [
                    spread_ref[pl.ds(128 * x + 32 * t + code, 1), :] for x in (2 * block, 2 * block + 1)
                ]
                cases[16 * code + 8 * block : 16 * code + 8 * block + 8, :] = jnp.where(
                    low_rows, jnp.broadcast_to(first, (8, 128)), jnp.broadcast_to(second, (8, 128))
                )

        def case(ex, ey, ez, block):
            code = 9 * (ex + 1) + 3 * (ey + 1) + ez + 1
            return cases[16 * code + 8 * block : 16 * code + 8 * block + 8, :]

        for dz in sorted({key[1] for key, _ in groups}):
            cross_z = crossing(half_layer, dz)
            in_z = {}

            def level_z(ex, ey, block):
                if (ex, ey, block) not in in_z:
                    value = case(ex, ey, 0, block)
                    if dz:
                        value = jnp.where(cross_z, case(ex, ey, sign(dz), block), value)
                    in_z[(ex, ey, block)] = value
                return in_z[(ex, ey, block)]

            for (dy, other_z), dxs in groups:
                if other_z != dz:
                    continue
                cross_y = crossing(2 * cell_y + parity, dy)
                in_y = {}

                def level_y(ex, block):
                    if (ex, block) not in in_y:
                        value = level_z(ex, 0, block)
                        if dy:
                            value = jnp.where(cross_y, level_z(ex, sign(dy), block), value)
                        in_y[(ex, block)] = value
                    return in_y[(ex, block)]

                for dx in dxs:
                    cross_x = crossing(2 * (rows_of() % 4) + parity, dx)
                    for block in range(2):
                        value = level_y(0, block)
                        if dx:
                            value = jnp.where(cross_x, level_y(sign(dx), block), value)
                        at = MASK_SLOT[(dx, dy, dz)] * SIZE + BASE + 8 * block
                        masks_ref[pl.ds(at + t * ROWS, 8), :] = value
        return carry

    lax.fori_loop(0, TZ, at_t, 0)


def step_kernel(step, across, arriving, leaving, groups, limit, *refs):
    nx, ny = across
    owners = nx * ny
    refs = list(refs)
    last = leaving is None

    def take(count):
        taken = refs[:count]
        del refs[:count]
        return taken

    recv, in_u, in_v, noise = take(4)
    if step == 0:
        (live,) = take(1)
    else:
        masks_ref, in_grid, in_bad = take(3)
    send, out_grid, out_bad, out_u, out_v = take(5)
    if step == 0:
        (masks_ref,) = take(1)
    window, moved, slope, slope_moved, gaps, inverses, landed, tails_at, noise_own = take(9)
    v_own, stage, mixed, starts = take(4)
    extra = refs
    u_own = out_u
    if step:
        v_own = out_v
    else:
        v_own, v_start = out_v, v_own
    if step == 0:
        table, spread_ref, cases = extra
    ids = neighbour_ids(across)
    lane = lanes_of()

    homes = receive_chunks(recv, landed, tails_at, arriving, ids, owners)
    if step == 0:
        make_masks(arriving, homes, landed, live, masks_ref, table, spread_ref, cases)

    tail = repeat_tail(tails_at[0:owners, :], arriving)
    if step == 0:
        table[...] = jnp.zeros((128, 128), jnp.float32)
        table[0:owners, :] = tail
        turned = jnp.transpose(table[...])[:owners]
        reach = 128
        while reach > owners:
            reach //= 2
            turned = turned + pltpu.roll(turned, reach, 1)
        grid = [turned[ny * x : ny * x + ny] for x in range(nx)]
        out_bad[...] = jnp.zeros((8, 128), jnp.float32)
    else:
        grid = [
            in_grid[ny * x : ny * x + ny, :] + tail[ny * x : ny * x + ny] * (1.0 / heat_capacity)
            for x in range(nx)
        ]
        grid = diffuse_grid(grid, across)
        where, start = arriving.reach
        from_row = owners * (where != arriving.tail)
        furthest = tails_at[from_row : from_row + owners, :]
        lane_n = lanes_of((owners, 128))
        furthest = jnp.where((lane_n >= start) & (lane_n < start + 32), furthest, 0.0)
        reached = jnp.max(furthest, axis=0, keepdims=True)
        reached = jnp.max(reached, axis=1, keepdims=True)
        over = jnp.broadcast_to(jnp.where(reached > limit, 1.0, 0.0), (8, 128))
        out_bad[...] = jnp.maximum(in_bad[...], over)
    for x in range(nx):
        out_grid[ny * x : ny * x + ny, :] = grid[x]
    local = temperatures_by_layer(out_grid[pl.ds(ids[(0, 0)], 1), :], owners)
    kick = jnp.sqrt(local * (2.0 * friction * atom_mass / time_step))

    def own_u(plane):
        return in_u[8 * plane : 8 * plane + 8, :]

    origin = jnp.minimum(lax.axis_index("gx"), 0)
    build_window(own_u, landed, homes, window, arriving, origin)
    mix_planes(3, window, mixed, origin)
    known = (window, moved, masks_ref, slope, gaps, inverses, groups)
    sweep = DensitySweep(window, moved, masks_ref, gaps, inverses, starts, groups, origin)
    shift_planes(3, window, mixed, moved, groups, coordinate_shift, origin, sweep.part)
    sweep.finish(slope)
    shift_planes(1, slope, None, slope_moved, groups, no_shift, origin)

    from_tiles(lambda c, ix, iy: noise[step, c, ix, :, iy, :], noise_own)
    speeds_in = in_v
    if step == 0:
        from_tiles(lambda c, ix, iy: in_v[c, ix, :, iy, :], v_start)
        speeds_in = v_start

    active = (lane >= 32) & (lane < 96)
    power = []
    furthest = jnp.zeros((8, 128), jnp.float32)
    for t in range(TZ):
        force = forces(t, window, moved, slope, slope_moved, gaps, inverses, groups, origin)
        layer = jnp.zeros((8, 128), jnp.float32)
        for c in range(3):
            at = 8 * (c * TZ + t)
            speed = speeds_in[at : at + 8, :]
            push = force[c] - friction * atom_mass * speed + kick[t : t + 1] * noise_own[at : at + 8, :]
            speed = speed + time_step / atom_mass * push
            speed = jnp.where(active, speed, 0.0)
            place = own_u(c * TZ + t) + time_step * speed
            v_own[at : at + 8, :] = speed
            u_own[at : at + 8, :] = place
            layer = layer + speed * speed
            furthest = jnp.maximum(furthest, jnp.abs(place))
        power.append(jnp.sum(layer, axis=0, keepdims=True))
    energy = energies_by_plane(power, owners) * (friction * atom_mass * time_step)
    if last:
        send[...] = jnp.broadcast_to(energy, (owners, 128))
        return
    furthest = jnp.max(furthest, axis=0, keepdims=True)
    furthest = jnp.broadcast_to(jnp.max(furthest, axis=1, keepdims=True), (1, 128))
    where, start = leaving.reach
    tail_row = [
        ((leaving.tail, leaving.tail_lane, 128), energy),
        ((where, start, start + 32), furthest),
    ]
    kinds = stage_halo(
        lambda plane: u_own[8 * plane : 8 * plane + 8, :], stage, leaving, tail_row, {}
    )
    send_chunks(stage, kinds, send, leaving, ids, owners)


def finish(across, recv, in_grid, heat):
    nx, ny = across
    grid = [
        in_grid[ny * x : ny * x + ny, :] + recv[ny * x : ny * x + ny, :] * (1.0 / heat_capacity)
        for x in range(nx)
    ]
    grid = diffuse_grid(grid, across)
    me = lax.axis_index("gx") * ny + lax.axis_index("gy")
    flat = rows_of((ny, 128)) == lanes_of((ny, 128))
    for x in range(nx):
        mine = jnp.where(lanes_of((ny, 128)) == me, grid[x], 0.0)
        mine = jnp.broadcast_to(jnp.sum(mine, axis=1, keepdims=True), (ny, 128))
        row = jnp.sum(jnp.where(flat, mine, 0.0), axis=0, keepdims=True)
        heat[0, x : x + 1, :] = row[:, :ny]


def leave(in_u, in_v, new_u, new_v):
    to_tiles(in_u, new_u)
    to_tiles(in_v, new_v)


def exchange(value):
    return lax.all_to_all(value, ("gx", "gy"), split_axis=0, concat_axis=0, tiled=True)


VMEM_BYTES = 28 * 1024 * 1024


def call(kernel, outs, scratch, operands, in_hbm=(), name=None):
    specs = [
        pl.BlockSpec(memory_space=pltpu.HBM if n in in_hbm else pltpu.VMEM)
        for n in range(len(operands))
    ]
    return pl.pallas_call(
        kernel,
        out_shape=[
            jax.ShapeDtypeStruct(*(out if isinstance(out[1], type) else (out, jnp.float32)))
            for out in outs
        ],
        in_specs=specs,
        out_specs=[pl.BlockSpec(memory_space=pltpu.VMEM)] * len(outs),
        scratch_shapes=scratch,
        compiler_params=pltpu.CompilerParams(
            vmem_limit_bytes=VMEM_BYTES,
        ),
        name=name,
    )(*operands)


def stencil_steps(displacement, velocity, noise, electron_temp, pair_list, pair_count):
    across = (lax.axis_size("gx"), lax.axis_size("gy"))
    owners = across[0] * across[1]

    def vmem(*shape):
        return pltpu.VMEM(shape, jnp.float32)

    tiles = (3, BXT, TZ, BYT, TILE)
    placed_u = jnp.swapaxes(displacement, 2, 3)
    placed_v = jnp.swapaxes(velocity, 2, 3)
    placed_noise = jnp.swapaxes(noise, 3, 4)
    slots = pair_list.shape[-1]
    first, two, three = Chunk(owners, 2, True), Chunk(owners, 2), Chunk(owners, 3)
    send, own_u, live, kept_heat, kept_count, own_v, near_noise = call(
        partial(prepare, across, first),
        [
            (owners, 1, 128 * first.rows),
            (72, 128),
            (8, 128),
            electron_temp.shape,
            ((8, 128), jnp.int32),
            placed_v.shape,
            placed_noise.shape,
        ],
        [
            pltpu.VMEM((8, (slots + 127) // 128 * 128), jnp.int32),
            vmem(*tiles),
            vmem(*electron_temp.shape),
            pltpu.VMEM(pair_list.shape, jnp.int32),
            pltpu.SMEM(pair_count.shape, jnp.int32),
            vmem(4 * 16, 128),
            pltpu.SemaphoreType.DMA((6,)),
        ],
        (
            placed_u,
            pltpu.with_memory_space_constraint(electron_temp, pltpu.HBM),
            pair_list,
            pair_count,
            placed_v,
            placed_noise,
        ),
        in_hbm=(0, 1, 2, 3, 4, 5),
        name="prepare",
    )
    near, far = grouped(NEAR), grouped(NEAR + FAR)
    plan = [
        (first, two, near, 1.0),
        (two, three, near, NEAR_LIMIT),
        (three, three, far, FAR_LIMIT),
        (three, None, far, FAR_LIMIT),
    ]
    masks = grid = bad = None
    for step, (arriving, leaving, groups, limit) in enumerate(plan):
        recv = exchange(send)
        last = leaving is None
        pairs = sum(len(dxs) for _, dxs in groups)
        outs = [
            (owners, 128) if last else (owners, 1, 128 * leaving.rows),
            (owners, 128),
            (8, 128),
            (72, 128),
            (72, 128),
        ]
        scratch = [
            vmem(3 * SIZE + PAD, 128),
            vmem(len(groups) * 3 * SIZE, 128),
            vmem(SIZE, 128),
            vmem(len(groups) * SIZE, 128),
            vmem(24 * pairs, 128),
            vmem(24 * pairs, 128),
            vmem(9 * 16 + 2 * PAD, 128),
            vmem(2 * owners, 128),
            vmem(72, 128),
            vmem(72, 128),
            vmem(4 * 16, 128),
            vmem(3 * SIZE, 128),
            vmem(8 * 5 * 7, 128),
        ]
        if step == 0:
            outs.append((MASKS * SIZE, 128))
            scratch += [vmem(128, 128), vmem(512, 128), vmem(27 * 16, 128)]
            operands = (recv, own_u, own_v, near_noise, live)
        else:
            operands = (recv, own_u, own_v, near_noise, masks, grid, bad)
        got = call(
            partial(step_kernel, step, across, arriving, leaving, groups, limit),
            outs,
            scratch,
            operands,
            name=f"step{step}",
        )
        send, grid, bad, own_u, own_v = got[:5]
        if step == 0:
            masks = got[5]
    recv = exchange(send)
    new_u, new_v = call(leave, [tiles, tiles], [], (own_u, own_v), name="leave")
    (heat,) = call(partial(finish, across), [electron_temp.shape], [], (recv, grid), name="finish")
    kept = (kept_heat, kept_count[:1, :1])
    return bad[0, 0], kept, jnp.swapaxes(new_u, 2, 3), jnp.swapaxes(new_v, 2, 3), heat


def per_device(displacement, velocity, noise, electron_temp, pair_list, pair_count):
    given = (displacement, velocity, noise, electron_temp, pair_list, pair_count)
    bad, (kept_heat, kept_count), new_u, new_v, heat = stencil_steps(*given)
    given = (displacement, velocity, noise, kept_heat, pair_list, kept_count)
    return lax.cond(bad > 0.5, lambda: whole_sweep(*given), lambda: (new_u, new_v, heat))


def solution(mesh):
    placed = (
        P(None, "gx", "gy", None, None),
        P(None, "gx", "gy", None, None),
        P(None, None, "gx", "gy", None, None),
        P(("gx", "gy"), None, None),
        P("gx", "gy", None, None),
        P("gx", "gy"),
    )
    return jax.shard_map(
        per_device,
        mesh=mesh,
        in_specs=placed,
        out_specs=(
            P(None, "gx", "gy", None, None),
            P(None, "gx", "gy", None, None),
            P(("gx", "gy"), None, None),
        ),
        check_vma=False,
    )
```

```python
from functools import partial

import jax
import jax.numpy as jnp
from jax import lax
from jax.experimental import pallas as pl
from jax.experimental.pallas import tpu as pltpu
from jax.sharding import PartitionSpec as P

CB = 4
TILE = 128
BXT = 2
BYT = 2
TZ = 3
TILES = 12
STEPS = 4
SUB = 6


lattice_edge = 3.1652
density_cut = 4.400224
embed_scale = 1.896373
pair_cut = 3.25
coef_zero = 47.1346499
coef_one = -33.7665655
coef_two = 6.2541999
time_step = 0.005
atom_mass = 0.0190534
friction = 1.0
heat_capacity = 0.02
diffusion_rate = 0.12


def padded_2(block, sides, width):
    for axis, dim in sides:
        count = lax.axis_size(axis)
        forward = [(i, i + 1) for i in range(count - 1)]
        forward.append((count - 1, 0))
        backward = [(target, source) for source, target in forward]
        low = lax.ppermute(
            lax.slice_in_dim(block, block.shape[dim] - width, None, axis=dim), axis, forward
        )
        high = lax.ppermute(lax.slice_in_dim(block, 0, width, axis=dim), axis, backward)
        block = jnp.concatenate([low, block, high], axis=dim)
    return block


def lattice_sites():
    serial = jnp.arange(TILE, dtype=jnp.int32)
    cell_number = serial // 2
    half_step = (serial % 2).astype(jnp.float32) * 0.5
    corners = jnp.stack([cell_number // (CB * CB), cell_number // CB % CB, cell_number % CB])
    return lattice_edge * (corners.astype(jnp.float32) + half_step[None, :])


def plane_table(plane_total):
    serial = jnp.arange(TILE, dtype=jnp.int32)
    cell_number = serial // 2
    layer = 2 * (cell_number % CB) + serial % 2
    tiles = jnp.arange(TZ, dtype=jnp.int32)
    whole = tiles[:, None] * (2 * CB) + layer[None, :]
    return whole * plane_total // (2 * CB * TZ)


def pair_geometry(window, tile_index, neighbour_code, lattice):
    wide_y = BYT + 2
    depth_t = tile_index % TZ
    inner_y = tile_index // TZ % BYT
    inner_x = tile_index // (TZ * BYT)
    shift_x = neighbour_code // 9
    shift_y = neighbour_code // 3 % 3
    shift_z = neighbour_code % 3
    flattened = window.reshape(window.shape[0], (BXT + 2) * wide_y * TZ, TILE)
    own_index = ((inner_x + 1) * wide_y + inner_y + 1) * TZ + depth_t
    other_index = ((inner_x + shift_x) * wide_y + inner_y + shift_y) * TZ + (
        depth_t + shift_z - 1 + TZ
    ) % TZ
    own_tile = lax.dynamic_index_in_dim(flattened, own_index, 1, keepdims=False)
    other_tile = lax.dynamic_index_in_dim(flattened, other_index, 1, keepdims=False)
    offset = jnp.stack([shift_x - 1, shift_y - 1, shift_z - 1]).astype(jnp.float32) * (
        CB * lattice_edge
    )
    left = lattice + own_tile
    right = lattice + other_tile + offset[:, None]
    delta = left[:, :, None] - right[:, None, :]
    square = jnp.sum(delta * delta, axis=0)
    serial = jnp.arange(TILE, dtype=jnp.int32)
    same_atom = (neighbour_code == 13) & (serial[:, None] == serial[None, :])
    distance = jnp.sqrt(jnp.where(same_atom, 100.0, square))
    return (delta, distance, own_index, other_index)


def density_term(window, lattice, tile_index, neighbour_code):
    delta, distance, own_index, other_index = pair_geometry(
        window, tile_index, neighbour_code, lattice
    )
    dens_gap = distance - density_cut
    return jnp.sum(jnp.where(distance < density_cut, dens_gap * dens_gap, 0.0), axis=1)[None]


def force_term(window, embed_window, lattice, tile_index, neighbour_code):
    delta, distance, own_index, other_index = pair_geometry(
        window, tile_index, neighbour_code, lattice
    )
    flat_embed = embed_window.reshape((BXT + 2) * (BYT + 2) * TZ, TILE)
    own_embed = lax.dynamic_index_in_dim(flat_embed, own_index, 0, keepdims=False)
    other_embed = lax.dynamic_index_in_dim(flat_embed, other_index, 0, keepdims=False)
    pair_gap = distance - pair_cut
    poly = coef_zero + coef_one * distance + coef_two * distance * distance
    pair_slope = jnp.where(
        distance < pair_cut,
        2.0 * pair_gap * poly + pair_gap * pair_gap * (coef_one + 2.0 * coef_two * distance),
        0.0,
    )
    dens_gap = distance - density_cut
    dens_slope = jnp.where(distance < density_cut, 2.0 * dens_gap, 0.0)
    scalar = (pair_slope + (own_embed[:, None] + other_embed[None, :]) * dens_slope) / distance
    return -jnp.sum(scalar[None] * delta, axis=2)


def sweep_pairs(term_fn, channels, pair_table, pair_total):
    initial = jnp.zeros((channels, TILES, TILE), jnp.float32)

    def block_add(block_index, running):
        start = block_index * 27
        chosen = lax.dynamic_slice_in_dim(pair_table, start, 27, 1)
        live = start + jnp.arange(27, dtype=jnp.int32) < pair_total
        terms = jax.vmap(term_fn)(chosen[0], chosen[1])
        terms = jnp.where(live[:, None, None], terms, 0.0)
        return running.at[:, chosen[0]].add(jnp.swapaxes(terms, 0, 1))

    blocks = (pair_total + 26) // 27
    total = lax.fori_loop(0, blocks, block_add, initial)
    return total.reshape(channels, BXT, BYT, TZ, TILE)


def relax_slab(padded):
    center = padded[1:-1]
    beside_all = padded[2:] + padded[:-2] + jnp.roll(center, 1, 1) + jnp.roll(center, -1, 1)
    beside_all = beside_all + jnp.roll(center, 1, 2) + jnp.roll(center, -1, 2)
    return center + diffusion_rate * (beside_all - 6.0 * center)


def one_step(lattice, pair_table, pair_total, planes, owners, across, carry, noise_now):
    positions, speeds, heat_field = carry
    slab_depth = heat_field.shape[0]
    plane_total = slab_depth * owners
    arrived = lax.all_to_all(
        heat_field.reshape(slab_depth, owners), ("gx", "gy"), split_axis=1, concat_axis=0, tiled=True
    )
    column = arrived.reshape(-1)
    column_temp = jnp.take(column, planes).reshape(TZ, TILE)
    local_temp = jnp.broadcast_to(column_temp, (BXT, BYT, TZ, TILE))
    window = padded_2(positions, (("gx", 1), ("gy", 2)), 1)
    density = sweep_pairs(partial(density_term, window, lattice), 1, pair_table, pair_total)
    embed_slope = -embed_scale / (2.0 * jnp.sqrt(density))
    embed_window = padded_2(embed_slope, (("gx", 1), ("gy", 2)), 1)
    force = sweep_pairs(partial(force_term, window, embed_window, lattice), 3, pair_table, pair_total)
    kicker = jnp.sqrt(2.0 * friction * atom_mass * local_temp / time_step)[None] * noise_now
    speeds = speeds + time_step / atom_mass * (force - friction * atom_mass * speeds + kicker)
    positions = positions + time_step * speeds
    power = friction * atom_mass * time_step * jnp.sum(speeds * speeds, axis=0)
    tile_power = jnp.sum(power, axis=(0, 1)).reshape(-1)
    energy = jnp.zeros((plane_total,), jnp.float32).at[planes].add(tile_power)
    arrived = lax.all_to_all(
        energy.reshape(plane_total, 1), ("gx", "gy"), split_axis=0, concat_axis=1, tiled=True
    )
    heat_field = heat_field + arrived.reshape(slab_depth, *across) / heat_capacity

    def relax(sub_index, heat):
        return relax_slab(padded_2(heat, ((("gx", "gy"), 0),), 1))

    heat_field = lax.fori_loop(0, SUB, relax, heat_field)
    return (positions, speeds, heat_field)


def whole_sweep(displacement, velocity, noise, electron_temp, pair_list, pair_count):
    across = (lax.axis_size("gx"), lax.axis_size("gy"))
    owners = across[0] * across[1]
    planes = plane_table(electron_temp.shape[0] * owners).reshape(-1)
    step = partial(
        one_step, lattice_sites(), pair_list[0, 0], pair_count[0, 0], planes, owners, across
    )
    return lax.fori_loop(
        0,
        STEPS,
        lambda n, carry: step(carry, lax.dynamic_index_in_dim(noise, n, 0, keepdims=False)),
        (displacement, velocity, electron_temp),
    )


NEAR_SHELLS = (3, 4, 8)
FAR_SHELLS = (11, 12)
NEAR_LIMIT = 0.2900
FAR_LIMIT = 0.8170
HALF = 0.5 * lattice_edge
FAR_AWAY = 1.0e6
ROWS = 20
BASE = 2
SIZE = TZ * ROWS
EDGES = (2, 3)


def site_offsets(shells):
    span = range(-3, 4)
    found = []
    for x in span:
        for y in span:
            for z in span:
                if x % 2 == y % 2 == z % 2 and x * x + y * y + z * z in shells:
                    found.append((x, y, z))
    return found


def grouped(offsets):
    table = {}
    for x, y, z in offsets:
        table.setdefault((y, z), []).append(x)
    return sorted(table.items())


NEAR = site_offsets(NEAR_SHELLS)
FAR = site_offsets(FAR_SHELLS)
MASK_SLOT = {offset: slot for slot, offset in enumerate(NEAR + FAR)}
MASKS = len(MASK_SLOT)


def by_x(groups):
    table = {}
    for n, ((dy, dz), dxs) in enumerate(groups):
        for dx in dxs:
            table.setdefault(dx, []).append((n, dy, dz))
    return sorted(table.items())


def sign(value):
    return (value > 0) - (value < 0)


def lanes_of(shape=(8, 128)):
    return lax.broadcasted_iota(jnp.int32, shape, len(shape) - 1)


def rows_of(shape=(8, 128)):
    return lax.broadcasted_iota(jnp.int32, shape, len(shape) - 2)


def turn(value, amount):
    amount = (-amount) % 128
    return value if amount == 0 else pltpu.roll(value, amount, value.ndim - 1)


def pick_lanes(value, index):
    return jnp.take_along_axis(value, index, axis=1, mode="promise_in_bounds")


class Chunk:
    def __init__(self, owners, cells, first=False):
        self.cells = cells
        self.narrow = owners <= 32
        halo = 9 if cells == 2 else 14
        if self.narrow:
            self.tail = 9 if cells == 2 else 13
            self.tail_lane = 96
            self.reach = (self.tail, 64)
            self.rows = self.tail + 1
        else:
            self.tail = halo
            self.tail_lane = 0
            self.reach = (halo + 1, 64)
            self.rows = halo + 2
        if first:
            self.live = [(self.reach[0], 0), (self.rows, 0), (self.rows, 64)]
            self.rows += 1

    def x_home(self, plane, row):
        if plane < 8:
            return self.cells * (plane // 2) + row, plane % 2
        return 4 * self.cells + row // 2, row % 2


def repeat_tail(value, chunk):
    if not chunk.narrow:
        return value
    return pick_lanes(value, 96 + lanes_of(value.shape) % 32)


def from_tiles(read, out):
    lane = lanes_of((TZ, 128))
    own = (lane >= 32) & (lane < 96)
    for c in range(3):
        for ix in range(BXT):
            first, second = [read(c, ix, iy) for iy in range(BYT)]
            for cx in range(CB):
                both = jnp.where(lane < 64, turn(first, 32 * cx - 32), turn(second, 32 * cx - 64))
                start = c * TZ * 8 + CB * ix + cx
                out[pl.ds(start, TZ, stride=8), :] = jnp.where(own, both, 0.0)


def to_tiles(source, out):
    lane = lanes_of((TZ, 128))
    for c in range(3):
        for ix in range(BXT):
            rows = [source[pl.ds(c * TZ * 8 + CB * ix + cx, TZ, stride=8), :] for cx in range(CB)]
            for iy in range(BYT):
                value = None
                for cx in range(CB):
                    piece = turn(rows[cx], 32 + 32 * iy - 32 * cx)
                    value = piece if value is None else jnp.where(lane >= 32 * cx, piece, value)
                out[c, ix, :, iy, :] = value


def each(count, body):
    if count <= 32:
        for index in range(count):
            body(index, 0)
    else:
        lax.fori_loop(0, count, body, 0, unroll=8)


def stage_halo(own, stage, chunk, tail_row, extras):
    w = chunk.cells
    lane, row = lanes_of(), rows_of()
    kinds = {}
    depth = stage.shape[0] // 4
    low = lane < 64
    third = [pick for pick in range(5)] if w == 3 else []
    for kind, (axis, side) in enumerate((("x", -1), ("x", 1), ("y", -1), ("y", 1))):
        at = kind * depth
        kinds[(axis, side)] = at
        if axis == "x":
            first = 8 - w if side == 1 else 0
            for pair in range(4):
                both = jnp.where(low, turn(own(2 * pair), 32), turn(own(2 * pair + 1), -32))
                stage[at + w * pair : at + w * pair + w, :] = both[first : first + w]
            last = own(8)
            a, b = turn(last, 32), turn(last, -32)
            low1 = lanes_of((1, 128)) < 64
            stage[at + 4 * w : at + 4 * w + 1, :] = jnp.where(
                low1, a[first : first + 1], b[first + 1 : first + 2]
            )
            if w == 3:
                stage[at + 13 : at + 14, :] = a[first + 2 : first + 3]
        else:
            start = 80 if side == 1 else 32
            packed = None
            for plane in range(8):
                piece = turn(own(plane), start - 16 * plane)
                packed = piece if packed is None else jnp.where(lane >= 16 * plane, piece, packed)
            stage[at : at + 8, :] = packed
            flat = pick_lanes(own(8), start + lane % 16)
            flat = jnp.where(lane // 16 == row, flat, 0.0)
            stage[at + 8 : at + 9, :] = jnp.sum(flat, axis=0, keepdims=True)
            start = 72 if side == 1 else 48
            for pair in third:
                flat = pick_lanes(own(2 * pair), start + lane % 8)
                if pair < 4:
                    flat = jnp.where(low, flat, pick_lanes(own(2 * pair + 1), start + lane % 8))
                flat = jnp.where(lane % 64 // 8 == row, flat, 0.0)
                stage[at + 9 + pair : at + 10 + pair, :] = jnp.sum(flat, axis=0, keepdims=True)
        for (where, lane_from, lane_to), value in tail_row + extras.get((axis, side), []):
            lane1 = lanes_of((1, 128))
            old = stage[at + where : at + where + 1, :]
            here = (lane1 >= lane_from) & (lane1 < lane_to)
            stage[at + where : at + where + 1, :] = jnp.where(here, value, old)
    return kinds


def send_chunks(stage, kinds, send_ref, chunk, ids, owners):
    tails = sorted({chunk.tail, chunk.reach[0]})
    at = kinds[("x", 1)]
    rows = {where: stage[at + where : at + where + 1, :] for where in tails}

    for (sx, sy), ident in ids.items():
        if (sx, sy) == (0, 0):
            continue
        at = kinds[("y", sy)] if sy else kinds[("x", sx)]
        for k in range(chunk.rows):
            if k not in tails:
                send_ref[ident, :, 128 * k : 128 * k + 128] = stage[at + k : at + k + 1, :]

    def fill(index, carry):
        for where in tails:
            send_ref[index, :, 128 * where : 128 * where + 128] = rows[where]
        return carry

    each(owners, fill)
    for (sx, sy), ident in ids.items():
        if (sx, sy) == (0, 0):
            continue
        at = kinds[("y", sy)] if sy else kinds[("x", sx)]
        for k in tails:
            send_ref[ident, :, 128 * k : 128 * k + 128] = stage[at + k : at + k + 1, :]


def receive_chunks(recv_ref, landed, tails_at, chunk, ids, owners):
    depth = (landed.shape[0] - 2 * PAD) // 9
    homes = {}
    for n, ((sx, sy), ident) in enumerate(ids.items()):
        if (sx, sy) == (0, 0):
            continue
        homes[(sx, sy)] = PAD + n * depth
        for k in range(chunk.rows):
            landed[PAD + n * depth + k : PAD + n * depth + k + 1, :] = recv_ref[ident, :, 128 * k : 128 * k + 128]

    tails = sorted({chunk.tail, chunk.reach[0]})

    def take(index, carry):
        for n, where in enumerate(tails):
            tails_at[pl.ds(n * owners + index, 1), :] = recv_ref[index, :, 128 * where : 128 * where + 128]
        return carry

    each(owners, take)
    return homes


PAD = 8


def build_window(own, landed, homes, window, chunk, origin):
    w = chunk.cells
    lane, row = lanes_of(), rows_of()
    zero = jnp.zeros((8, 128), jnp.float32)
    middle = (lane >= 32) & (lane < 96)
    first_rows = row < 4

    def outer(start, size, sy):
        values = [landed[homes[(sx, sy)] + start : homes[(sx, sy)] + start + size, :] for sx in (1, -1)]
        if size == 1:
            values = [jnp.broadcast_to(value, (8, 128)) for value in values]
        return jnp.where(first_rows, values[0], values[1])

    def inner(start, size, sy):
        value = landed[homes[(0, sy)] + start : homes[(0, sy)] + start + size, :]
        return jnp.broadcast_to(value, (8, 128))

    sides = (-1, 1)
    packed = {(sy, out): (outer if out else inner)(0, 8, sy) for sy in sides for out in (0, 1)}
    for plane in range(9):
        at = plane * ROWS + BASE
        parts = [own(plane), zero]
        for sy in sides:
            target = 16 if sy == -1 else 96
            here = (lane >= target) & (lane < target + 16)
            beyond = 8 if sy == -1 else 112
            here_third = (lane >= beyond) & (lane < beyond + 8)
            for out in (0, 1):
                if plane < 8:
                    piece = turn(packed[(sy, out)], 16 * plane - target)
                else:
                    wide = (outer if out else inner)(8, 1, sy)
                    piece = pick_lanes(wide, 16 * row + lane % 16)
                parts[out] = jnp.where(here, piece, parts[out])
                if w == 3:
                    wide = (outer if out else inner)(9 + plane // 2, 1, sy)
                    piece = pick_lanes(wide, 64 * (plane % 2) + 8 * row + lane % 8)
                    parts[out] = jnp.where(here_third, piece, parts[out])
        centre, rim = parts
        if plane < 8:
            home, half = chunk.x_home(plane, 0)
            back = -32 if half == 0 else 32
            behind = landed[pl.ds(origin + homes[(1, 0)] + home, 8), :]
            ahead = landed[pl.ds(origin + homes[(-1, 0)] + home - (4 - w) - 4, 8), :]
            piece = turn(jnp.where(first_rows, behind, ahead), back)
            rim = jnp.where(middle & ((row < w) | (row >= 8 - w)), piece, rim)
        else:
            for k in range(w):
                home, half = chunk.x_home(plane, k)
                back = -32 if half == 0 else 32
                for sx, to in ((1, k), (-1, 8 - w + k)):
                    base = homes[(sx, 0)] + home
                    piece = turn(jnp.broadcast_to(landed[base : base + 1, :], (8, 128)), back)
                    rim = jnp.where(middle & (row == to), piece, rim)
        window[pl.ds(origin + at, 8), :] = pltpu.roll(rim, 4, 0)
        window[pl.ds(origin + at + 12, 8), :] = rim
        window[pl.ds(origin + at + 4, 8), :] = centre


def mix_planes(count, source, mixed, origin):
    even = lanes_of((16, 128)) % 2 == 0
    for plane in range(count * TZ):
        at = plane * ROWS + BASE
        here = source[pl.ds(origin + at, 16), :]
        after = turn(source[pl.ds(origin + at + 1, 16), :], 8)
        mixed[pl.ds(origin + at, 16), :] = jnp.where(even, after, here)


def sources(dy, dz, use_mixed):
    s = sign(dz)
    low = dy // 2
    if dy % 2 == 0 or use_mixed:
        out = [(None, 0, dz + 8 * low, 0)]
        if s:
            out.append((None, s, dz - 8 * s + 8 * low, 0))
        return out
    out = [(0, 0, dz + 8 * low, 0), (1, 0, dz + 8 * (low + 1), 1)]
    for parity, k in ((0, low), (1, low + 1)):
        if any(not 0 <= iz + dz < 8 for iz in range(parity, 8, 2)):
            out.append((parity, s, dz - 8 * s + 8 * k, parity))
    return out


def shift_planes(count, source, mixed, out, groups, constants, origin, ready=None):
    half_layer = lanes_of((16, 128)) % 8
    parity = half_layer % 2
    slots = {key: n for n, (key, _) in enumerate(groups)}
    planes = [(c, t) for c in range(count) for t in range(TZ)]
    for dz in sorted({key[1] for key in slots}, key=lambda z: (z % 2, abs(z))):
        dys = sorted((key[0] for key in slots if key[1] == dz), key=abs)
        carried = (half_layer + dz >= 8) | (half_layer + dz < 0)
        ref = mixed if dz % 2 and mixed is not None else source
        turned = {}

        def taken(c, t, shift, down):
            key = (c, t, shift, down)
            if key not in turned:
                at = (c * TZ + t) * ROWS + BASE + down
                turned[key] = turn(ref[pl.ds(origin + at, 16), :], shift)
            return turned[key]

        for dy in dys:
            parts = sources(dy, dz, mixed is not None)
            for want, carry_z, shift, down in parts:
                for c, t in planes:
                    taken(c, t, shift, down)
            for c, t in planes:
                value = None
                for want, carry_z, shift, down in parts:
                    piece = taken(c, (t + carry_z) % TZ, shift, down)
                    if value is None:
                        value = piece
                        continue
                    here = None
                    if want is not None:
                        here = parity == want
                    if carry_z:
                        here = carried if here is None else here & carried
                    value = jnp.where(here, piece, value)
                shift_by = constants(c, dy, dz)
                if shift_by:
                    value = value + shift_by
                at = slots[(dy, dz)] * count * SIZE + (c * TZ + t) * ROWS + BASE
                out[pl.ds(origin + at, 16), :] = value
            if ready is not None:
                ready(slots[(dy, dz)], dy, dz)


def coordinate_shift(c, dy, dz):
    return (0.0, HALF * dy, HALF * dz)[c]


def no_shift(c, dy, dz):
    return 0.0


def row_start(dx):
    return dx // 2 if dx % 2 == 0 else (dx - 1) // 2


class DensitySweep:
    def __init__(self, window, moved, masks_ref, gaps, inverses, starts, groups, origin):
        self.refs = (window, moved, masks_ref, gaps, inverses, starts)
        self.groups = dict(groups)
        self.targets = []
        for t in range(TZ):
            self.targets.append((self.own_rows(origin, t * ROWS + BASE + 4), 8 * t, 8))
        for edge in EDGES:
            self.targets.append((self.edge_rows(origin, BASE + edge), None, 2 * TZ))
        self.xs = sorted({dx for dxs in self.groups.values() for dx in dxs})
        self.totals = [jnp.zeros((height, 128), jnp.float32) for _, _, height in self.targets]
        self.own = []
        for k, (rows, _, height) in enumerate(self.targets):
            self.own.append([window[rows(c * SIZE), :] for c in (1, 2)])
            own_x = window[rows(0), :]
            for j, dx in enumerate(self.xs):
                at = 8 * (k * len(self.xs) + j)
                starts[at : at + height, :] = own_x - HALF * dx

    @staticmethod
    def own_rows(origin, start):
        return lambda base: pl.ds(origin + (base + start), 8)

    @staticmethod
    def edge_rows(origin, start):
        return lambda base: pl.ds(origin + (base + start), 2 * TZ, stride=ROWS // 2)

    def part(self, n, dy, dz):
        window, moved, masks_ref, gaps, inverses, starts = self.refs
        for dx in self.groups[(dy, dz)]:
            down = row_start(dx)
            slot = MASK_SLOT[(dx, dy, dz)]
            for k, (rows, keep, height) in enumerate(self.targets):
                other = [moved[rows((3 * n + c) * SIZE + down), :] for c in range(3)]
                at = 8 * (k * len(self.xs) + self.xs.index(dx))
                ex = starts[at : at + height, :] - other[0]
                ey = self.own[k][0] - other[1]
                ez = self.own[k][1] - other[2]
                square = ex * ex + ey * ey + (ez * ez + masks_ref[rows(slot * SIZE), :])
                inverse = lax.rsqrt(square)
                gap = jnp.minimum(square * inverse - density_cut, 0.0)
                self.totals[k] = self.totals[k] + gap * gap
                if keep is not None:
                    gaps[keep + 24 * slot : keep + 24 * slot + 8, :] = gap
                    inverses[keep + 24 * slot : keep + 24 * slot + 8, :] = inverse

    def finish(self, slope):
        for total, (rows, _, _) in zip(self.totals, self.targets):
            slope[rows(0), :] = -embed_scale * lax.rsqrt(total)


class ForceSweep:
    def __init__(self, window, moved, slope, slope_moved, gaps, inverses, groups, origin):
        self.refs = (window, moved, slope_moved, gaps, inverses)
        self.groups = dict(groups)
        self.origin = origin
        self.slopes = [slope[pl.ds(origin + self.at(t), 8), :] for t in range(TZ)]
        self.others = [[None] * 3 for _ in range(TZ)]
        self.weights = [{} for _ in range(TZ)]

    @staticmethod
    def at(t):
        return t * ROWS + BASE + 4

    def part(self, n, dy, dz):
        window, moved, slope_moved, gaps, inverses = self.refs
        first = 2.0 * (coef_zero + coef_one * pair_cut + coef_two * pair_cut * pair_cut)
        second = 3.0 * (coef_one + 2.0 * coef_two * pair_cut)
        third = 4.0 * coef_two
        for dx in self.groups[(dy, dz)]:
            down = row_start(dx)
            slot = MASK_SLOT[(dx, dy, dz)]
            for t in range(TZ):
                row = self.at(t) + down
                other_slope = slope_moved[pl.ds(self.origin + (n * SIZE + row), 8), :]
                gap = gaps[24 * slot + 8 * t : 24 * slot + 8 * t + 8, :]
                inverse = inverses[24 * slot + 8 * t : 24 * slot + 8 * t + 8, :]
                near = jnp.minimum(gap + (density_cut - pair_cut), 0.0)
                scalar = (self.slopes[t] + other_slope) * gap
                scalar = scalar + near * (first + near * (second + third * near))
                scalar = scalar * inverse
                known = self.weights[t].get(dx)
                self.weights[t][dx] = scalar if known is None else known + scalar
                for c in range(3):
                    other = moved[pl.ds(self.origin + ((3 * n + c) * SIZE + row), 8), :]
                    known = self.others[t][c]
                    self.others[t][c] = scalar * other if known is None else known + scalar * other

    def finish(self, t):
        window = self.refs[0]
        total = list(self.others[t])
        weight = None
        for dx, value in sorted(self.weights[t].items()):
            weight = value if weight is None else weight + value
            if dx:
                total[0] = total[0] + (HALF * dx) * value
        own = [window[pl.ds(self.origin + (c * SIZE + self.at(t)), 8), :] for c in range(3)]
        return [total[c] - own[c] * weight for c in range(3)]


def binomial(n, k):
    value = 1
    for j in range(k):
        value = value * (n - j) // (j + 1)
    return value


def diffuse_grid(grid, across):
    nx, ny = across
    d = diffusion_rate
    pairs = [
        [heat] + [pltpu.roll(heat, k, 1) + pltpu.roll(heat, 128 - k, 1) for k in range(1, SUB + 1)]
        for heat in grid
    ]

    def powers(x, k):
        total = None
        for j in range(k // 2 + 1):
            weight = binomial(k, j) * binomial(SUB, k) * d**k
            term = weight * pairs[x][k - 2 * j]
            total = term if total is None else total + term
        return total

    result = [powers(x, 0) for x in range(nx)]
    for k in range(1, SUB + 1):
        columns = []
        for x in range(nx):
            heat = result[x]
            beside = result[(x + 1) % nx] + result[(x - 1) % nx]
            beside = beside + pltpu.roll(heat, 1, 0) + pltpu.roll(heat, ny - 1, 0)
            columns.append(((1.0 - 6.0 * d) * heat + powers(x, k)) + d * beside)
        result = columns
    return result


LAYERS = 2 * CB * TZ


def temperatures_by_layer(column, plane_total):
    layer = 2 * CB * rows_of() + lanes_of() % (2 * CB)
    layer = jnp.minimum(layer, LAYERS - 1)
    return pick_lanes(jnp.broadcast_to(column, (8, 128)), layer * plane_total // LAYERS)


def energies_by_plane(power, plane_total):
    row, lane = rows_of(), lanes_of()
    stacked = jnp.zeros((8, 128), jnp.float32)
    for t in range(TZ):
        stacked = jnp.where(row == t, power[t], stacked)
    plane = lane % plane_total
    start = (plane * LAYERS + plane_total - 1) // plane_total
    total = jnp.zeros((8, 128), jnp.float32)
    for extra in range(max(1, -(-LAYERS // plane_total))):
        layer = start + extra
        inside = layer - 2 * CB * row
        here = (inside >= 0) & (inside < 2 * CB) & (layer < LAYERS)
        here = here & (layer * plane_total // LAYERS == plane)
        first = 32 + jnp.clip(inside, 0, 2 * CB - 1)
        taken = [pick_lanes(stacked, first + 8 * y) for y in range(BYT * CB)]
        while len(taken) > 1:
            taken = [a + b for a, b in zip(taken[::2], taken[1::2])]
        total = total + jnp.where(here, taken[0], 0.0)
    return jnp.sum(total, axis=0, keepdims=True)


def neighbour_ids(across):
    nx, ny = across
    bx, by = lax.axis_index("gx"), lax.axis_index("gy")
    at_x = {-1: jnp.where(bx == 0, nx - 1, bx - 1), 0: bx, 1: jnp.where(bx == nx - 1, 0, bx + 1)}
    at_y = {-1: jnp.where(by == 0, ny - 1, by - 1), 0: by, 1: jnp.where(by == ny - 1, 0, by + 1)}
    return {(sx, sy): at_x[sx] * ny + at_y[sy] for sx in (-1, 0, 1) for sy in (-1, 0, 1)}


def prepare(across, chunk, disp, heat, pairs, count, vel, noise, send, own_u, live, kept_heat, kept_count, near_vel, near_noise, lists, disp_in, heat_in, pairs_in, count_in, stage, sems):
    nx, ny = across
    owners = nx * ny
    copies = [
        pltpu.make_async_copy(source, target, sems.at[n])
        for n, (source, target) in enumerate(
            ((disp, disp_in), (heat, heat_in), (pairs, pairs_in), (count, count_in))
        )
    ]
    later = [
        pltpu.make_async_copy(vel, near_vel, sems.at[4]),
        pltpu.make_async_copy(noise, near_noise, sems.at[5]),
    ]
    for copy in copies + later:
        copy.start()
    lists[...] = jnp.full(lists.shape, -1, jnp.int32)
    for copy in copies:
        copy.wait()

    from_tiles(lambda c, ix, iy: disp_in[c, ix, :, iy, :], own_u)
    kept_heat[...] = heat_in[...]
    kept_count[...] = jnp.full((8, 128), count_in[0, 0], jnp.int32)

    slots = pairs_in.shape[3]
    width = lists.shape[1]
    lists[0:2, 0:slots] = pairs_in[0, 0]
    tile = lists[0:1, :]
    code = lists[1:2, :]
    valid = (lanes_of((1, width)) < count_in[0, 0]) & (tile >= 0)
    column = jnp.where(tile >= 3, 1, 0) + jnp.where(tile >= 6, 1, 0) + jnp.where(tile >= 9, 1, 0)
    depth = jnp.where(valid, tile - 3 * column, -1)
    place = 32 * column + code
    left = jnp.where(rows_of((8, width)) == depth, 1.0, 0.0)
    right = jnp.where(rows_of((128, width)) == place, 1.0, 0.0)
    found = lax.dot_general(
        left, right, (((1,), (1,)), ((), ())), preferred_element_type=jnp.float32
    )
    live[...] = found

    lane_n = lanes_of((nx, 128))
    planes = jnp.zeros((nx, 128), jnp.float32)
    for y in range(ny):
        value = jnp.broadcast_to(heat_in[0, :, y : y + 1], (nx, 128))
        planes = jnp.where(lane_n % ny == y, value, planes)
    planes = jnp.where(lane_n % owners // ny == rows_of((nx, 128)), planes, 0.0)
    field = jnp.sum(planes, axis=0, keepdims=True)

    lane = lanes_of()
    halves = {
        ("x", -1): found,
        ("x", 1): turn(found, 64),
        ("y", -1): jnp.where(lane < 32, found, turn(found, 32)),
        ("y", 1): jnp.where(lane < 32, turn(found, 32), turn(found, 64)),
    }
    extras = {}
    for key, value in halves.items():
        extras[key] = [
            ((where, to, to + 64), value[t : t + 1] if to == 0 else turn(value, -64)[t : t + 1])
            for t, (where, to) in enumerate(chunk.live)
        ]
    kinds = stage_halo(
        lambda plane: own_u[8 * plane : 8 * plane + 8, :],
        stage,
        chunk,
        [((chunk.tail, chunk.tail_lane, 128), field)],
        extras,
    )
    send_chunks(stage, kinds, send, chunk, neighbour_ids(across), owners)
    for copy in later:
        copy.wait()


def make_masks(chunk, homes, landed, live, masks_ref, table, spread_ref, cases):
    lane1 = lanes_of((1, 128))
    table[...] = jnp.zeros((128, 128), jnp.float32)
    for x in range(4):
        for y in range(4):
            sx, sy = (-1, 0, 0, 1)[x], (-1, 0, 0, 1)[y]
            ix, iy = (1, 0, 1, 0)[x], (1, 0, 1, 0)[y]
            row = jnp.zeros((1, 128), jnp.float32)
            for t in range(TZ):
                if (sx, sy) == (0, 0):
                    value, start = live[t : t + 1, :], 32 * (2 * ix + iy)
                else:
                    where, start = chunk.live[t]
                    value = landed[homes[(sx, sy)] + where : homes[(sx, sy)] + where + 1, :]
                    start = start + 32 * (ix if sy else iy)
                here = (lane1 >= 32 * t) & (lane1 < 32 * t + 32)
                row = jnp.where(here, turn(value, start - 32 * t), row)
            table[4 * x + y : 4 * x + y + 1, :] = row
    by_code = jnp.transpose(table[...])
    big = (128, 128)
    for x in range(4):
        pick = jnp.where(rows_of(big) == 4 * x + lanes_of(big) // 32, 1.0, 0.0)
        alive = jnp.dot(by_code, pick, preferred_element_type=jnp.float32)
        spread_ref[128 * x : 128 * x + 128, :] = FAR_AWAY * (1.0 - alive)

    lane = lanes_of()
    half_layer = lane % 8
    parity = lane % 2
    cell_y = lane // 8 % 4
    low_rows = rows_of() < 4

    def crossing(position, step):
        return (position + step < 0) | (position + step >= 8)

    groups = grouped(NEAR + FAR)

    def at_t(t, carry):
        for code in range(27):
            for block in range(2):
                first, second = [
                    spread_ref[pl.ds(128 * x + 32 * t + code, 1), :] for x in (2 * block, 2 * block + 1)
                ]
                cases[16 * code + 8 * block : 16 * code + 8 * block + 8, :] = jnp.where(
                    low_rows, jnp.broadcast_to(first, (8, 128)), jnp.broadcast_to(second, (8, 128))
                )

        def case(ex, ey, ez, block):
            code = 9 * (ex + 1) + 3 * (ey + 1) + ez + 1
            return cases[16 * code + 8 * block : 16 * code + 8 * block + 8, :]

        for dz in sorted({key[1] for key, _ in groups}):
            cross_z = crossing(half_layer, dz)
            in_z = {}

            def level_z(ex, ey, block):
                if (ex, ey, block) not in in_z:
                    value = case(ex, ey, 0, block)
                    if dz:
                        value = jnp.where(cross_z, case(ex, ey, sign(dz), block), value)
                    in_z[(ex, ey, block)] = value
                return in_z[(ex, ey, block)]

            for (dy, other_z), dxs in groups:
                if other_z != dz:
                    continue
                cross_y = crossing(2 * cell_y + parity, dy)
                in_y = {}

                def level_y(ex, block):
                    if (ex, block) not in in_y:
                        value = level_z(ex, 0, block)
                        if dy:
                            value = jnp.where(cross_y, level_z(ex, sign(dy), block), value)
                        in_y[(ex, block)] = value
                    return in_y[(ex, block)]

                for dx in dxs:
                    cross_x = crossing(2 * (rows_of() % 4) + parity, dx)
                    for block in range(2):
                        value = level_y(0, block)
                        if dx:
                            value = jnp.where(cross_x, level_y(sign(dx), block), value)
                        at = MASK_SLOT[(dx, dy, dz)] * SIZE + BASE + 8 * block
                        masks_ref[pl.ds(at + t * ROWS, 8), :] = value
        return carry

    lax.fori_loop(0, TZ, at_t, 0)


def step_kernel(step, across, arriving, leaving, groups, limit, *refs):
    nx, ny = across
    owners = nx * ny
    refs = list(refs)
    last = leaving is None

    def take(count):
        taken = refs[:count]
        del refs[:count]
        return taken

    recv, in_u, in_v, noise = take(4)
    if step == 0:
        (live,) = take(1)
    else:
        masks_ref, in_grid, in_bad = take(3)
    send, out_grid, out_bad, out_u, out_v = take(5)
    if step == 0:
        (masks_ref,) = take(1)
    window, moved, slope, slope_moved, gaps, inverses, landed, tails_at, noise_own = take(9)
    v_own, stage, mixed, starts = take(4)
    extra = refs
    u_own = out_u
    if step:
        v_own = out_v
    else:
        v_own, v_start = out_v, v_own
    if step == 0:
        table, spread_ref, cases = extra
    ids = neighbour_ids(across)
    lane = lanes_of()

    homes = receive_chunks(recv, landed, tails_at, arriving, ids, owners)
    if step == 0:
        make_masks(arriving, homes, landed, live, masks_ref, table, spread_ref, cases)

    tail = repeat_tail(tails_at[0:owners, :], arriving)
    if step == 0:
        table[...] = jnp.zeros((128, 128), jnp.float32)
        table[0:owners, :] = tail
        turned = jnp.transpose(table[...])[:owners]
        reach = 128
        while reach > owners:
            reach //= 2
            turned = turned + pltpu.roll(turned, reach, 1)
        grid = [turned[ny * x : ny * x + ny] for x in range(nx)]
        out_bad[...] = jnp.zeros((8, 128), jnp.float32)
    else:
        grid = [
            in_grid[ny * x : ny * x + ny, :] + tail[ny * x : ny * x + ny] * (1.0 / heat_capacity)
            for x in range(nx)
        ]
        grid = diffuse_grid(grid, across)
        where, start = arriving.reach
        from_row = owners * (where != arriving.tail)
        furthest = tails_at[from_row : from_row + owners, :]
        lane_n = lanes_of((owners, 128))
        furthest = jnp.where((lane_n >= start) & (lane_n < start + 32), furthest, 0.0)
        reached = jnp.max(furthest, axis=0, keepdims=True)
        reached = jnp.max(reached, axis=1, keepdims=True)
        over = jnp.broadcast_to(jnp.where(reached > limit, 1.0, 0.0), (8, 128))
        out_bad[...] = jnp.maximum(in_bad[...], over)
    for x in range(nx):
        out_grid[ny * x : ny * x + ny, :] = grid[x]
    local = temperatures_by_layer(out_grid[pl.ds(ids[(0, 0)], 1), :], owners)
    kick = jnp.sqrt(local * (2.0 * friction * atom_mass / time_step))

    def own_u(plane):
        return in_u[8 * plane : 8 * plane + 8, :]

    origin = jnp.minimum(lax.axis_index("gx"), 0)
    build_window(own_u, landed, homes, window, arriving, origin)
    mix_planes(3, window, mixed, origin)
    known = (window, moved, masks_ref, slope, gaps, inverses, groups)
    sweep = DensitySweep(window, moved, masks_ref, gaps, inverses, starts, groups, origin)
    shift_planes(3, window, mixed, moved, groups, coordinate_shift, origin, sweep.part)
    sweep.finish(slope)
    pull = ForceSweep(window, moved, slope, slope_moved, gaps, inverses, groups, origin)
    mix_planes(1, slope, mixed, origin)
    shift_planes(1, slope, mixed, slope_moved, groups, no_shift, origin, pull.part)

    from_tiles(lambda c, ix, iy: noise[step, c, ix, :, iy, :], noise_own)
    speeds_in = in_v
    if step == 0:
        from_tiles(lambda c, ix, iy: in_v[c, ix, :, iy, :], v_start)
        speeds_in = v_start

    active = (lane >= 32) & (lane < 96)
    power = []
    furthest = jnp.zeros((8, 128), jnp.float32)
    for t in range(TZ):
        force = pull.finish(t)
        layer = jnp.zeros((8, 128), jnp.float32)
        for c in range(3):
            at = 8 * (c * TZ + t)
            speed = speeds_in[at : at + 8, :]
            push = force[c] - friction * atom_mass * speed + kick[t : t + 1] * noise_own[at : at + 8, :]
            speed = speed + time_step / atom_mass * push
            speed = jnp.where(active, speed, 0.0)
            place = own_u(c * TZ + t) + time_step * speed
            v_own[at : at + 8, :] = speed
            u_own[at : at + 8, :] = place
            layer = layer + speed * speed
            furthest = jnp.maximum(furthest, jnp.abs(place))
        power.append(jnp.sum(layer, axis=0, keepdims=True))
    energy = energies_by_plane(power, owners) * (friction * atom_mass * time_step)
    if last:
        send[...] = jnp.broadcast_to(energy, (owners, 128))
        return
    furthest = jnp.max(furthest, axis=0, keepdims=True)
    furthest = jnp.broadcast_to(jnp.max(furthest, axis=1, keepdims=True), (1, 128))
    where, start = leaving.reach
    tail_row = [
        ((leaving.tail, leaving.tail_lane, 128), energy),
        ((where, start, start + 32), furthest),
    ]
    kinds = stage_halo(
        lambda plane: u_own[8 * plane : 8 * plane + 8, :], stage, leaving, tail_row, {}
    )
    send_chunks(stage, kinds, send, leaving, ids, owners)


def finish(across, recv, in_grid, heat):
    nx, ny = across
    grid = [
        in_grid[ny * x : ny * x + ny, :] + recv[ny * x : ny * x + ny, :] * (1.0 / heat_capacity)
        for x in range(nx)
    ]
    grid = diffuse_grid(grid, across)
    me = lax.axis_index("gx") * ny + lax.axis_index("gy")
    flat = rows_of((ny, 128)) == lanes_of((ny, 128))
    for x in range(nx):
        mine = jnp.where(lanes_of((ny, 128)) == me, grid[x], 0.0)
        mine = jnp.broadcast_to(jnp.sum(mine, axis=1, keepdims=True), (ny, 128))
        row = jnp.sum(jnp.where(flat, mine, 0.0), axis=0, keepdims=True)
        heat[0, x : x + 1, :] = row[:, :ny]


def leave(in_u, in_v, new_u, new_v):
    to_tiles(in_u, new_u)
    to_tiles(in_v, new_v)


def exchange(value):
    return lax.all_to_all(value, ("gx", "gy"), split_axis=0, concat_axis=0, tiled=True)


VMEM_BYTES = 28 * 1024 * 1024


def call(kernel, outs, scratch, operands, in_hbm=(), name=None):
    specs = [
        pl.BlockSpec(memory_space=pltpu.HBM if n in in_hbm else pltpu.VMEM)
        for n in range(len(operands))
    ]
    return pl.pallas_call(
        kernel,
        out_shape=[
            jax.ShapeDtypeStruct(*(out if isinstance(out[1], type) else (out, jnp.float32)))
            for out in outs
        ],
        in_specs=specs,
        out_specs=[pl.BlockSpec(memory_space=pltpu.VMEM)] * len(outs),
        scratch_shapes=scratch,
        compiler_params=pltpu.CompilerParams(
            vmem_limit_bytes=VMEM_BYTES,
        ),
        name=name,
    )(*operands)


def stencil_steps(displacement, velocity, noise, electron_temp, pair_list, pair_count):
    across = (lax.axis_size("gx"), lax.axis_size("gy"))
    owners = across[0] * across[1]

    def vmem(*shape):
        return pltpu.VMEM(shape, jnp.float32)

    tiles = (3, BXT, TZ, BYT, TILE)
    placed_u = jnp.swapaxes(displacement, 2, 3)
    placed_v = jnp.swapaxes(velocity, 2, 3)
    placed_noise = jnp.swapaxes(noise, 3, 4)
    slots = pair_list.shape[-1]
    first, two, three = Chunk(owners, 2, True), Chunk(owners, 2), Chunk(owners, 3)
    send, own_u, live, kept_heat, kept_count, own_v, near_noise = call(
        partial(prepare, across, first),
        [
            (owners, 1, 128 * first.rows),
            (72, 128),
            (8, 128),
            electron_temp.shape,
            ((8, 128), jnp.int32),
            placed_v.shape,
            placed_noise.shape,
        ],
        [
            pltpu.VMEM((8, (slots + 127) // 128 * 128), jnp.int32),
            vmem(*tiles),
            vmem(*electron_temp.shape),
            pltpu.VMEM(pair_list.shape, jnp.int32),
            pltpu.SMEM(pair_count.shape, jnp.int32),
            vmem(4 * 16, 128),
            pltpu.SemaphoreType.DMA((6,)),
        ],
        (
            placed_u,
            pltpu.with_memory_space_constraint(electron_temp, pltpu.HBM),
            pair_list,
            pair_count,
            placed_v,
            placed_noise,
        ),
        in_hbm=(0, 1, 2, 3, 4, 5),
        name="prepare",
    )
    near, far = grouped(NEAR), grouped(NEAR + FAR)
    plan = [
        (first, two, near, 1.0),
        (two, three, near, NEAR_LIMIT),
        (three, three, far, FAR_LIMIT),
        (three, None, far, FAR_LIMIT),
    ]
    masks = grid = bad = None
    for step, (arriving, leaving, groups, limit) in enumerate(plan):
        recv = exchange(send)
        last = leaving is None
        pairs = sum(len(dxs) for _, dxs in groups)
        outs = [
            (owners, 128) if last else (owners, 1, 128 * leaving.rows),
            (owners, 128),
            (8, 128),
            (72, 128),
            (72, 128),
        ]
        scratch = [
            vmem(3 * SIZE + PAD, 128),
            vmem(len(groups) * 3 * SIZE, 128),
            vmem(SIZE, 128),
            vmem(len(groups) * SIZE, 128),
            vmem(24 * pairs, 128),
            vmem(24 * pairs, 128),
            vmem(9 * 16 + 2 * PAD, 128),
            vmem(2 * owners, 128),
            vmem(72, 128),
            vmem(72, 128),
            vmem(4 * 16, 128),
            vmem(3 * SIZE, 128),
            vmem(8 * 5 * 7, 128),
        ]
        if step == 0:
            outs.append((MASKS * SIZE, 128))
            scratch += [vmem(128, 128), vmem(512, 128), vmem(27 * 16, 128)]
            operands = (recv, own_u, own_v, near_noise, live)
        else:
            operands = (recv, own_u, own_v, near_noise, masks, grid, bad)
        got = call(
            partial(step_kernel, step, across, arriving, leaving, groups, limit),
            outs,
            scratch,
            operands,
            name=f"step{step}",
        )
        send, grid, bad, own_u, own_v = got[:5]
        if step == 0:
            masks = got[5]
    recv = exchange(send)
    new_u, new_v = call(leave, [tiles, tiles], [], (own_u, own_v), name="leave")
    (heat,) = call(partial(finish, across), [electron_temp.shape], [], (recv, grid), name="finish")
    kept = (kept_heat, kept_count[:1, :1])
    return bad[0, 0], kept, jnp.swapaxes(new_u, 2, 3), jnp.swapaxes(new_v, 2, 3), heat


def per_device(displacement, velocity, noise, electron_temp, pair_list, pair_count):
    given = (displacement, velocity, noise, electron_temp, pair_list, pair_count)
    bad, (kept_heat, kept_count), new_u, new_v, heat = stencil_steps(*given)
    given = (displacement, velocity, noise, kept_heat, pair_list, kept_count)
    return lax.cond(bad > 0.5, lambda: whole_sweep(*given), lambda: (new_u, new_v, heat))


def solution(mesh):
    placed = (
        P(None, "gx", "gy", None, None),
        P(None, "gx", "gy", None, None),
        P(None, None, "gx", "gy", None, None),
        P(("gx", "gy"), None, None),
        P("gx", "gy", None, None),
        P("gx", "gy"),
    )
    return jax.shard_map(
        per_device,
        mesh=mesh,
        in_specs=placed,
        out_specs=(
            P(None, "gx", "gy", None, None),
            P(None, "gx", "gy", None, None),
            P(("gx", "gy"), None, None),
        ),
        check_vma=False,
    )
```

```python
from functools import partial

import jax
import jax.numpy as jnp
from jax import lax
from jax.experimental import pallas as pl
from jax.experimental.pallas import tpu as pltpu
from jax.sharding import PartitionSpec as P

CB = 4
TILE = 128
BXT = 2
BYT = 2
TZ = 3
TILES = 12
STEPS = 4
SUB = 6


lattice_edge = 3.1652
density_cut = 4.400224
embed_scale = 1.896373
pair_cut = 3.25
coef_zero = 47.1346499
coef_one = -33.7665655
coef_two = 6.2541999
time_step = 0.005
atom_mass = 0.0190534
friction = 1.0
heat_capacity = 0.02
diffusion_rate = 0.12


def padded_2(block, sides, width):
    for axis, dim in sides:
        count = lax.axis_size(axis)
        forward = [(i, i + 1) for i in range(count - 1)]
        forward.append((count - 1, 0))
        backward = [(target, source) for source, target in forward]
        low = lax.ppermute(
            lax.slice_in_dim(block, block.shape[dim] - width, None, axis=dim), axis, forward
        )
        high = lax.ppermute(lax.slice_in_dim(block, 0, width, axis=dim), axis, backward)
        block = jnp.concatenate([low, block, high], axis=dim)
    return block


def lattice_sites():
    serial = jnp.arange(TILE, dtype=jnp.int32)
    cell_number = serial // 2
    half_step = (serial % 2).astype(jnp.float32) * 0.5
    corners = jnp.stack([cell_number // (CB * CB), cell_number // CB % CB, cell_number % CB])
    return lattice_edge * (corners.astype(jnp.float32) + half_step[None, :])


def plane_table(plane_total):
    serial = jnp.arange(TILE, dtype=jnp.int32)
    cell_number = serial // 2
    layer = 2 * (cell_number % CB) + serial % 2
    tiles = jnp.arange(TZ, dtype=jnp.int32)
    whole = tiles[:, None] * (2 * CB) + layer[None, :]
    return whole * plane_total // (2 * CB * TZ)


def pair_geometry(window, tile_index, neighbour_code, lattice):
    wide_y = BYT + 2
    depth_t = tile_index % TZ
    inner_y = tile_index // TZ % BYT
    inner_x = tile_index // (TZ * BYT)
    shift_x = neighbour_code // 9
    shift_y = neighbour_code // 3 % 3
    shift_z = neighbour_code % 3
    flattened = window.reshape(window.shape[0], (BXT + 2) * wide_y * TZ, TILE)
    own_index = ((inner_x + 1) * wide_y + inner_y + 1) * TZ + depth_t
    other_index = ((inner_x + shift_x) * wide_y + inner_y + shift_y) * TZ + (
        depth_t + shift_z - 1 + TZ
    ) % TZ
    own_tile = lax.dynamic_index_in_dim(flattened, own_index, 1, keepdims=False)
    other_tile = lax.dynamic_index_in_dim(flattened, other_index, 1, keepdims=False)
    offset = jnp.stack([shift_x - 1, shift_y - 1, shift_z - 1]).astype(jnp.float32) * (
        CB * lattice_edge
    )
    left = lattice + own_tile
    right = lattice + other_tile + offset[:, None]
    delta = left[:, :, None] - right[:, None, :]
    square = jnp.sum(delta * delta, axis=0)
    serial = jnp.arange(TILE, dtype=jnp.int32)
    same_atom = (neighbour_code == 13) & (serial[:, None] == serial[None, :])
    distance = jnp.sqrt(jnp.where(same_atom, 100.0, square))
    return (delta, distance, own_index, other_index)


def density_term(window, lattice, tile_index, neighbour_code):
    delta, distance, own_index, other_index = pair_geometry(
        window, tile_index, neighbour_code, lattice
    )
    dens_gap = distance - density_cut
    return jnp.sum(jnp.where(distance < density_cut, dens_gap * dens_gap, 0.0), axis=1)[None]


def force_term(window, embed_window, lattice, tile_index, neighbour_code):
    delta, distance, own_index, other_index = pair_geometry(
        window, tile_index, neighbour_code, lattice
    )
    flat_embed = embed_window.reshape((BXT + 2) * (BYT + 2) * TZ, TILE)
    own_embed = lax.dynamic_index_in_dim(flat_embed, own_index, 0, keepdims=False)
    other_embed = lax.dynamic_index_in_dim(flat_embed, other_index, 0, keepdims=False)
    pair_gap = distance - pair_cut
    poly = coef_zero + coef_one * distance + coef_two * distance * distance
    pair_slope = jnp.where(
        distance < pair_cut,
        2.0 * pair_gap * poly + pair_gap * pair_gap * (coef_one + 2.0 * coef_two * distance),
        0.0,
    )
    dens_gap = distance - density_cut
    dens_slope = jnp.where(distance < density_cut, 2.0 * dens_gap, 0.0)
    scalar = (pair_slope + (own_embed[:, None] + other_embed[None, :]) * dens_slope) / distance
    return -jnp.sum(scalar[None] * delta, axis=2)


def sweep_pairs(term_fn, channels, pair_table, pair_total):
    initial = jnp.zeros((channels, TILES, TILE), jnp.float32)

    def block_add(block_index, running):
        start = block_index * 27
        chosen = lax.dynamic_slice_in_dim(pair_table, start, 27, 1)
        live = start + jnp.arange(27, dtype=jnp.int32) < pair_total
        terms = jax.vmap(term_fn)(chosen[0], chosen[1])
        terms = jnp.where(live[:, None, None], terms, 0.0)
        return running.at[:, chosen[0]].add(jnp.swapaxes(terms, 0, 1))

    blocks = (pair_total + 26) // 27
    total = lax.fori_loop(0, blocks, block_add, initial)
    return total.reshape(channels, BXT, BYT, TZ, TILE)


def relax_slab(padded):
    center = padded[1:-1]
    beside_all = padded[2:] + padded[:-2] + jnp.roll(center, 1, 1) + jnp.roll(center, -1, 1)
    beside_all = beside_all + jnp.roll(center, 1, 2) + jnp.roll(center, -1, 2)
    return center + diffusion_rate * (beside_all - 6.0 * center)


def one_step(lattice, pair_table, pair_total, planes, owners, across, carry, noise_now):
    positions, speeds, heat_field = carry
    slab_depth = heat_field.shape[0]
    plane_total = slab_depth * owners
    arrived = lax.all_to_all(
        heat_field.reshape(slab_depth, owners), ("gx", "gy"), split_axis=1, concat_axis=0, tiled=True
    )
    column = arrived.reshape(-1)
    column_temp = jnp.take(column, planes).reshape(TZ, TILE)
    local_temp = jnp.broadcast_to(column_temp, (BXT, BYT, TZ, TILE))
    window = padded_2(positions, (("gx", 1), ("gy", 2)), 1)
    density = sweep_pairs(partial(density_term, window, lattice), 1, pair_table, pair_total)
    embed_slope = -embed_scale / (2.0 * jnp.sqrt(density))
    embed_window = padded_2(embed_slope, (("gx", 1), ("gy", 2)), 1)
    force = sweep_pairs(partial(force_term, window, embed_window, lattice), 3, pair_table, pair_total)
    kicker = jnp.sqrt(2.0 * friction * atom_mass * local_temp / time_step)[None] * noise_now
    speeds = speeds + time_step / atom_mass * (force - friction * atom_mass * speeds + kicker)
    positions = positions + time_step * speeds
    power = friction * atom_mass * time_step * jnp.sum(speeds * speeds, axis=0)
    tile_power = jnp.sum(power, axis=(0, 1)).reshape(-1)
    energy = jnp.zeros((plane_total,), jnp.float32).at[planes].add(tile_power)
    arrived = lax.all_to_all(
        energy.reshape(plane_total, 1), ("gx", "gy"), split_axis=0, concat_axis=1, tiled=True
    )
    heat_field = heat_field + arrived.reshape(slab_depth, *across) / heat_capacity

    def relax(sub_index, heat):
        return relax_slab(padded_2(heat, ((("gx", "gy"), 0),), 1))

    heat_field = lax.fori_loop(0, SUB, relax, heat_field)
    return (positions, speeds, heat_field)


def whole_sweep(displacement, velocity, noise, electron_temp, pair_list, pair_count):
    across = (lax.axis_size("gx"), lax.axis_size("gy"))
    owners = across[0] * across[1]
    planes = plane_table(electron_temp.shape[0] * owners).reshape(-1)
    step = partial(
        one_step, lattice_sites(), pair_list[0, 0], pair_count[0, 0], planes, owners, across
    )
    return lax.fori_loop(
        0,
        STEPS,
        lambda n, carry: step(carry, lax.dynamic_index_in_dim(noise, n, 0, keepdims=False)),
        (displacement, velocity, electron_temp),
    )


NEAR_SHELLS = (3, 4, 8)
FAR_SHELLS = (11, 12)
NEAR_LIMIT = 0.2900
FAR_LIMIT = 0.8170
NEAR_NO_PAIR = (8,)
HALF = 0.5 * lattice_edge
FAR_AWAY = 1.0e6
ROWS = 20
BASE = 2
SIZE = TZ * ROWS
EDGES = (2, 3)


def site_offsets(shells):
    span = range(-3, 4)
    found = []
    for x in span:
        for y in span:
            for z in span:
                if x % 2 == y % 2 == z % 2 and x * x + y * y + z * z in shells:
                    found.append((x, y, z))
    return found


def grouped(offsets):
    table = {}
    for x, y, z in offsets:
        table.setdefault((y, z), []).append(x)
    return sorted(table.items())


NEAR = site_offsets(NEAR_SHELLS)
FAR = site_offsets(FAR_SHELLS)
MASK_SLOT = {offset: slot for slot, offset in enumerate(NEAR + FAR)}
MASKS = len(MASK_SLOT)


def by_x(groups):
    table = {}
    for n, ((dy, dz), dxs) in enumerate(groups):
        for dx in dxs:
            table.setdefault(dx, []).append((n, dy, dz))
    return sorted(table.items())


def sign(value):
    return (value > 0) - (value < 0)


def lanes_of(shape=(8, 128)):
    return lax.broadcasted_iota(jnp.int32, shape, len(shape) - 1)


def rows_of(shape=(8, 128)):
    return lax.broadcasted_iota(jnp.int32, shape, len(shape) - 2)


def turn(value, amount):
    amount = (-amount) % 128
    return value if amount == 0 else pltpu.roll(value, amount, value.ndim - 1)


def pick_lanes(value, index):
    return jnp.take_along_axis(value, index, axis=1, mode="promise_in_bounds")


class Chunk:
    def __init__(self, owners, cells, first=False):
        self.cells = cells
        self.narrow = owners <= 32
        halo = 9 if cells == 2 else 14
        if self.narrow:
            self.tail = 9 if cells == 2 else 13
            self.tail_lane = 96
            self.reach = (self.tail, 64)
            self.rows = self.tail + 1
        else:
            self.tail = halo
            self.tail_lane = 0
            self.reach = (halo + 1, 64)
            self.rows = halo + 2
        if first:
            self.live = [(self.reach[0], 0), (self.rows, 0), (self.rows, 64)]
            self.rows += 1

    def x_home(self, plane, row):
        if plane < 8:
            return self.cells * (plane // 2) + row, plane % 2
        return 4 * self.cells + row // 2, row % 2


def repeat_tail(value, chunk):
    if not chunk.narrow:
        return value
    return pick_lanes(value, 96 + lanes_of(value.shape) % 32)


def from_tiles(read, out):
    lane = lanes_of((TZ, 128))
    own = (lane >= 32) & (lane < 96)
    for c in range(3):
        for ix in range(BXT):
            first, second = [read(c, ix, iy) for iy in range(BYT)]
            for cx in range(CB):
                both = jnp.where(lane < 64, turn(first, 32 * cx - 32), turn(second, 32 * cx - 64))
                start = c * TZ * 8 + CB * ix + cx
                out[pl.ds(start, TZ, stride=8), :] = jnp.where(own, both, 0.0)


def to_tiles(source, out):
    lane = lanes_of((TZ, 128))
    for c in range(3):
        for ix in range(BXT):
            rows = [source[pl.ds(c * TZ * 8 + CB * ix + cx, TZ, stride=8), :] for cx in range(CB)]
            for iy in range(BYT):
                value = None
                for cx in range(CB):
                    piece = turn(rows[cx], 32 + 32 * iy - 32 * cx)
                    value = piece if value is None else jnp.where(lane >= 32 * cx, piece, value)
                out[c, ix, :, iy, :] = value


def each(count, body):
    if count <= 32:
        for index in range(count):
            body(index, 0)
    else:
        lax.fori_loop(0, count, body, 0, unroll=8)


def stage_halo(own, stage, chunk, tail_row, extras):
    w = chunk.cells
    lane, row = lanes_of(), rows_of()
    kinds = {}
    depth = stage.shape[0] // 4
    low = lane < 64
    third = [pick for pick in range(5)] if w == 3 else []
    for kind, (axis, side) in enumerate((("x", -1), ("x", 1), ("y", -1), ("y", 1))):
        at = kind * depth
        kinds[(axis, side)] = at
        if axis == "x":
            first = 8 - w if side == 1 else 0
            for pair in range(4):
                both = jnp.where(low, turn(own(2 * pair), 32), turn(own(2 * pair + 1), -32))
                stage[at + w * pair : at + w * pair + w, :] = both[first : first + w]
            last = own(8)
            a, b = turn(last, 32), turn(last, -32)
            low1 = lanes_of((1, 128)) < 64
            stage[at + 4 * w : at + 4 * w + 1, :] = jnp.where(
                low1, a[first : first + 1], b[first + 1 : first + 2]
            )
            if w == 3:
                stage[at + 13 : at + 14, :] = a[first + 2 : first + 3]
        else:
            start = 80 if side == 1 else 32
            packed = None
            for plane in range(8):
                piece = turn(own(plane), start - 16 * plane)
                packed = piece if packed is None else jnp.where(lane >= 16 * plane, piece, packed)
            stage[at : at + 8, :] = packed
            flat = pick_lanes(own(8), start + lane % 16)
            flat = jnp.where(lane // 16 == row, flat, 0.0)
            stage[at + 8 : at + 9, :] = jnp.sum(flat, axis=0, keepdims=True)
            start = 72 if side == 1 else 48
            for pair in third:
                flat = pick_lanes(own(2 * pair), start + lane % 8)
                if pair < 4:
                    flat = jnp.where(low, flat, pick_lanes(own(2 * pair + 1), start + lane % 8))
                flat = jnp.where(lane % 64 // 8 == row, flat, 0.0)
                stage[at + 9 + pair : at + 10 + pair, :] = jnp.sum(flat, axis=0, keepdims=True)
        for (where, lane_from, lane_to), value in tail_row + extras.get((axis, side), []):
            lane1 = lanes_of((1, 128))
            old = stage[at + where : at + where + 1, :]
            here = (lane1 >= lane_from) & (lane1 < lane_to)
            stage[at + where : at + where + 1, :] = jnp.where(here, value, old)
    return kinds


def send_chunks(stage, kinds, send_ref, chunk, ids, owners):
    tails = sorted({chunk.tail, chunk.reach[0]})
    at = kinds[("x", 1)]
    rows = {where: stage[at + where : at + where + 1, :] for where in tails}

    for (sx, sy), ident in ids.items():
        if (sx, sy) == (0, 0):
            continue
        at = kinds[("y", sy)] if sy else kinds[("x", sx)]
        for k in range(chunk.rows):
            if k not in tails:
                send_ref[ident, :, 128 * k : 128 * k + 128] = stage[at + k : at + k + 1, :]

    def fill(index, carry):
        for where in tails:
            send_ref[index, :, 128 * where : 128 * where + 128] = rows[where]
        return carry

    each(owners, fill)
    for (sx, sy), ident in ids.items():
        if (sx, sy) == (0, 0):
            continue
        at = kinds[("y", sy)] if sy else kinds[("x", sx)]
        for k in tails:
            send_ref[ident, :, 128 * k : 128 * k + 128] = stage[at + k : at + k + 1, :]


def receive_chunks(recv_ref, landed, tails_at, chunk, ids, owners):
    depth = (landed.shape[0] - 2 * PAD) // 9
    homes = {}
    for n, ((sx, sy), ident) in enumerate(ids.items()):
        if (sx, sy) == (0, 0):
            continue
        homes[(sx, sy)] = PAD + n * depth
        for k in range(chunk.rows):
            landed[PAD + n * depth + k : PAD + n * depth + k + 1, :] = recv_ref[ident, :, 128 * k : 128 * k + 128]

    tails = sorted({chunk.tail, chunk.reach[0]})

    def take(index, carry):
        for n, where in enumerate(tails):
            tails_at[pl.ds(n * owners + index, 1), :] = recv_ref[index, :, 128 * where : 128 * where + 128]
        return carry

    each(owners, take)
    return homes


PAD = 8


def build_window(own, landed, homes, window, chunk, origin):
    w = chunk.cells
    lane, row = lanes_of(), rows_of()
    zero = jnp.zeros((8, 128), jnp.float32)
    middle = (lane >= 32) & (lane < 96)
    first_rows = row < 4

    def outer(start, size, sy):
        values = [landed[homes[(sx, sy)] + start : homes[(sx, sy)] + start + size, :] for sx in (1, -1)]
        if size == 1:
            values = [jnp.broadcast_to(value, (8, 128)) for value in values]
        return jnp.where(first_rows, values[0], values[1])

    def inner(start, size, sy):
        value = landed[homes[(0, sy)] + start : homes[(0, sy)] + start + size, :]
        return jnp.broadcast_to(value, (8, 128))

    sides = (-1, 1)
    packed = {(sy, out): (outer if out else inner)(0, 8, sy) for sy in sides for out in (0, 1)}
    for plane in range(9):
        at = plane * ROWS + BASE
        parts = [own(plane), zero]
        for sy in sides:
            target = 16 if sy == -1 else 96
            here = (lane >= target) & (lane < target + 16)
            beyond = 8 if sy == -1 else 112
            here_third = (lane >= beyond) & (lane < beyond + 8)
            for out in (0, 1):
                if plane < 8:
                    piece = turn(packed[(sy, out)], 16 * plane - target)
                else:
                    wide = (outer if out else inner)(8, 1, sy)
                    piece = pick_lanes(wide, 16 * row + lane % 16)
                parts[out] = jnp.where(here, piece, parts[out])
                if w == 3:
                    wide = (outer if out else inner)(9 + plane // 2, 1, sy)
                    piece = pick_lanes(wide, 64 * (plane % 2) + 8 * row + lane % 8)
                    parts[out] = jnp.where(here_third, piece, parts[out])
        centre, rim = parts
        if plane < 8:
            home, half = chunk.x_home(plane, 0)
            back = -32 if half == 0 else 32
            behind = landed[pl.ds(origin + homes[(1, 0)] + home, 8), :]
            ahead = landed[pl.ds(origin + homes[(-1, 0)] + home - (4 - w) - 4, 8), :]
            piece = turn(jnp.where(first_rows, behind, ahead), back)
            rim = jnp.where(middle & ((row < w) | (row >= 8 - w)), piece, rim)
        else:
            for k in range(w):
                home, half = chunk.x_home(plane, k)
                back = -32 if half == 0 else 32
                for sx, to in ((1, k), (-1, 8 - w + k)):
                    base = homes[(sx, 0)] + home
                    piece = turn(jnp.broadcast_to(landed[base : base + 1, :], (8, 128)), back)
                    rim = jnp.where(middle & (row == to), piece, rim)
        window[pl.ds(origin + at, 8), :] = pltpu.roll(rim, 4, 0)
        window[pl.ds(origin + at + 12, 8), :] = rim
        window[pl.ds(origin + at + 4, 8), :] = centre


def mix_planes(count, source, mixed, origin):
    even = lanes_of((16, 128)) % 2 == 0
    for plane in range(count * TZ):
        at = plane * ROWS + BASE
        here = source[pl.ds(origin + at, 16), :]
        after = turn(source[pl.ds(origin + at + 1, 16), :], 8)
        mixed[pl.ds(origin + at, 16), :] = jnp.where(even, after, here)


def sources(dy, dz, use_mixed):
    s = sign(dz)
    low = dy // 2
    if dy % 2 == 0 or use_mixed:
        out = [(None, 0, dz + 8 * low, 0)]
        if s:
            out.append((None, s, dz - 8 * s + 8 * low, 0))
        return out
    out = [(0, 0, dz + 8 * low, 0), (1, 0, dz + 8 * (low + 1), 1)]
    for parity, k in ((0, low), (1, low + 1)):
        if any(not 0 <= iz + dz < 8 for iz in range(parity, 8, 2)):
            out.append((parity, s, dz - 8 * s + 8 * k, parity))
    return out


def shift_planes(count, source, mixed, out, groups, constants, origin, ready=None):
    half_layer = lanes_of((16, 128)) % 8
    parity = half_layer % 2
    slots = {key: n for n, (key, _) in enumerate(groups)}
    planes = [(c, t) for c in range(count) for t in range(TZ)]
    for dz in sorted({key[1] for key in slots}, key=lambda z: (z % 2, abs(z))):
        dys = sorted((key[0] for key in slots if key[1] == dz), key=abs)
        carried = (half_layer + dz >= 8) | (half_layer + dz < 0)
        ref = mixed if dz % 2 and mixed is not None else source
        turned = {}

        def taken(c, t, shift, down):
            key = (c, t, shift, down)
            if key not in turned:
                at = (c * TZ + t) * ROWS + BASE + down
                turned[key] = turn(ref[pl.ds(origin + at, 16), :], shift)
            return turned[key]

        for dy in dys:
            parts = sources(dy, dz, mixed is not None)
            for want, carry_z, shift, down in parts:
                for c, t in planes:
                    taken(c, t, shift, down)
            for c, t in planes:
                value = None
                for want, carry_z, shift, down in parts:
                    piece = taken(c, (t + carry_z) % TZ, shift, down)
                    if value is None:
                        value = piece
                        continue
                    here = None
                    if want is not None:
                        here = parity == want
                    if carry_z:
                        here = carried if here is None else here & carried
                    value = jnp.where(here, piece, value)
                shift_by = constants(c, dy, dz)
                if shift_by:
                    value = value + shift_by
                at = slots[(dy, dz)] * count * SIZE + (c * TZ + t) * ROWS + BASE
                out[pl.ds(origin + at, 16), :] = value
            if ready is not None:
                ready(slots[(dy, dz)], dy, dz)


def coordinate_shift(c, dy, dz):
    return (0.0, HALF * dy, HALF * dz)[c]


def no_shift(c, dy, dz):
    return 0.0


def row_start(dx):
    return dx // 2 if dx % 2 == 0 else (dx - 1) // 2


class DensitySweep:
    def __init__(self, window, moved, masks_ref, gaps, inverses, starts, groups, origin):
        self.refs = (window, moved, masks_ref, gaps, inverses, starts)
        self.groups = dict(groups)
        self.targets = []
        for t in range(TZ):
            self.targets.append((self.own_rows(origin, t * ROWS + BASE + 4), 8 * t, 8))
        for edge in EDGES:
            self.targets.append((self.edge_rows(origin, BASE + edge), None, 2 * TZ))
        self.xs = sorted({dx for dxs in self.groups.values() for dx in dxs})
        self.totals = [jnp.zeros((height, 128), jnp.float32) for _, _, height in self.targets]
        self.own = []
        for k, (rows, _, height) in enumerate(self.targets):
            self.own.append([window[rows(c * SIZE), :] for c in (1, 2)])
            own_x = window[rows(0), :]
            for j, dx in enumerate(self.xs):
                at = 8 * (k * len(self.xs) + j)
                starts[at : at + height, :] = own_x - HALF * dx

    @staticmethod
    def own_rows(origin, start):
        return lambda base: pl.ds(origin + (base + start), 8)

    @staticmethod
    def edge_rows(origin, start):
        return lambda base: pl.ds(origin + (base + start), 2 * TZ, stride=ROWS // 2)

    def part(self, n, dy, dz):
        window, moved, masks_ref, gaps, inverses, starts = self.refs
        for dx in self.groups[(dy, dz)]:
            down = row_start(dx)
            slot = MASK_SLOT[(dx, dy, dz)]
            for k, (rows, keep, height) in enumerate(self.targets):
                other = [moved[rows((3 * n + c) * SIZE + down), :] for c in range(3)]
                at = 8 * (k * len(self.xs) + self.xs.index(dx))
                ex = starts[at : at + height, :] - other[0]
                ey = self.own[k][0] - other[1]
                ez = self.own[k][1] - other[2]
                square = ex * ex + ey * ey + (ez * ez + masks_ref[rows(slot * SIZE), :])
                inverse = lax.rsqrt(square)
                gap = jnp.minimum(square * inverse - density_cut, 0.0)
                self.totals[k] = self.totals[k] + gap * gap
                if keep is not None:
                    gaps[keep + 24 * slot : keep + 24 * slot + 8, :] = gap
                    inverses[keep + 24 * slot : keep + 24 * slot + 8, :] = inverse

    def finish(self, slope):
        for total, (rows, _, _) in zip(self.totals, self.targets):
            slope[rows(0), :] = -embed_scale * lax.rsqrt(total)


class ForceSweep:
    def __init__(self, window, moved, slope, slope_moved, gaps, inverses, groups, no_pair, origin):
        self.no_pair = no_pair
        self.refs = (window, moved, slope_moved, gaps, inverses)
        self.groups = dict(groups)
        self.origin = origin
        self.slopes = [slope[pl.ds(origin + self.at(t), 8), :] for t in range(TZ)]
        self.others = [[None] * 3 for _ in range(TZ)]
        self.weights = [{} for _ in range(TZ)]

    @staticmethod
    def at(t):
        return t * ROWS + BASE + 4

    def part(self, n, dy, dz):
        window, moved, slope_moved, gaps, inverses = self.refs
        first = 2.0 * (coef_zero + coef_one * pair_cut + coef_two * pair_cut * pair_cut)
        second = 3.0 * (coef_one + 2.0 * coef_two * pair_cut)
        third = 4.0 * coef_two
        for dx in self.groups[(dy, dz)]:
            down = row_start(dx)
            slot = MASK_SLOT[(dx, dy, dz)]
            for t in range(TZ):
                row = self.at(t) + down
                other_slope = slope_moved[pl.ds(self.origin + (n * SIZE + row), 8), :]
                gap = gaps[24 * slot + 8 * t : 24 * slot + 8 * t + 8, :]
                inverse = inverses[24 * slot + 8 * t : 24 * slot + 8 * t + 8, :]
                scalar = (self.slopes[t] + other_slope) * gap
                if dx * dx + dy * dy + dz * dz not in self.no_pair:
                    near = jnp.minimum(gap + (density_cut - pair_cut), 0.0)
                    scalar = scalar + near * (first + near * (second + third * near))
                scalar = scalar * inverse
                known = self.weights[t].get(dx)
                self.weights[t][dx] = scalar if known is None else known + scalar
                for c in range(3):
                    other = moved[pl.ds(self.origin + ((3 * n + c) * SIZE + row), 8), :]
                    known = self.others[t][c]
                    self.others[t][c] = scalar * other if known is None else known + scalar * other

    def finish(self, t):
        window = self.refs[0]
        total = list(self.others[t])
        weight = None
        for dx, value in sorted(self.weights[t].items()):
            weight = value if weight is None else weight + value
            if dx:
                total[0] = total[0] + (HALF * dx) * value
        own = [window[pl.ds(self.origin + (c * SIZE + self.at(t)), 8), :] for c in range(3)]
        return [total[c] - own[c] * weight for c in range(3)]


def binomial(n, k):
    value = 1
    for j in range(k):
        value = value * (n - j) // (j + 1)
    return value


def diffuse_grid(grid, across):
    nx, ny = across
    d = diffusion_rate
    pairs = [
        [heat] + [pltpu.roll(heat, k, 1) + pltpu.roll(heat, 128 - k, 1) for k in range(1, SUB + 1)]
        for heat in grid
    ]

    def powers(x, k):
        total = None
        for j in range(k // 2 + 1):
            weight = binomial(k, j) * binomial(SUB, k) * d**k
            term = weight * pairs[x][k - 2 * j]
            total = term if total is None else total + term
        return total

    result = [powers(x, 0) for x in range(nx)]
    for k in range(1, SUB + 1):
        columns = []
        for x in range(nx):
            heat = result[x]
            beside = result[(x + 1) % nx] + result[(x - 1) % nx]
            beside = beside + pltpu.roll(heat, 1, 0) + pltpu.roll(heat, ny - 1, 0)
            columns.append(((1.0 - 6.0 * d) * heat + powers(x, k)) + d * beside)
        result = columns
    return result


LAYERS = 2 * CB * TZ


def temperatures_by_layer(column, plane_total):
    layer = 2 * CB * rows_of() + lanes_of() % (2 * CB)
    layer = jnp.minimum(layer, LAYERS - 1)
    return pick_lanes(jnp.broadcast_to(column, (8, 128)), layer * plane_total // LAYERS)


def energies_by_plane(power, plane_total):
    row, lane = rows_of(), lanes_of()
    stacked = jnp.zeros((8, 128), jnp.float32)
    for t in range(TZ):
        stacked = jnp.where(row == t, power[t], stacked)
    plane = lane % plane_total
    start = (plane * LAYERS + plane_total - 1) // plane_total
    total = jnp.zeros((8, 128), jnp.float32)
    for extra in range(max(1, -(-LAYERS // plane_total))):
        layer = start + extra
        inside = layer - 2 * CB * row
        here = (inside >= 0) & (inside < 2 * CB) & (layer < LAYERS)
        here = here & (layer * plane_total // LAYERS == plane)
        first = 32 + jnp.clip(inside, 0, 2 * CB - 1)
        taken = [pick_lanes(stacked, first + 8 * y) for y in range(BYT * CB)]
        while len(taken) > 1:
            taken = [a + b for a, b in zip(taken[::2], taken[1::2])]
        total = total + jnp.where(here, taken[0], 0.0)
    return jnp.sum(total, axis=0, keepdims=True)


def neighbour_ids(across):
    nx, ny = across
    bx, by = lax.axis_index("gx"), lax.axis_index("gy")
    at_x = {-1: jnp.where(bx == 0, nx - 1, bx - 1), 0: bx, 1: jnp.where(bx == nx - 1, 0, bx + 1)}
    at_y = {-1: jnp.where(by == 0, ny - 1, by - 1), 0: by, 1: jnp.where(by == ny - 1, 0, by + 1)}
    return {(sx, sy): at_x[sx] * ny + at_y[sy] for sx in (-1, 0, 1) for sy in (-1, 0, 1)}


def prepare(across, chunk, disp, heat, pairs, count, vel, noise, send, own_u, live, kept_heat, kept_count, near_vel, near_noise, lists, disp_in, heat_in, pairs_in, count_in, stage, sems):
    nx, ny = across
    owners = nx * ny
    copies = [
        pltpu.make_async_copy(source, target, sems.at[n])
        for n, (source, target) in enumerate(
            ((disp, disp_in), (heat, heat_in), (pairs, pairs_in), (count, count_in))
        )
    ]
    later = [
        pltpu.make_async_copy(vel, near_vel, sems.at[4]),
        pltpu.make_async_copy(noise, near_noise, sems.at[5]),
    ]
    for copy in copies + later:
        copy.start()
    lists[...] = jnp.full(lists.shape, -1, jnp.int32)
    for copy in copies:
        copy.wait()

    from_tiles(lambda c, ix, iy: disp_in[c, ix, :, iy, :], own_u)
    kept_heat[...] = heat_in[...]
    kept_count[...] = jnp.full((8, 128), count_in[0, 0], jnp.int32)

    slots = pairs_in.shape[3]
    width = lists.shape[1]
    lists[0:2, 0:slots] = pairs_in[0, 0]
    tile = lists[0:1, :]
    code = lists[1:2, :]
    valid = (lanes_of((1, width)) < count_in[0, 0]) & (tile >= 0)
    column = jnp.where(tile >= 3, 1, 0) + jnp.where(tile >= 6, 1, 0) + jnp.where(tile >= 9, 1, 0)
    depth = jnp.where(valid, tile - 3 * column, -1)
    place = 32 * column + code
    left = jnp.where(rows_of((8, width)) == depth, 1.0, 0.0)
    right = jnp.where(rows_of((128, width)) == place, 1.0, 0.0)
    found = lax.dot_general(
        left, right, (((1,), (1,)), ((), ())), preferred_element_type=jnp.float32
    )
    live[...] = found

    lane_n = lanes_of((nx, 128))
    planes = jnp.zeros((nx, 128), jnp.float32)
    for y in range(ny):
        value = jnp.broadcast_to(heat_in[0, :, y : y + 1], (nx, 128))
        planes = jnp.where(lane_n % ny == y, value, planes)
    planes = jnp.where(lane_n % owners // ny == rows_of((nx, 128)), planes, 0.0)
    field = jnp.sum(planes, axis=0, keepdims=True)

    lane = lanes_of()
    halves = {
        ("x", -1): found,
        ("x", 1): turn(found, 64),
        ("y", -1): jnp.where(lane < 32, found, turn(found, 32)),
        ("y", 1): jnp.where(lane < 32, turn(found, 32), turn(found, 64)),
    }
    extras = {}
    for key, value in halves.items():
        extras[key] = [
            ((where, to, to + 64), value[t : t + 1] if to == 0 else turn(value, -64)[t : t + 1])
            for t, (where, to) in enumerate(chunk.live)
        ]
    kinds = stage_halo(
        lambda plane: own_u[8 * plane : 8 * plane + 8, :],
        stage,
        chunk,
        [((chunk.tail, chunk.tail_lane, 128), field)],
        extras,
    )
    send_chunks(stage, kinds, send, chunk, neighbour_ids(across), owners)
    for copy in later:
        copy.wait()


def make_masks(chunk, homes, landed, live, masks_ref, table, spread_ref, cases):
    lane1 = lanes_of((1, 128))
    table[...] = jnp.zeros((128, 128), jnp.float32)
    for x in range(4):
        for y in range(4):
            sx, sy = (-1, 0, 0, 1)[x], (-1, 0, 0, 1)[y]
            ix, iy = (1, 0, 1, 0)[x], (1, 0, 1, 0)[y]
            row = jnp.zeros((1, 128), jnp.float32)
            for t in range(TZ):
                if (sx, sy) == (0, 0):
                    value, start = live[t : t + 1, :], 32 * (2 * ix + iy)
                else:
                    where, start = chunk.live[t]
                    value = landed[homes[(sx, sy)] + where : homes[(sx, sy)] + where + 1, :]
                    start = start + 32 * (ix if sy else iy)
                here = (lane1 >= 32 * t) & (lane1 < 32 * t + 32)
                row = jnp.where(here, turn(value, start - 32 * t), row)
            table[4 * x + y : 4 * x + y + 1, :] = row
    by_code = jnp.transpose(table[...])
    big = (128, 128)
    for x in range(4):
        pick = jnp.where(rows_of(big) == 4 * x + lanes_of(big) // 32, 1.0, 0.0)
        alive = jnp.dot(by_code, pick, preferred_element_type=jnp.float32)
        spread_ref[128 * x : 128 * x + 128, :] = FAR_AWAY * (1.0 - alive)

    lane = lanes_of()
    half_layer = lane % 8
    parity = lane % 2
    cell_y = lane // 8 % 4
    low_rows = rows_of() < 4

    def crossing(position, step):
        return (position + step < 0) | (position + step >= 8)

    groups = grouped(NEAR + FAR)

    def at_t(t, carry):
        for code in range(27):
            for block in range(2):
                first, second = [
                    spread_ref[pl.ds(128 * x + 32 * t + code, 1), :] for x in (2 * block, 2 * block + 1)
                ]
                cases[16 * code + 8 * block : 16 * code + 8 * block + 8, :] = jnp.where(
                    low_rows, jnp.broadcast_to(first, (8, 128)), jnp.broadcast_to(second, (8, 128))
                )

        def case(ex, ey, ez, block):
            code = 9 * (ex + 1) + 3 * (ey + 1) + ez + 1
            return cases[16 * code + 8 * block : 16 * code + 8 * block + 8, :]

        for dz in sorted({key[1] for key, _ in groups}):
            cross_z = crossing(half_layer, dz)
            in_z = {}

            def level_z(ex, ey, block):
                if (ex, ey, block) not in in_z:
                    value = case(ex, ey, 0, block)
                    if dz:
                        value = jnp.where(cross_z, case(ex, ey, sign(dz), block), value)
                    in_z[(ex, ey, block)] = value
                return in_z[(ex, ey, block)]

            for (dy, other_z), dxs in groups:
                if other_z != dz:
                    continue
                cross_y = crossing(2 * cell_y + parity, dy)
                in_y = {}

                def level_y(ex, block):
                    if (ex, block) not in in_y:
                        value = level_z(ex, 0, block)
                        if dy:
                            value = jnp.where(cross_y, level_z(ex, sign(dy), block), value)
                        in_y[(ex, block)] = value
                    return in_y[(ex, block)]

                for dx in dxs:
                    cross_x = crossing(2 * (rows_of() % 4) + parity, dx)
                    for block in range(2):
                        value = level_y(0, block)
                        if dx:
                            value = jnp.where(cross_x, level_y(sign(dx), block), value)
                        at = MASK_SLOT[(dx, dy, dz)] * SIZE + BASE + 8 * block
                        masks_ref[pl.ds(at + t * ROWS, 8), :] = value
        return carry

    lax.fori_loop(0, TZ, at_t, 0)


def step_kernel(step, across, arriving, leaving, groups, limit, *refs):
    nx, ny = across
    owners = nx * ny
    refs = list(refs)
    last = leaving is None

    def take(count):
        taken = refs[:count]
        del refs[:count]
        return taken

    recv, in_u, in_v, noise = take(4)
    if step == 0:
        (live,) = take(1)
    else:
        masks_ref, in_grid, in_bad = take(3)
    send, out_grid, out_bad, out_u, out_v = take(5)
    if step == 0:
        (masks_ref,) = take(1)
    window, moved, slope, slope_moved, gaps, inverses, landed, tails_at, noise_own = take(9)
    v_own, stage, mixed, starts = take(4)
    extra = refs
    u_own = out_u
    if step:
        v_own = out_v
    else:
        v_own, v_start = out_v, v_own
    if step == 0:
        table, spread_ref, cases = extra
    ids = neighbour_ids(across)
    lane = lanes_of()

    homes = receive_chunks(recv, landed, tails_at, arriving, ids, owners)
    if step == 0:
        make_masks(arriving, homes, landed, live, masks_ref, table, spread_ref, cases)

    tail = repeat_tail(tails_at[0:owners, :], arriving)
    if step == 0:
        table[...] = jnp.zeros((128, 128), jnp.float32)
        table[0:owners, :] = tail
        turned = jnp.transpose(table[...])[:owners]
        reach = 128
        while reach > owners:
            reach //= 2
            turned = turned + pltpu.roll(turned, reach, 1)
        grid = [turned[ny * x : ny * x + ny] for x in range(nx)]
        out_bad[...] = jnp.zeros((8, 128), jnp.float32)
    else:
        grid = [
            in_grid[ny * x : ny * x + ny, :] + tail[ny * x : ny * x + ny] * (1.0 / heat_capacity)
            for x in range(nx)
        ]
        grid = diffuse_grid(grid, across)
        where, start = arriving.reach
        from_row = owners * (where != arriving.tail)
        furthest = tails_at[from_row : from_row + owners, :]
        lane_n = lanes_of((owners, 128))
        furthest = jnp.where((lane_n >= start) & (lane_n < start + 32), furthest, 0.0)
        reached = jnp.max(furthest, axis=0, keepdims=True)
        reached = jnp.max(reached, axis=1, keepdims=True)
        over = jnp.broadcast_to(jnp.where(reached > limit, 1.0, 0.0), (8, 128))
        out_bad[...] = jnp.maximum(in_bad[...], over)
    for x in range(nx):
        out_grid[ny * x : ny * x + ny, :] = grid[x]
    local = temperatures_by_layer(out_grid[pl.ds(ids[(0, 0)], 1), :], owners)
    kick = jnp.sqrt(local * (2.0 * friction * atom_mass / time_step))

    def own_u(plane):
        return in_u[8 * plane : 8 * plane + 8, :]

    origin = jnp.minimum(lax.axis_index("gx"), 0)
    build_window(own_u, landed, homes, window, arriving, origin)
    mix_planes(3, window, mixed, origin)
    known = (window, moved, masks_ref, slope, gaps, inverses, groups)
    sweep = DensitySweep(window, moved, masks_ref, gaps, inverses, starts, groups, origin)
    shift_planes(3, window, mixed, moved, groups, coordinate_shift, origin, sweep.part)
    sweep.finish(slope)
    no_pair = NEAR_NO_PAIR if step < 2 else ()
    pull = ForceSweep(window, moved, slope, slope_moved, gaps, inverses, groups, no_pair, origin)
    mix_planes(1, slope, mixed, origin)
    shift_planes(1, slope, mixed, slope_moved, groups, no_shift, origin, pull.part)

    from_tiles(lambda c, ix, iy: noise[step, c, ix, :, iy, :], noise_own)
    speeds_in = in_v
    if step == 0:
        from_tiles(lambda c, ix, iy: in_v[c, ix, :, iy, :], v_start)
        speeds_in = v_start

    active = (lane >= 32) & (lane < 96)
    power = []
    furthest = jnp.zeros((8, 128), jnp.float32)
    for t in range(TZ):
        force = pull.finish(t)
        layer = jnp.zeros((8, 128), jnp.float32)
        for c in range(3):
            at = 8 * (c * TZ + t)
            speed = speeds_in[at : at + 8, :]
            push = force[c] - friction * atom_mass * speed + kick[t : t + 1] * noise_own[at : at + 8, :]
            speed = speed + time_step / atom_mass * push
            speed = jnp.where(active, speed, 0.0)
            place = own_u(c * TZ + t) + time_step * speed
            v_own[at : at + 8, :] = speed
            u_own[at : at + 8, :] = place
            layer = layer + speed * speed
            furthest = jnp.maximum(furthest, jnp.abs(place))
        power.append(jnp.sum(layer, axis=0, keepdims=True))
    energy = energies_by_plane(power, owners) * (friction * atom_mass * time_step)
    if last:
        send[...] = jnp.broadcast_to(energy, (owners, 128))
        return
    furthest = jnp.max(furthest, axis=0, keepdims=True)
    furthest = jnp.broadcast_to(jnp.max(furthest, axis=1, keepdims=True), (1, 128))
    where, start = leaving.reach
    tail_row = [
        ((leaving.tail, leaving.tail_lane, 128), energy),
        ((where, start, start + 32), furthest),
    ]
    kinds = stage_halo(
        lambda plane: u_own[8 * plane : 8 * plane + 8, :], stage, leaving, tail_row, {}
    )
    send_chunks(stage, kinds, send, leaving, ids, owners)


def finish(across, recv, in_grid, heat):
    nx, ny = across
    grid = [
        in_grid[ny * x : ny * x + ny, :] + recv[ny * x : ny * x + ny, :] * (1.0 / heat_capacity)
        for x in range(nx)
    ]
    grid = diffuse_grid(grid, across)
    me = lax.axis_index("gx") * ny + lax.axis_index("gy")
    flat = rows_of((ny, 128)) == lanes_of((ny, 128))
    for x in range(nx):
        mine = jnp.where(lanes_of((ny, 128)) == me, grid[x], 0.0)
        mine = jnp.broadcast_to(jnp.sum(mine, axis=1, keepdims=True), (ny, 128))
        row = jnp.sum(jnp.where(flat, mine, 0.0), axis=0, keepdims=True)
        heat[0, x : x + 1, :] = row[:, :ny]


def leave(in_u, in_v, new_u, new_v):
    to_tiles(in_u, new_u)
    to_tiles(in_v, new_v)


def exchange(value):
    return lax.all_to_all(value, ("gx", "gy"), split_axis=0, concat_axis=0, tiled=True)


VMEM_BYTES = 28 * 1024 * 1024


def call(kernel, outs, scratch, operands, in_hbm=(), name=None):
    specs = [
        pl.BlockSpec(memory_space=pltpu.HBM if n in in_hbm else pltpu.VMEM)
        for n in range(len(operands))
    ]
    return pl.pallas_call(
        kernel,
        out_shape=[
            jax.ShapeDtypeStruct(*(out if isinstance(out[1], type) else (out, jnp.float32)))
            for out in outs
        ],
        in_specs=specs,
        out_specs=[pl.BlockSpec(memory_space=pltpu.VMEM)] * len(outs),
        scratch_shapes=scratch,
        compiler_params=pltpu.CompilerParams(
            vmem_limit_bytes=VMEM_BYTES,
        ),
        name=name,
    )(*operands)


def stencil_steps(displacement, velocity, noise, electron_temp, pair_list, pair_count):
    across = (lax.axis_size("gx"), lax.axis_size("gy"))
    owners = across[0] * across[1]

    def vmem(*shape):
        return pltpu.VMEM(shape, jnp.float32)

    tiles = (3, BXT, TZ, BYT, TILE)
    placed_u = jnp.swapaxes(displacement, 2, 3)
    placed_v = jnp.swapaxes(velocity, 2, 3)
    placed_noise = jnp.swapaxes(noise, 3, 4)
    slots = pair_list.shape[-1]
    first, two, three = Chunk(owners, 2, True), Chunk(owners, 2), Chunk(owners, 3)
    send, own_u, live, kept_heat, kept_count, own_v, near_noise = call(
        partial(prepare, across, first),
        [
            (owners, 1, 128 * first.rows),
            (72, 128),
            (8, 128),
            electron_temp.shape,
            ((8, 128), jnp.int32),
            placed_v.shape,
            placed_noise.shape,
        ],
        [
            pltpu.VMEM((8, (slots + 127) // 128 * 128), jnp.int32),
            vmem(*tiles),
            vmem(*electron_temp.shape),
            pltpu.VMEM(pair_list.shape, jnp.int32),
            pltpu.SMEM(pair_count.shape, jnp.int32),
            vmem(4 * 16, 128),
            pltpu.SemaphoreType.DMA((6,)),
        ],
        (
            placed_u,
            pltpu.with_memory_space_constraint(electron_temp, pltpu.HBM),
            pair_list,
            pair_count,
            placed_v,
            placed_noise,
        ),
        in_hbm=(0, 1, 2, 3, 4, 5),
        name="prepare",
    )
    near, far = grouped(NEAR), grouped(NEAR + FAR)
    plan = [
        (first, two, near, 1.0),
        (two, three, near, NEAR_LIMIT),
        (three, three, far, FAR_LIMIT),
        (three, None, far, FAR_LIMIT),
    ]
    masks = grid = bad = None
    for step, (arriving, leaving, groups, limit) in enumerate(plan):
        recv = exchange(send)
        last = leaving is None
        pairs = sum(len(dxs) for _, dxs in groups)
        outs = [
            (owners, 128) if last else (owners, 1, 128 * leaving.rows),
            (owners, 128),
            (8, 128),
            (72, 128),
            (72, 128),
        ]
        scratch = [
            vmem(3 * SIZE + PAD, 128),
            vmem(len(groups) * 3 * SIZE, 128),
            vmem(SIZE, 128),
            vmem(len(groups) * SIZE, 128),
            vmem(24 * pairs, 128),
            vmem(24 * pairs, 128),
            vmem(9 * 16 + 2 * PAD, 128),
            vmem(2 * owners, 128),
            vmem(72, 128),
            vmem(72, 128),
            vmem(4 * 16, 128),
            vmem(3 * SIZE, 128),
            vmem(8 * 5 * 7, 128),
        ]
        if step == 0:
            outs.append((MASKS * SIZE, 128))
            scratch += [vmem(128, 128), vmem(512, 128), vmem(27 * 16, 128)]
            operands = (recv, own_u, own_v, near_noise, live)
        else:
            operands = (recv, own_u, own_v, near_noise, masks, grid, bad)
        got = call(
            partial(step_kernel, step, across, arriving, leaving, groups, limit),
            outs,
            scratch,
            operands,
            name=f"step{step}",
        )
        send, grid, bad, own_u, own_v = got[:5]
        if step == 0:
            masks = got[5]
    recv = exchange(send)
    new_u, new_v = call(leave, [tiles, tiles], [], (own_u, own_v), name="leave")
    (heat,) = call(partial(finish, across), [electron_temp.shape], [], (recv, grid), name="finish")
    kept = (kept_heat, kept_count[:1, :1])
    return bad[0, 0], kept, jnp.swapaxes(new_u, 2, 3), jnp.swapaxes(new_v, 2, 3), heat


def per_device(displacement, velocity, noise, electron_temp, pair_list, pair_count):
    given = (displacement, velocity, noise, electron_temp, pair_list, pair_count)
    bad, (kept_heat, kept_count), new_u, new_v, heat = stencil_steps(*given)
    given = (displacement, velocity, noise, kept_heat, pair_list, kept_count)
    return lax.cond(bad > 0.5, lambda: whole_sweep(*given), lambda: (new_u, new_v, heat))


def solution(mesh):
    placed = (
        P(None, "gx", "gy", None, None),
        P(None, "gx", "gy", None, None),
        P(None, None, "gx", "gy", None, None),
        P(("gx", "gy"), None, None),
        P("gx", "gy", None, None),
        P("gx", "gy"),
    )
    return jax.shard_map(
        per_device,
        mesh=mesh,
        in_specs=placed,
        out_specs=(
            P(None, "gx", "gy", None, None),
            P(None, "gx", "gy", None, None),
            P(("gx", "gy"), None, None),
        ),
        check_vma=False,
    )
```
